256 devices in a mesh: ew: 16 (over x_hi, z), ns: 16 (over y, x_lo, core).
Axes of the slice: x: 4 (x_hi: 2, x_lo: 2; x = x_hi * 2 + x_lo), y: 4, z: 8, core: 2. Of those that a mesh axis runs over, the one named last changes fastest.
Arguments:
- temp: float32 [32, 256, 2048], P(None, 'ns', 'ew'), may hold values from -6 to 6
- salt: float32 [32, 256, 2048], P(None, 'ns', 'ew'), may hold values from -6 to 6
- u_east: float32 [32, 256, 2048], P(None, 'ns', 'ew'), may hold values from -0.25 to 0.25
- v_north: float32 [32, 256, 2048], P(None, 'ns', 'ew'), may hold values from -0.25 to 0.25
- wet: int32 [32, 256, 2048], P(None, 'ns', 'ew'), may hold values 0 or 1
- cot_temp: float32 [32, 256, 2048], P(None, 'ns', 'ew'), may hold values from -6 to 6
- cot_salt: float32 [32, 256, 2048], P(None, 'ns', 'ew'), may hold values from -6 to 6
Outputs:
- temp_final: float32 [32, 256, 2048], P(None, 'ns', 'ew')
- salt_final: float32 [32, 256, 2048], P(None, 'ns', 'ew')
- grad_temp: float32 [32, 256, 2048], P(None, 'ns', 'ew')
- grad_salt: float32 [32, 256, 2048], P(None, 'ns', 'ew')
The draws below stay inside these ranges and needn't reach their ends.
All inputs are finite; a program needn't handle non-finite values. No bound on the sum of `wet` on one device may be relied on, other than what follows from the above.
Results may differ from the reference program's by a relative error of at most 0.00002.
Values sent between devices are 32-bit elements; how exact they have to be, the bound alone decides.
A program may use at most 64 MiB of HBM per device.

```python
import jax
import jax.numpy as jnp
from jax import lax

LEVELS = 32
NY = 256
NX = 2048


def place_ends(entries, rng, least, top_value):
    longest = entries.shape.index(max(entries.shape))
    spots = []
    for shift in (0, 1):
        where = [jax.random.randint(jax.random.fold_in(rng, axis), (), 0, length) for axis, length in enumerate(entries.shape)]
        where[longest] = (where[longest] + shift) % entries.shape[longest]
        spots.append(tuple(where))
    return entries.at[spots[0]].set(least).at[spots[1]].set(top_value)


def shard_levels(own_key, dims, shards, low, largest):
    level = 1.0
    for position, blocks in shards:
        heights = jax.random.uniform(jax.random.fold_in(jax.random.fold_in(own_key, 6), position), (blocks,), jnp.float32, low / len(shards), largest / len(shards))
        level = level * jnp.repeat(jnp.exp(heights), dims[position] // blocks).reshape((-1,) + (1,) * (len(dims) - 1 - position))
    return level


def bell_draw(stream_key, extent, deviation, limit, pieces=(), kind=jnp.bfloat16):
    entries = deviation * jax.random.normal(stream_key, extent, jnp.float32)
    if pieces:
        entries = entries * shard_levels(stream_key, extent, pieces, -0.22, 0.18)
    return jnp.clip(entries, -limit, limit).astype(kind)


def setup_inputs(seed: int = 0) -> dict:
    keys = jax.random.split(jax.random.key(seed), 8)
    temp = bell_draw(keys[0], (LEVELS, NY, NX), 1.0, 6.0, ((1, 16), (2, 16)), jnp.float32)
    salt = bell_draw(keys[1], (LEVELS, NY, NX), 1.0, 6.0, ((1, 16), (2, 16)), jnp.float32)
    u_east = jnp.clip(jax.random.uniform(keys[2], (LEVELS, NY, NX), jnp.float32, -0.25, 0.25) * shard_levels(keys[2], (LEVELS, NY, NX), ((1, 16), (2, 16)), -0.4, 0.0), -0.25, 0.25)
    v_north = jnp.clip(jax.random.uniform(keys[3], (LEVELS, NY, NX), jnp.float32, -0.25, 0.25) * shard_levels(keys[3], (LEVELS, NY, NX), ((1, 16), (2, 16)), -0.4, 0.0), -0.25, 0.25)
    wet = place_ends((jax.random.randint(keys[4], (LEVELS, NY, NX), 0, 4) < 3).astype(jnp.int32), jax.random.fold_in(keys[4], 1), 0, 1)
    cot_temp = bell_draw(keys[5], (LEVELS, NY, NX), 1.0, 6.0, ((1, 16), (2, 16)), jnp.float32)
    cot_salt = bell_draw(keys[6], (LEVELS, NY, NX), 1.0, 6.0, ((1, 16), (2, 16)), jnp.float32)
    return dict(temp=temp, salt=salt, u_east=u_east, v_north=v_north, wet=wet, cot_temp=cot_temp, cot_salt=cot_salt)


horizontal_mix = 0.05
vertical_mix = 0.2

def window_of(array, start, stop, axis):
    return lax.slice_in_dim(array, start, array.shape[axis] + stop, 1, axis)

def coefficients(speed):
    magnitude = jnp.abs(speed)
    return ((-speed - magnitude) / 12.0, (7.0 * speed + 3.0 * magnitude) / 12.0 + horizontal_mix, (7.0 * speed - 3.0 * magnitude) / 12.0 - horizontal_mix, (-speed + magnitude) / 12.0)

def face_change(field, speed, wetness, axis):
    far_left = window_of(field, 0, -3, axis)
    left = window_of(field, 1, -2, axis)
    right = window_of(field, 2, -1, axis)
    far_right = window_of(field, 3, 0, axis)
    weights = coefficients(window_of(speed, 1, -2, axis))
    open_face = window_of(wetness, 1, -2, axis) * window_of(wetness, 2, -1, axis)
    flux = open_face * (weights[0] * far_left + weights[1] * left + weights[2] * right + weights[3] * far_right)
    return window_of(flux, 0, -1, axis) - window_of(flux, 1, 0, axis)

def vertical_change(field, wetness):
    open_face = wetness[:, :-1] * wetness[:, 1:]
    flux = vertical_mix * open_face * (field[:, :-1] - field[:, 1:])
    return jnp.pad(flux, ((0, 0), (1, 0), (0, 0), (0, 0))) - jnp.pad(flux, ((0, 0), (0, 1), (0, 0), (0, 0)))

def advance(padded, flow_wide):
    margin = (flow_wide.shape[2] - padded.shape[2]) // 2
    flow_wide = flow_wide[:, :, margin:flow_wide.shape[2] - margin, margin:flow_wide.shape[3] - margin]
    east_speed = flow_wide[0:1]
    north_speed = flow_wide[1:2]
    wetness = flow_wide[2:3]
    change_x = face_change(window_of(padded, 2, -2, 2), window_of(east_speed, 2, -2, 2), window_of(wetness, 2, -2, 2), 3)
    change_y = face_change(window_of(padded, 2, -2, 3), window_of(north_speed, 2, -2, 3), window_of(wetness, 2, -2, 3), 2)
    inner = window_of(window_of(padded, 2, -2, 2), 2, -2, 3)
    inner_wet = window_of(window_of(wetness, 2, -2, 2), 2, -2, 3)
    change_z = vertical_change(inner, inner_wet)
    return inner + inner_wet * (change_x + change_y + change_z)

def pad_grid(field, width):
    wrapped = jnp.concatenate([field[..., -width:], field, field[..., :width]], axis=-1)
    return jnp.pad(wrapped, ((0, 0), (0, 0), (width, width), (0, 0)))

def reference(temp, salt, u_east, v_north, wet, cot_temp, cot_salt):
    flow_wide = pad_grid(jnp.stack([u_east, v_north, wet.astype(jnp.float32)]), 2)

    def forward(state):
        for turn in range(2):
            state = advance(pad_grid(state, 2), flow_wide)
        return state
    results = []
    gradients = []
    for tracer, sensitivity in ((temp, cot_temp), (salt, cot_salt)):
        final, pullback = jax.vjp(forward, tracer[None])
        gradient, = pullback(sensitivity[None])
        results.append(final[0])
        gradients.append(gradient[0])
    return (results[0], results[1], gradients[0], gradients[1])
```

```python
import jax
import jax.numpy as jnp
from jax import lax
from jax.sharding import PartitionSpec as P

horizontal_mix = 0.05
vertical_mix = 0.2
HALO = 4


def window_of(array, start, stop, axis):
    return lax.slice_in_dim(array, start, array.shape[axis] + stop, 1, axis)


def coefficients(speed):
    magnitude = jnp.abs(speed)
    return (
        (-speed - magnitude) / 12.0,
        (7.0 * speed + 3.0 * magnitude) / 12.0 + horizontal_mix,
        (7.0 * speed - 3.0 * magnitude) / 12.0 - horizontal_mix,
        (-speed + magnitude) / 12.0,
    )


def face_change(field, speed, wetness, axis):
    far_left = window_of(field, 0, -3, axis)
    left = window_of(field, 1, -2, axis)
    right = window_of(field, 2, -1, axis)
    far_right = window_of(field, 3, 0, axis)
    weights = coefficients(window_of(speed, 1, -2, axis))
    open_face = window_of(wetness, 1, -2, axis) * window_of(wetness, 2, -1, axis)
    flux = open_face * (
        weights[0] * far_left + weights[1] * left + weights[2] * right + weights[3] * far_right
    )
    return window_of(flux, 0, -1, axis) - window_of(flux, 1, 0, axis)


def face_adjoint(field, speed, wetness, axis):
    weighted = wetness * field
    jump = window_of(weighted, 1, 0, axis) - window_of(weighted, 0, -1, axis)
    open_face = window_of(wetness, 0, -1, axis) * window_of(wetness, 1, 0, axis)
    weights = coefficients(window_of(speed, 0, -1, axis))
    scaled = open_face * jump
    return (
        window_of(weights[0] * scaled, 3, 0, axis)
        + window_of(weights[1] * scaled, 2, -1, axis)
        + window_of(weights[2] * scaled, 1, -2, axis)
        + window_of(weights[3] * scaled, 0, -3, axis)
    )


def vertical_change(field, wetness):
    open_face = wetness[:, :-1] * wetness[:, 1:]
    flux = vertical_mix * open_face * (field[:, :-1] - field[:, 1:])
    return jnp.pad(flux, ((0, 0), (1, 0), (0, 0), (0, 0))) - jnp.pad(
        flux, ((0, 0), (0, 1), (0, 0), (0, 0))
    )


def vertical_adjoint(field, wetness):
    weighted = wetness * field
    open_face = wetness[:, :-1] * wetness[:, 1:]
    flux = vertical_mix * open_face * (weighted[:, 1:] - weighted[:, :-1])
    return jnp.pad(flux, ((0, 0), (0, 1), (0, 0), (0, 0))) - jnp.pad(
        flux, ((0, 0), (1, 0), (0, 0), (0, 0))
    )


def split_flow(flow):
    return flow[0:1], flow[1:2], flow[2:3]


def advance(padded, flow):
    east_speed, north_speed, wetness = split_flow(flow)
    change_x = face_change(
        window_of(padded, 2, -2, 2), window_of(east_speed, 2, -2, 2), window_of(wetness, 2, -2, 2), 3
    )
    change_y = face_change(
        window_of(padded, 2, -2, 3), window_of(north_speed, 2, -2, 3), window_of(wetness, 2, -2, 3), 2
    )
    inner = window_of(window_of(padded, 2, -2, 2), 2, -2, 3)
    inner_wet = window_of(window_of(wetness, 2, -2, 2), 2, -2, 3)
    change_z = vertical_change(inner, inner_wet)
    return inner + inner_wet * (change_x + change_y + change_z)


def retreat(padded, flow):
    east_speed, north_speed, wetness = split_flow(flow)
    back_x = face_adjoint(
        window_of(padded, 2, -2, 2), window_of(east_speed, 2, -2, 2), window_of(wetness, 2, -2, 2), 3
    )
    back_y = face_adjoint(
        window_of(padded, 2, -2, 3), window_of(north_speed, 2, -2, 3), window_of(wetness, 2, -2, 3), 2
    )
    inner = window_of(window_of(padded, 2, -2, 2), 2, -2, 3)
    inner_wet = window_of(window_of(wetness, 2, -2, 2), 2, -2, 3)
    back_z = vertical_adjoint(inner, inner_wet)
    return inner + back_x + back_y + back_z


def with_halo(cells, width):
    n_ns = lax.axis_size("ns")
    n_ew = lax.axis_size("ew")
    axes = ("ew", "ns")

    def send(piece, d_ns, d_ew):
        pairs = []
        for a in range(n_ns):
            b = a + d_ns
            if b < 0 or b >= n_ns:
                continue
            for e in range(n_ew):
                f = (e + d_ew) % n_ew
                pairs.append((e * n_ns + a, f * n_ns + b))
        return lax.ppermute(piece, axes, pairs)

    rows, cols = cells.shape[-2], cells.shape[-1]
    lo_r, hi_r = slice(0, width), slice(rows - width, rows)
    lo_c, hi_c = slice(0, width), slice(cols - width, cols)
    every = slice(None)
    lead = (every,) * (cells.ndim - 2)

    def part(r, c):
        return cells[lead + (r, c)]

    south_west = send(part(hi_r, hi_c), 1, 1)
    south = send(part(hi_r, every), 1, 0)
    south_east = send(part(hi_r, lo_c), 1, -1)
    west = send(part(every, hi_c), 0, 1)
    east = send(part(every, lo_c), 0, -1)
    north_west = send(part(lo_r, hi_c), -1, 1)
    north = send(part(lo_r, every), -1, 0)
    north_east = send(part(lo_r, lo_c), -1, -1)
    bottom = jnp.concatenate([south_west, south, south_east], axis=-1)
    middle = jnp.concatenate([west, cells, east], axis=-1)
    top = jnp.concatenate([north_west, north, north_east], axis=-1)
    return jnp.concatenate([bottom, middle, top], axis=-2)


def local(temp, salt, u_east, v_north, wet, cot_temp, cot_salt):
    fields = jnp.stack(
        [temp, salt, cot_temp, cot_salt, u_east, v_north, wet.astype(jnp.float32)]
    )
    wide = with_halo(fields, HALO)
    tracers, flow = wide[0:2], wide[4:7]
    sens = wide[2:4]
    for turn in range(2):
        tracers = advance(tracers, flow)
        sens = retreat(sens, flow)
        flow = window_of(window_of(flow, 2, -2, 2), 2, -2, 3)
    return (tracers[0], tracers[1], sens[0], sens[1])


def solution(mesh):
    spec = P(None, "ns", "ew")
    return jax.shard_map(
        local, mesh=mesh, in_specs=(spec,) * 7, out_specs=(spec,) * 4, check_vma=False
    )
```

```python
import functools

import jax
import jax.numpy as jnp
from jax import lax
from jax.experimental import pallas as pl
from jax.experimental.pallas import tpu as pltpu
from jax.sharding import PartitionSpec as P

horizontal_mix = 0.05
vertical_mix = 0.2

PAD = 8
KC = 2
N_FIELDS = 7
N_TRACERS = 4
U, V, M = 4, 5, 6
MESH = pl.DeviceIdType.MESH


def coefficients(speed):
    magnitude = jnp.abs(speed)
    return (
        (-speed - magnitude) / 12.0,
        (7.0 * speed + 3.0 * magnitude) / 12.0 + horizontal_mix,
        (7.0 * speed - 3.0 * magnitude) / 12.0 - horizontal_mix,
        (-speed + magnitude) / 12.0,
    )


def shift_x(c, left, right, lane, cols):
    cm1 = pltpu.roll(jnp.where(lane >= cols - 1, left, c), 1, 2)
    cm2 = pltpu.roll(jnp.where(lane >= cols - 2, left, c), 2, 2)
    cp1 = pltpu.roll(jnp.where(lane < 1, right, c), cols - 1, 2)
    cp2 = pltpu.roll(jnp.where(lane < 2, right, c), cols - 2, 2)
    return cm2, cm1, cp1, cp2


def kernel(n_ew, n_ns, levels, rows, cols,
           t_hbm, s_hbm, ct_hbm, cs_hbm, u_hbm, v_hbm, wet_ref,
           o_t, o_s, o_ct, o_cs,
           b0, x0, ts0, rt0, b1, x1, ts1, rt1, w, oz, load_sem, send_sem, recv_sem):
    ew = lax.axis_index("ew")
    ns = lax.axis_index("ns")
    east = (lax.rem(ew + 1, n_ew), ns)
    west = (lax.rem(ew + n_ew - 1, n_ew), ns)
    north = (ew, jnp.minimum(ns + 1, n_ns - 1))
    south = (ew, jnp.maximum(ns - 1, 0))
    has_north = ns < n_ns - 1
    has_south = ns > 0
    inner = pl.ds(PAD, rows)
    lev = pl.ds(1, levels)

    loads = []
    for f, src in enumerate((t_hbm, s_hbm, ct_hbm, cs_hbm, u_hbm, v_hbm)):
        cp = pltpu.make_async_copy(src, b0.at[f, lev, inner, :], load_sem.at[f])
        cp.start()
        loads.append(cp)

    for buf, nf in ((b0, N_FIELDS), (b1, N_TRACERS)):
        zl = jnp.zeros((nf, 1, rows + 2 * PAD, cols), jnp.float32)
        buf[:, pl.ds(0, 1), :, :] = zl
        buf[:, pl.ds(levels + 1, 1), :, :] = zl
        zr = jnp.zeros((nf, levels, PAD, cols), jnp.float32)
        buf[:, lev, pl.ds(0, PAD), :] = zr
        buf[:, lev, pl.ds(PAD + rows, PAD), :] = zr
    b0[M, lev, inner, :] = wet_ref[...].astype(jnp.float32)
    oz[pl.ds(0, 1), :, :] = jnp.zeros((1, rows, cols), jnp.float32)
    for cp in loads:
        cp.wait()

    barrier = pltpu.get_barrier_semaphore()
    pl.semaphore_signal(barrier, 1, device_id=east, device_id_type=MESH)
    pl.semaphore_signal(barrier, 1, device_id=west, device_id_type=MESH)

    @pl.when(has_north)
    def _():
        pl.semaphore_signal(barrier, 1, device_id=north, device_id_type=MESH)

    @pl.when(has_south)
    def _():
        pl.semaphore_signal(barrier, 1, device_id=south, device_id_type=MESH)

    peers = 2 + has_north.astype(jnp.int32) + has_south.astype(jnp.int32)
    pl.semaphore_wait(barrier, peers)

    def edge_copy(r, d, dev):
        buf, ts, rt = (b0, ts0, rt0) if r == 0 else (b1, ts1, rt1)
        if d == 0:
            src = buf.at[:, lev, pl.ds(PAD + rows - 2, 2), :]
            dst = buf.at[:, lev, pl.ds(PAD - 2, 2), :]
        elif d == 1:
            src = buf.at[:, lev, pl.ds(PAD, 2), :]
            dst = buf.at[:, lev, pl.ds(PAD + rows, 2), :]
        elif d == 2:
            src = ts.at[:, pl.ds(cols - 2, 2), :]
            dst = rt.at[:, pl.ds(cols - 2, 2), :]
        else:
            src = ts.at[:, pl.ds(0, 2), :]
            dst = rt.at[:, pl.ds(0, 2), :]
        return pltpu.make_async_remote_copy(
            src_ref=src, dst_ref=dst, send_sem=send_sem.at[r, d], recv_sem=recv_sem.at[r, d],
            device_id=dev, device_id_type=MESH,
        )

    def pack_columns(r):
        buf, ts = (b0, ts0) if r == 0 else (b1, ts1)
        for f in range(ts.shape[0]):
            ts[f] = buf[f, lev, inner, :].reshape(levels * rows, cols).T

    def unpack_columns(r):
        x, rt = (x0, rt0) if r == 0 else (x1, rt1)
        for f in range(rt.shape[0]):
            x[f] = rt[f].T.reshape(levels, rows, cols)

    def exchange(r):
        pack_columns(r)
        outgoing = ((0, north, has_north), (1, south, has_south), (2, east, None), (3, west, None))
        incoming = ((0, south, has_south), (1, north, has_north), (2, west, None), (3, east, None))
        for d, dev, cond in outgoing:
            if cond is None:
                edge_copy(r, d, dev).start()
            else:
                pl.when(cond)(lambda d=d, dev=dev: edge_copy(r, d, dev).start())
        for d, dev, cond in incoming:
            if cond is None:
                edge_copy(r, d, dev).wait_recv()
            else:
                pl.when(cond)(lambda d=d, dev=dev: edge_copy(r, d, dev).wait_recv())
        unpack_columns(r)

    def finish_sends(r):
        outgoing = ((0, north, has_north), (1, south, has_south), (2, east, None), (3, west, None))
        for d, dev, cond in outgoing:
            if cond is None:
                edge_copy(r, d, dev).wait_send()
            else:
                pl.when(cond)(lambda d=d, dev=dev: edge_copy(r, d, dev).wait_send())

    exchange(0)

    lane = lax.broadcasted_iota(jnp.int32, (KC, rows, cols), 2)

    def rows_at(buf, f, k0, d):
        return buf[f, pl.ds(1 + k0, KC), pl.ds(PAD + d, rows), :]

    def weights_body(i, carry):
        k0 = pl.multiple_of(i * KC, KC)
        kk = pl.ds(k0, KC)
        u0 = rows_at(b0, U, k0, 0)
        um2, um1, up1, _ = shift_x(u0, x0[U, kk], x0[U, kk], lane, cols)
        m0 = rows_at(b0, M, k0, 0)
        mm2, mm1, mp1, mp2 = shift_x(m0, x0[M, kk], x0[M, kk], lane, cols)
        v0 = rows_at(b0, V, k0, 0)
        vm1, vm2, vp1 = rows_at(b0, V, k0, -1), rows_at(b0, V, k0, -2), rows_at(b0, V, k0, 1)
        nm2, nm1 = rows_at(b0, M, k0, -2), rows_at(b0, M, k0, -1)
        np1, np2 = rows_at(b0, M, k0, 1), rows_at(b0, M, k0, 2)
        for base, (s_m2, s_m1, s_0, s_p1), (q_m2, q_m1, q_0, q_p1, q_p2) in (
            (0, (um2, um1, u0, up1), (mm2, mm1, m0, mp1, mp2)),
            (10, (vm2, vm1, v0, vp1), (nm2, nm1, m0, np1, np2)),
        ):
            a0 = coefficients(s_0)
            am1 = coefficients(s_m1)
            o0 = q_0 * q_p1
            om1 = q_m1 * q_0
            for k in range(4):
                w[base + k, kk] = o0 * a0[k]
                w[base + 4 + k, kk] = om1 * am1[k]
            w[base + 8, kk] = (q_p1 * q_p2) * coefficients(s_p1)[0]
            w[base + 9, kk] = (q_m2 * q_m1) * coefficients(s_m2)[3]
        m_up = b0[M, pl.ds(2 + k0, KC), inner, :]
        oz[pl.ds(1 + k0, KC)] = vertical_mix * (m0 * m_up)
        return carry

    lax.fori_loop(0, levels // KC, weights_body, 0)

    def step(src, xh, f, k0, forward):
        kk = pl.ds(k0, KC)
        c = rows_at(src, f, k0, 0)
        cm2, cm1, cp1, cp2 = shift_x(c, xh[f, kk], xh[f, kk], lane, cols)
        ym2, ym1 = rows_at(src, f, k0, -2), rows_at(src, f, k0, -1)
        yp1, yp2 = rows_at(src, f, k0, 1), rows_at(src, f, k0, 2)
        zm = src[f, pl.ds(k0, KC), inner, :]
        zp = src[f, pl.ds(2 + k0, KC), inner, :]
        oz_lo = oz[pl.ds(k0, KC)]
        oz_hi = oz[pl.ds(1 + k0, KC)]
        if forward:
            fxr = w[0, kk] * cm1 + w[1, kk] * c + w[2, kk] * cp1 + w[3, kk] * cp2
            fxl = w[4, kk] * cm2 + w[5, kk] * cm1 + w[6, kk] * c + w[7, kk] * cp1
            fyr = w[10, kk] * ym1 + w[11, kk] * c + w[12, kk] * yp1 + w[13, kk] * yp2
            fyl = w[14, kk] * ym2 + w[15, kk] * ym1 + w[16, kk] * c + w[17, kk] * yp1
            gl = oz_lo * (zm - c)
            gr = oz_hi * (c - zp)
            return c + (((fxl - fxr) + (fyl - fyr)) + (gl - gr))
        bx = (w[8, kk] * (cp2 - cp1) + w[1, kk] * (cp1 - c)
              + w[6, kk] * (c - cm1) + w[9, kk] * (cm1 - cm2))
        by = (w[18, kk] * (yp2 - yp1) + w[11, kk] * (yp1 - c)
              + w[16, kk] * (c - ym1) + w[19, kk] * (ym1 - ym2))
        bz = oz_hi * (zp - c) - oz_lo * (c - zm)
        return c + bx + by + bz

    def step1_body(i, carry):
        k0 = pl.multiple_of(i * KC, KC)
        for f in range(N_TRACERS):
            b1[f, pl.ds(1 + k0, KC), inner, :] = step(b0, x0, f, k0, f < 2)
        return carry

    lax.fori_loop(0, levels // KC, step1_body, 0)
    finish_sends(0)
    exchange(1)

    outs = (o_t, o_s, o_ct, o_cs)

    def step2_body(i, carry):
        k0 = pl.multiple_of(i * KC, KC)
        for f in range(N_TRACERS):
            outs[f][pl.ds(k0, KC)] = step(b1, x1, f, k0, f < 2)
        return carry

    lax.fori_loop(0, levels // KC, step2_body, 0)
    finish_sends(1)


def local(n_ew, n_ns, temp, salt, u_east, v_north, wet, cot_temp, cot_salt):
    levels, rows, cols = temp.shape
    f32 = jnp.float32
    any_spec = pl.BlockSpec(memory_space=pl.ANY)
    vmem_spec = pl.BlockSpec(memory_space=pltpu.VMEM)
    out = jax.ShapeDtypeStruct((levels, rows, cols), f32)
    call = pl.pallas_call(
        functools.partial(kernel, n_ew, n_ns, levels, rows, cols),
        out_shape=(out,) * 4,
        in_specs=[any_spec] * 6 + [vmem_spec],
        out_specs=(vmem_spec,) * 4,
        scratch_shapes=[
            pltpu.VMEM((N_FIELDS, levels + 2, rows + 2 * PAD, cols), f32),
            pltpu.VMEM((N_FIELDS, levels, rows, cols), f32),
            pltpu.VMEM((N_FIELDS, cols, levels * rows), f32),
            pltpu.VMEM((N_FIELDS, cols, levels * rows), f32),
            pltpu.VMEM((N_TRACERS, levels + 2, rows + 2 * PAD, cols), f32),
            pltpu.VMEM((N_TRACERS, levels, rows, cols), f32),
            pltpu.VMEM((N_TRACERS, cols, levels * rows), f32),
            pltpu.VMEM((N_TRACERS, cols, levels * rows), f32),
            pltpu.VMEM((20, levels, rows, cols), f32),
            pltpu.VMEM((levels + 1, rows, cols), f32),
            pltpu.SemaphoreType.DMA((6,)),
            pltpu.SemaphoreType.DMA((2, 4)),
            pltpu.SemaphoreType.DMA((2, 4)),
        ],
        compiler_params=pltpu.CompilerParams(
            collective_id=0, has_side_effects=True, vmem_limit_bytes=56 * 1024 * 1024
        ),
    )
    o_t, o_s, o_ct, o_cs = call(temp, salt, cot_temp, cot_salt, u_east, v_north, wet)
    return o_t, o_s, o_ct, o_cs


def solution(mesh):
    spec = P(None, "ns", "ew")
    n_ew = mesh.shape["ew"]
    n_ns = mesh.shape["ns"]
    return jax.shard_map(
        functools.partial(local, n_ew, n_ns), mesh=mesh,
        in_specs=(spec,) * 7, out_specs=(spec,) * 4, check_vma=False,
    )
```

```python
import functools

import jax
import jax.numpy as jnp
from jax import lax
from jax.experimental import pallas as pl
from jax.experimental.pallas import tpu as pltpu
from jax.sharding import PartitionSpec as P

horizontal_mix = 0.05
vertical_mix = 0.2

PAD = 8
KC = 2
N_FIELDS = 7
X_FIELDS = 6
N_TRACERS = 4
U, M, V = 4, 5, 6
MESH = pl.DeviceIdType.MESH


def coefficients(speed):
    magnitude = jnp.abs(speed)
    return (
        (-speed - magnitude) / 12.0,
        (7.0 * speed + 3.0 * magnitude) / 12.0 + horizontal_mix,
        (7.0 * speed - 3.0 * magnitude) / 12.0 - horizontal_mix,
        (-speed + magnitude) / 12.0,
    )


def shift_x(c, left, right, lane, cols):
    cm1 = pltpu.roll(jnp.where(lane >= cols - 1, left, c), 1, 2)
    cm2 = pltpu.roll(jnp.where(lane >= cols - 2, left, c), 2, 2)
    cp1 = pltpu.roll(jnp.where(lane < 1, right, c), cols - 1, 2)
    cp2 = pltpu.roll(jnp.where(lane < 2, right, c), cols - 2, 2)
    return cm2, cm1, cp1, cp2


def kernel(n_ew, n_ns, levels, rows, cols,
           t_hbm, s_hbm, ct_hbm, cs_hbm, u_hbm, v_hbm, wet_ref,
           o_t, o_s, o_ct, o_cs,
           b0, x0, ts0, rt0, b1, x1, ts1, rt1, w, oz, load_sem, send_sem, recv_sem):
    ew = lax.axis_index("ew")
    ns = lax.axis_index("ns")
    east = (lax.rem(ew + 1, n_ew), ns)
    west = (lax.rem(ew + n_ew - 1, n_ew), ns)
    north = (ew, jnp.minimum(ns + 1, n_ns - 1))
    south = (ew, jnp.maximum(ns - 1, 0))
    has_north = ns < n_ns - 1
    has_south = ns > 0
    inner = pl.ds(PAD, rows)
    lev = pl.ds(1, levels)

    loads = []
    fields = ((0, t_hbm), (1, s_hbm), (2, ct_hbm), (3, cs_hbm), (U, u_hbm), (V, v_hbm))
    for j, (f, src) in enumerate(fields):
        cp = pltpu.make_async_copy(src, b0.at[f, lev, inner, :], load_sem.at[j])
        cp.start()
        loads.append(cp)

    for buf, nf in ((b0, N_FIELDS), (b1, N_TRACERS)):
        zl = jnp.zeros((nf, 1, rows + 2 * PAD, cols), jnp.float32)
        buf[:, pl.ds(0, 1), :, :] = zl
        buf[:, pl.ds(levels + 1, 1), :, :] = zl
        zr = jnp.zeros((nf, levels, PAD, cols), jnp.float32)
        buf[:, lev, pl.ds(0, PAD), :] = zr
        buf[:, lev, pl.ds(PAD + rows, PAD), :] = zr
    b0[M, lev, inner, :] = wet_ref[...].astype(jnp.float32)
    oz[pl.ds(0, 1), :, :] = jnp.zeros((1, rows, cols), jnp.float32)
    for cp in loads:
        cp.wait()

    barrier = pltpu.get_barrier_semaphore()
    pl.semaphore_signal(barrier, 1, device_id=east, device_id_type=MESH)
    pl.semaphore_signal(barrier, 1, device_id=west, device_id_type=MESH)

    @pl.when(has_north)
    def _():
        pl.semaphore_signal(barrier, 1, device_id=north, device_id_type=MESH)

    @pl.when(has_south)
    def _():
        pl.semaphore_signal(barrier, 1, device_id=south, device_id_type=MESH)

    peers = 2 + has_north.astype(jnp.int32) + has_south.astype(jnp.int32)
    pl.semaphore_wait(barrier, peers)

    def group(r):
        if r == 0:
            return b0, ts0, rt0, x0, pl.ds(0, N_FIELDS), pl.ds(0, X_FIELDS)
        g = pl.ds(2 * (r - 1), 2)
        return b1, ts1, rt1, x1, g, g

    def edge_copy(r, d, dev):
        buf, ts, rt, _, fy, fx = group(r)
        if d == 0:
            src = buf.at[fy, lev, pl.ds(PAD + rows - 2, 2), :]
            dst = buf.at[fy, lev, pl.ds(PAD - 2, 2), :]
        elif d == 1:
            src = buf.at[fy, lev, pl.ds(PAD, 2), :]
            dst = buf.at[fy, lev, pl.ds(PAD + rows, 2), :]
        elif d == 2:
            src = ts.at[fx, pl.ds(cols - 2, 2), :]
            dst = rt.at[fx, pl.ds(cols - 2, 2), :]
        else:
            src = ts.at[fx, pl.ds(0, 2), :]
            dst = rt.at[fx, pl.ds(0, 2), :]
        return pltpu.make_async_remote_copy(
            src_ref=src, dst_ref=dst, send_sem=send_sem.at[r, d], recv_sem=recv_sem.at[r, d],
            device_id=dev, device_id_type=MESH,
        )

    def x_fields(r):
        return range(X_FIELDS) if r == 0 else range(2 * (r - 1), 2 * r)

    outgoing = ((0, north, has_north), (1, south, has_south), (2, east, None), (3, west, None))
    incoming = ((0, south, has_south), (1, north, has_north), (2, west, None), (3, east, None))

    def each(r, pairs, action):
        for d, dev, cond in pairs:
            if cond is None:
                action(edge_copy(r, d, dev))
            else:
                pl.when(cond)(lambda d=d, dev=dev: action(edge_copy(r, d, dev)))

    def send(r):
        buf, ts = group(r)[:2]
        for f in x_fields(r):
            ts[f] = buf[f, lev, inner, :].reshape(levels * rows, cols).T
        each(r, outgoing, lambda c: c.start())

    def receive(r):
        rt, x = group(r)[2:4]
        each(r, incoming, lambda c: c.wait_recv())
        for f in x_fields(r):
            x[f] = rt[f].T.reshape(levels, rows, cols)

    def finish_sends(r):
        each(r, outgoing, lambda c: c.wait_send())

    send(0)
    receive(0)

    lane = lax.broadcasted_iota(jnp.int32, (KC, rows, cols), 2)

    def rows_at(buf, f, k0, d):
        return buf[f, pl.ds(1 + k0, KC), pl.ds(PAD + d, rows), :]

    def weights_body(i, carry):
        k0 = pl.multiple_of(i * KC, KC)
        kk = pl.ds(k0, KC)
        u0 = rows_at(b0, U, k0, 0)
        um2, um1, up1, _ = shift_x(u0, x0[U, kk], x0[U, kk], lane, cols)
        m0 = rows_at(b0, M, k0, 0)
        mm2, mm1, mp1, mp2 = shift_x(m0, x0[M, kk], x0[M, kk], lane, cols)
        v0 = rows_at(b0, V, k0, 0)
        vm1, vm2, vp1 = rows_at(b0, V, k0, -1), rows_at(b0, V, k0, -2), rows_at(b0, V, k0, 1)
        nm2, nm1 = rows_at(b0, M, k0, -2), rows_at(b0, M, k0, -1)
        np1, np2 = rows_at(b0, M, k0, 1), rows_at(b0, M, k0, 2)
        for base, (s_m2, s_m1, s_0, s_p1), (q_m2, q_m1, q_0, q_p1, q_p2) in (
            (0, (um2, um1, u0, up1), (mm2, mm1, m0, mp1, mp2)),
            (10, (vm2, vm1, v0, vp1), (nm2, nm1, m0, np1, np2)),
        ):
            a0 = coefficients(s_0)
            am1 = coefficients(s_m1)
            o0 = q_0 * q_p1
            om1 = q_m1 * q_0
            for k in range(4):
                w[base + k, kk] = o0 * a0[k]
                w[base + 4 + k, kk] = om1 * am1[k]
            w[base + 8, kk] = (q_p1 * q_p2) * coefficients(s_p1)[0]
            w[base + 9, kk] = (q_m2 * q_m1) * coefficients(s_m2)[3]
        m_up = b0[M, pl.ds(2 + k0, KC), inner, :]
        oz[pl.ds(1 + k0, KC)] = vertical_mix * (m0 * m_up)
        return carry

    lax.fori_loop(0, levels // KC, weights_body, 0)

    def step(src, xh, f, k0, forward):
        kk = pl.ds(k0, KC)
        c = rows_at(src, f, k0, 0)
        cm2, cm1, cp1, cp2 = shift_x(c, xh[f, kk], xh[f, kk], lane, cols)
        ym2, ym1 = rows_at(src, f, k0, -2), rows_at(src, f, k0, -1)
        yp1, yp2 = rows_at(src, f, k0, 1), rows_at(src, f, k0, 2)
        zm = src[f, pl.ds(k0, KC), inner, :]
        zp = src[f, pl.ds(2 + k0, KC), inner, :]
        oz_lo = oz[pl.ds(k0, KC)]
        oz_hi = oz[pl.ds(1 + k0, KC)]
        if forward:
            fxr = w[0, kk] * cm1 + w[1, kk] * c + w[2, kk] * cp1 + w[3, kk] * cp2
            fxl = w[4, kk] * cm2 + w[5, kk] * cm1 + w[6, kk] * c + w[7, kk] * cp1
            fyr = w[10, kk] * ym1 + w[11, kk] * c + w[12, kk] * yp1 + w[13, kk] * yp2
            fyl = w[14, kk] * ym2 + w[15, kk] * ym1 + w[16, kk] * c + w[17, kk] * yp1
            gl = oz_lo * (zm - c)
            gr = oz_hi * (c - zp)
            return c + (((fxl - fxr) + (fyl - fyr)) + (gl - gr))
        bx = (w[8, kk] * (cp2 - cp1) + w[1, kk] * (cp1 - c)
              + w[6, kk] * (c - cm1) + w[9, kk] * (cm1 - cm2))
        by = (w[18, kk] * (yp2 - yp1) + w[11, kk] * (yp1 - c)
              + w[16, kk] * (c - ym1) + w[19, kk] * (ym1 - ym2))
        bz = oz_hi * (zp - c) - oz_lo * (c - zm)
        return c + bx + by + bz

    outs = (o_t, o_s, o_ct, o_cs)

    def step1_loop(g):
        def body(i, carry):
            k0 = pl.multiple_of(i * KC, KC)
            for f in (2 * g, 2 * g + 1):
                b1[f, pl.ds(1 + k0, KC), inner, :] = step(b0, x0, f, k0, g == 0)
            return carry

        lax.fori_loop(0, levels // KC, body, 0)

    def step2_loop(g):
        def body(i, carry):
            k0 = pl.multiple_of(i * KC, KC)
            for f in (2 * g, 2 * g + 1):
                outs[f][pl.ds(k0, KC)] = step(b1, x1, f, k0, g == 0)
            return carry

        lax.fori_loop(0, levels // KC, body, 0)

    step1_loop(0)
    send(1)
    step1_loop(1)
    send(2)
    finish_sends(0)
    receive(1)
    step2_loop(0)
    receive(2)
    step2_loop(1)
    finish_sends(1)
    finish_sends(2)


def local(n_ew, n_ns, temp, salt, u_east, v_north, wet, cot_temp, cot_salt):
    levels, rows, cols = temp.shape
    f32 = jnp.float32
    any_spec = pl.BlockSpec(memory_space=pl.ANY)
    vmem_spec = pl.BlockSpec(memory_space=pltpu.VMEM)
    out = jax.ShapeDtypeStruct((levels, rows, cols), f32)
    call = pl.pallas_call(
        functools.partial(kernel, n_ew, n_ns, levels, rows, cols),
        out_shape=(out,) * 4,
        in_specs=[any_spec] * 6 + [vmem_spec],
        out_specs=(vmem_spec,) * 4,
        scratch_shapes=[
            pltpu.VMEM((N_FIELDS, levels + 2, rows + 2 * PAD, cols), f32),
            pltpu.VMEM((X_FIELDS, levels, rows, cols), f32),
            pltpu.VMEM((X_FIELDS, cols, levels * rows), f32),
            pltpu.VMEM((X_FIELDS, cols, levels * rows), f32),
            pltpu.VMEM((N_TRACERS, levels + 2, rows + 2 * PAD, cols), f32),
            pltpu.VMEM((N_TRACERS, levels, rows, cols), f32),
            pltpu.VMEM((N_TRACERS, cols, levels * rows), f32),
            pltpu.VMEM((N_TRACERS, cols, levels * rows), f32),
            pltpu.VMEM((20, levels, rows, cols), f32),
            pltpu.VMEM((levels + 1, rows, cols), f32),
            pltpu.SemaphoreType.DMA((6,)),
            pltpu.SemaphoreType.DMA((3, 4)),
            pltpu.SemaphoreType.DMA((3, 4)),
        ],
        compiler_params=pltpu.CompilerParams(
            collective_id=0, has_side_effects=True, vmem_limit_bytes=56 * 1024 * 1024
        ),
    )
    o_t, o_s, o_ct, o_cs = call(temp, salt, cot_temp, cot_salt, u_east, v_north, wet)
    return o_t, o_s, o_ct, o_cs


def solution(mesh):
    spec = P(None, "ns", "ew")
    n_ew = mesh.shape["ew"]
    n_ns = mesh.shape["ns"]
    return jax.shard_map(
        functools.partial(local, n_ew, n_ns), mesh=mesh,
        in_specs=(spec,) * 7, out_specs=(spec,) * 4, check_vma=False,
    )
```

```python
import functools

import jax
import jax.numpy as jnp
from jax import lax
from jax.experimental import pallas as pl
from jax.experimental.pallas import tpu as pltpu
from jax.sharding import PartitionSpec as P

horizontal_mix = 0.05
vertical_mix = 0.2

PAD = 8
KC = 2
N_FIELDS = 7
X_FIELDS = 6
Y_FIRST = 1
N_TRACERS = 4
U, M, V = 0, 5, 6
MESH = pl.DeviceIdType.MESH


def coefficients(speed):
    magnitude = jnp.abs(speed)
    return (
        (-speed - magnitude) / 12.0,
        (7.0 * speed + 3.0 * magnitude) / 12.0 + horizontal_mix,
        (7.0 * speed - 3.0 * magnitude) / 12.0 - horizontal_mix,
        (-speed + magnitude) / 12.0,
    )


def shift_x(c, left, right, lane, cols):
    cm1 = pltpu.roll(jnp.where(lane >= cols - 1, left, c), 1, 2)
    cm2 = pltpu.roll(jnp.where(lane >= cols - 2, left, c), 2, 2)
    cp1 = pltpu.roll(jnp.where(lane < 1, right, c), cols - 1, 2)
    cp2 = pltpu.roll(jnp.where(lane < 2, right, c), cols - 2, 2)
    return cm2, cm1, cp1, cp2


def kernel(n_ew, n_ns, levels, rows, cols,
           t_hbm, s_hbm, ct_hbm, cs_hbm, u_hbm, v_hbm, wet_ref,
           o_t, o_s, o_ct, o_cs,
           b0, x0, ts0, rt0, b1, x1, ts1, rt1, w, oz, load_sem, send_sem, recv_sem):
    ew = lax.axis_index("ew")
    ns = lax.axis_index("ns")
    east = (lax.rem(ew + 1, n_ew), ns)
    west = (lax.rem(ew + n_ew - 1, n_ew), ns)
    north = (ew, jnp.minimum(ns + 1, n_ns - 1))
    south = (ew, jnp.maximum(ns - 1, 0))
    has_north = ns < n_ns - 1
    has_south = ns > 0
    inner = pl.ds(PAD, rows)
    lev = pl.ds(1, levels)

    barrier = pltpu.get_barrier_semaphore()
    pl.semaphore_signal(barrier, 1, device_id=east, device_id_type=MESH)
    pl.semaphore_signal(barrier, 1, device_id=west, device_id_type=MESH)

    @pl.when(has_north)
    def _():
        pl.semaphore_signal(barrier, 1, device_id=north, device_id_type=MESH)

    @pl.when(has_south)
    def _():
        pl.semaphore_signal(barrier, 1, device_id=south, device_id_type=MESH)

    loads = []
    fields = ((1, t_hbm), (2, s_hbm), (3, ct_hbm), (4, cs_hbm), (U, u_hbm), (V, v_hbm))
    for j, (f, src) in enumerate(fields):
        cp = pltpu.make_async_copy(src, b0.at[f, lev, inner, :], load_sem.at[j])
        cp.start()
        loads.append(cp)

    for buf, nf in ((b0, N_FIELDS), (b1, N_TRACERS)):
        zl = jnp.zeros((nf, 1, rows + 2 * PAD, cols), jnp.float32)
        buf[:, pl.ds(0, 1), :, :] = zl
        buf[:, pl.ds(levels + 1, 1), :, :] = zl
        zr = jnp.zeros((nf, levels, 2, cols), jnp.float32)

        @pl.when(jnp.logical_not(has_south))
        def _():
            buf[:, lev, pl.ds(PAD - 2, 2), :] = zr

        @pl.when(jnp.logical_not(has_north))
        def _():
            buf[:, lev, pl.ds(PAD + rows, 2), :] = zr

    b0[M, lev, inner, :] = wet_ref[...].astype(jnp.float32)
    oz[pl.ds(0, 1), :, :] = jnp.zeros((1, rows, cols), jnp.float32)
    for cp in loads:
        cp.wait()

    peers = 2 + has_north.astype(jnp.int32) + has_south.astype(jnp.int32)
    pl.semaphore_wait(barrier, peers)

    def group(r):
        if r == 0:
            return b0, ts0, rt0, x0, pl.ds(Y_FIRST, N_FIELDS - Y_FIRST), pl.ds(0, X_FIELDS)
        g = pl.ds(2 * (r - 1), 2)
        return b1, ts1, rt1, x1, g, g

    def edge_copy(r, d, dev):
        buf, ts, rt, _, fy, fx = group(r)
        if d == 0:
            src = buf.at[fy, lev, pl.ds(PAD + rows - 2, 2), :]
            dst = buf.at[fy, lev, pl.ds(PAD - 2, 2), :]
        elif d == 1:
            src = buf.at[fy, lev, pl.ds(PAD, 2), :]
            dst = buf.at[fy, lev, pl.ds(PAD + rows, 2), :]
        elif d == 2:
            src = ts.at[fx, pl.ds(cols - 2, 2), :]
            dst = rt.at[fx, pl.ds(cols - 2, 2), :]
        else:
            src = ts.at[fx, pl.ds(0, 2), :]
            dst = rt.at[fx, pl.ds(0, 2), :]
        return pltpu.make_async_remote_copy(
            src_ref=src, dst_ref=dst, send_sem=send_sem.at[r, d], recv_sem=recv_sem.at[r, d],
            device_id=dev, device_id_type=MESH,
        )

    def x_fields(r):
        return range(X_FIELDS) if r == 0 else range(2 * (r - 1), 2 * r)

    outgoing = ((0, north, has_north), (1, south, has_south), (2, east, None), (3, west, None))
    incoming = ((0, south, has_south), (1, north, has_north), (2, west, None), (3, east, None))

    def each(r, pairs, action):
        for d, dev, cond in pairs:
            if cond is None:
                action(edge_copy(r, d, dev))
            else:
                pl.when(cond)(lambda d=d, dev=dev: action(edge_copy(r, d, dev)))

    def send(r):
        buf, ts = group(r)[:2]
        for f in x_fields(r):
            ts[f] = buf[f, lev, inner, :].reshape(levels * rows, cols).T
        each(r, outgoing, lambda c: c.start())

    def receive(r):
        rt, x = group(r)[2:4]
        each(r, incoming, lambda c: c.wait_recv())
        for f in x_fields(r):
            x[f] = rt[f].T.reshape(levels, rows, cols)

    def finish_sends(r):
        each(r, outgoing, lambda c: c.wait_send())

    send(0)
    receive(0)

    lane = lax.broadcasted_iota(jnp.int32, (KC, rows, cols), 2)

    def rows_at(buf, f, k0, d):
        return buf[f, pl.ds(1 + k0, KC), pl.ds(PAD + d, rows), :]

    def weights_body(i, carry):
        k0 = pl.multiple_of(i * KC, KC)
        kk = pl.ds(k0, KC)
        u0 = rows_at(b0, U, k0, 0)
        um2, um1, up1, _ = shift_x(u0, x0[U, kk], x0[U, kk], lane, cols)
        m0 = rows_at(b0, M, k0, 0)
        mm2, mm1, mp1, mp2 = shift_x(m0, x0[M, kk], x0[M, kk], lane, cols)
        v0 = rows_at(b0, V, k0, 0)
        vm1, vm2, vp1 = rows_at(b0, V, k0, -1), rows_at(b0, V, k0, -2), rows_at(b0, V, k0, 1)
        nm2, nm1 = rows_at(b0, M, k0, -2), rows_at(b0, M, k0, -1)
        np1, np2 = rows_at(b0, M, k0, 1), rows_at(b0, M, k0, 2)
        for base, (s_m2, s_m1, s_0, s_p1), (q_m2, q_m1, q_0, q_p1, q_p2) in (
            (0, (um2, um1, u0, up1), (mm2, mm1, m0, mp1, mp2)),
            (10, (vm2, vm1, v0, vp1), (nm2, nm1, m0, np1, np2)),
        ):
            a0 = coefficients(s_0)
            am1 = coefficients(s_m1)
            o0 = q_0 * q_p1
            om1 = q_m1 * q_0
            for k in range(4):
                w[base + k, kk] = o0 * a0[k]
                w[base + 4 + k, kk] = om1 * am1[k]
            w[base + 8, kk] = (q_p1 * q_p2) * coefficients(s_p1)[0]
            w[base + 9, kk] = (q_m2 * q_m1) * coefficients(s_m2)[3]
        m_up = b0[M, pl.ds(2 + k0, KC), inner, :]
        oz[pl.ds(1 + k0, KC)] = vertical_mix * (m0 * m_up)
        return carry

    lax.fori_loop(0, levels // KC, weights_body, 0)

    def step(src, xh, f, k0, forward):
        kk = pl.ds(k0, KC)
        c = rows_at(src, f, k0, 0)
        cm2, cm1, cp1, cp2 = shift_x(c, xh[f, kk], xh[f, kk], lane, cols)
        ym2, ym1 = rows_at(src, f, k0, -2), rows_at(src, f, k0, -1)
        yp1, yp2 = rows_at(src, f, k0, 1), rows_at(src, f, k0, 2)
        zm = src[f, pl.ds(k0, KC), inner, :]
        zp = src[f, pl.ds(2 + k0, KC), inner, :]
        oz_lo = oz[pl.ds(k0, KC)]
        oz_hi = oz[pl.ds(1 + k0, KC)]
        if forward:
            fxr = w[0, kk] * cm1 + w[1, kk] * c + w[2, kk] * cp1 + w[3, kk] * cp2
            fxl = w[4, kk] * cm2 + w[5, kk] * cm1 + w[6, kk] * c + w[7, kk] * cp1
            fyr = w[10, kk] * ym1 + w[11, kk] * c + w[12, kk] * yp1 + w[13, kk] * yp2
            fyl = w[14, kk] * ym2 + w[15, kk] * ym1 + w[16, kk] * c + w[17, kk] * yp1
            gl = oz_lo * (zm - c)
            gr = oz_hi * (c - zp)
            return c + (((fxl - fxr) + (fyl - fyr)) + (gl - gr))
        bx = (w[8, kk] * (cp2 - cp1) + w[1, kk] * (cp1 - c)
              + w[6, kk] * (c - cm1) + w[9, kk] * (cm1 - cm2))
        by = (w[18, kk] * (yp2 - yp1) + w[11, kk] * (yp1 - c)
              + w[16, kk] * (c - ym1) + w[19, kk] * (ym1 - ym2))
        bz = oz_hi * (zp - c) - oz_lo * (c - zm)
        return c + bx + by + bz

    outs = (o_t, o_s, o_ct, o_cs)

    def step1_loop(g):
        def body(i, carry):
            k0 = pl.multiple_of(i * KC, KC)
            for f in (2 * g, 2 * g + 1):
                b1[f, pl.ds(1 + k0, KC), inner, :] = step(b0, x0, f + 1, k0, g == 0)
            return carry

        lax.fori_loop(0, levels // KC, body, 0)

    def step2_loop(g):
        def body(i, carry):
            k0 = pl.multiple_of(i * KC, KC)
            for f in (2 * g, 2 * g + 1):
                outs[f][pl.ds(k0, KC)] = step(b1, x1, f, k0, g == 0)
            return carry

        lax.fori_loop(0, levels // KC, body, 0)

    step1_loop(0)
    send(1)
    step1_loop(1)
    send(2)
    finish_sends(0)
    receive(1)
    step2_loop(0)
    receive(2)
    step2_loop(1)
    finish_sends(1)
    finish_sends(2)


def local(n_ew, n_ns, temp, salt, u_east, v_north, wet, cot_temp, cot_salt):
    levels, rows, cols = temp.shape
    f32 = jnp.float32
    any_spec = pl.BlockSpec(memory_space=pl.ANY)
    vmem_spec = pl.BlockSpec(memory_space=pltpu.VMEM)
    out = jax.ShapeDtypeStruct((levels, rows, cols), f32)
    call = pl.pallas_call(
        functools.partial(kernel, n_ew, n_ns, levels, rows, cols),
        out_shape=(out,) * 4,
        in_specs=[any_spec] * 6 + [vmem_spec],
        out_specs=(vmem_spec,) * 4,
        scratch_shapes=[
            pltpu.VMEM((N_FIELDS, levels + 2, rows + 2 * PAD, cols), f32),
            pltpu.VMEM((X_FIELDS, levels, rows, cols), f32),
            pltpu.VMEM((X_FIELDS, cols, levels * rows), f32),
            pltpu.VMEM((X_FIELDS, cols, levels * rows), f32),
            pltpu.VMEM((N_TRACERS, levels + 2, rows + 2 * PAD, cols), f32),
            pltpu.VMEM((N_TRACERS, levels, rows, cols), f32),
            pltpu.VMEM((N_TRACERS, cols, levels * rows), f32),
            pltpu.VMEM((N_TRACERS, cols, levels * rows), f32),
            pltpu.VMEM((20, levels, rows, cols), f32),
            pltpu.VMEM((levels + 1, rows, cols), f32),
            pltpu.SemaphoreType.DMA((6,)),
            pltpu.SemaphoreType.DMA((3, 4)),
            pltpu.SemaphoreType.DMA((3, 4)),
        ],
        compiler_params=pltpu.CompilerParams(
            collective_id=0, has_side_effects=True, vmem_limit_bytes=56 * 1024 * 1024
        ),
    )
    o_t, o_s, o_ct, o_cs = call(temp, salt, cot_temp, cot_salt, u_east, v_north, wet)
    return o_t, o_s, o_ct, o_cs


def solution(mesh):
    spec = P(None, "ns", "ew")
    n_ew = mesh.shape["ew"]
    n_ns = mesh.shape["ns"]
    return jax.shard_map(
        functools.partial(local, n_ew, n_ns), mesh=mesh,
        in_specs=(spec,) * 7, out_specs=(spec,) * 4, check_vma=False,
    )
```

```python
import functools

import jax
import jax.numpy as jnp
from jax import lax
from jax.experimental import pallas as pl
from jax.experimental.pallas import tpu as pltpu
from jax.sharding import PartitionSpec as P

horizontal_mix = 0.05
vertical_mix = 0.2

PAD = 8
KC = 2
N_FIELDS = 7
X_FIELDS = 6
Y_FIRST = 1
N_TRACERS = 4
U, M, V = 0, 5, 6
MESH = pl.DeviceIdType.MESH


def coefficients(speed):
    magnitude = jnp.abs(speed)
    return (
        (-speed - magnitude) / 12.0,
        (7.0 * speed + 3.0 * magnitude) / 12.0 + horizontal_mix,
        (7.0 * speed - 3.0 * magnitude) / 12.0 - horizontal_mix,
        (-speed + magnitude) / 12.0,
    )


def shift_x(c, left, right, lane, cols):
    cm1 = pltpu.roll(jnp.where(lane >= cols - 1, left, c), 1, 2)
    cm2 = pltpu.roll(jnp.where(lane >= cols - 2, left, c), 2, 2)
    cp1 = pltpu.roll(jnp.where(lane < 1, right, c), cols - 1, 2)
    cp2 = pltpu.roll(jnp.where(lane < 2, right, c), cols - 2, 2)
    return cm2, cm1, cp1, cp2


def kernel(n_ew, n_ns, levels, rows, cols,
           t_hbm, s_hbm, ct_hbm, cs_hbm, u_hbm, v_hbm, wet_ref,
           o_all,
           b0, x0, ts0, rt0, b1, x1, ts1, rt1, w, oz, load_sem, send_sem, recv_sem):
    ew = lax.axis_index("ew")
    ns = lax.axis_index("ns")
    east = (lax.rem(ew + 1, n_ew), ns)
    west = (lax.rem(ew + n_ew - 1, n_ew), ns)
    north = (ew, jnp.minimum(ns + 1, n_ns - 1))
    south = (ew, jnp.maximum(ns - 1, 0))
    has_north = ns < n_ns - 1
    has_south = ns > 0
    inner = pl.ds(PAD, rows)
    lev = pl.ds(1, levels)

    barrier = pltpu.get_barrier_semaphore()
    pl.semaphore_signal(barrier, 1, device_id=east, device_id_type=MESH)
    pl.semaphore_signal(barrier, 1, device_id=west, device_id_type=MESH)

    @pl.when(has_north)
    def _():
        pl.semaphore_signal(barrier, 1, device_id=north, device_id_type=MESH)

    @pl.when(has_south)
    def _():
        pl.semaphore_signal(barrier, 1, device_id=south, device_id_type=MESH)

    loads = []
    fields = ((1, t_hbm), (2, s_hbm), (3, ct_hbm), (4, cs_hbm), (U, u_hbm), (V, v_hbm))
    for j, (f, src) in enumerate(fields):
        cp = pltpu.make_async_copy(src, b0.at[f, lev, inner, :], load_sem.at[j])
        cp.start()
        loads.append(cp)

    for buf, nf in ((b0, N_FIELDS), (b1, N_TRACERS)):
        zl = jnp.zeros((nf, 1, rows + 2 * PAD, cols), jnp.float32)
        buf[:, pl.ds(0, 1), :, :] = zl
        buf[:, pl.ds(levels + 1, 1), :, :] = zl
        zr = jnp.zeros((nf, levels, 2, cols), jnp.float32)

        @pl.when(jnp.logical_not(has_south))
        def _():
            buf[:, lev, pl.ds(PAD - 2, 2), :] = zr

        @pl.when(jnp.logical_not(has_north))
        def _():
            buf[:, lev, pl.ds(PAD + rows, 2), :] = zr

    b0[M, lev, inner, :] = wet_ref[...].astype(jnp.float32)
    oz[pl.ds(0, 1), :, :] = jnp.zeros((1, rows, cols), jnp.float32)
    for cp in loads:
        cp.wait()

    peers = 2 + has_north.astype(jnp.int32) + has_south.astype(jnp.int32)
    pl.semaphore_wait(barrier, peers)

    def group(r):
        if r == 0:
            return b0, ts0, rt0, x0, pl.ds(Y_FIRST, N_FIELDS - Y_FIRST), pl.ds(0, X_FIELDS)
        g = pl.ds(2 * (r - 1), 2)
        return b1, ts1, rt1, x1, g, g

    def edge_copy(r, d, dev):
        buf, ts, rt, _, fy, fx = group(r)
        if d == 0:
            src = buf.at[fy, lev, pl.ds(PAD + rows - 2, 2), :]
            dst = buf.at[fy, lev, pl.ds(PAD - 2, 2), :]
        elif d == 1:
            src = buf.at[fy, lev, pl.ds(PAD, 2), :]
            dst = buf.at[fy, lev, pl.ds(PAD + rows, 2), :]
        elif d == 2:
            src = ts.at[fx, pl.ds(cols - 2, 2), :]
            dst = rt.at[fx, pl.ds(cols - 2, 2), :]
        else:
            src = ts.at[fx, pl.ds(0, 2), :]
            dst = rt.at[fx, pl.ds(0, 2), :]
        return pltpu.make_async_remote_copy(
            src_ref=src, dst_ref=dst, send_sem=send_sem.at[r, d], recv_sem=recv_sem.at[r, d],
            device_id=dev, device_id_type=MESH,
        )

    def x_fields(r):
        return range(X_FIELDS) if r == 0 else range(2 * (r - 1), 2 * r)

    outgoing = ((0, north, has_north), (1, south, has_south), (2, east, None), (3, west, None))
    incoming = ((0, south, has_south), (1, north, has_north), (2, west, None), (3, east, None))

    def each(r, pairs, action):
        for d, dev, cond in pairs:
            if cond is None:
                action(edge_copy(r, d, dev))
            else:
                pl.when(cond)(lambda d=d, dev=dev: action(edge_copy(r, d, dev)))

    def send(r):
        buf, ts = group(r)[:2]
        for f in x_fields(r):
            ts[f] = buf[f, lev, inner, :].reshape(levels * rows, cols).T
        each(r, outgoing, lambda c: c.start())

    def receive(r):
        rt, x = group(r)[2:4]
        each(r, incoming, lambda c: c.wait_recv())
        for f in x_fields(r):
            x[f] = rt[f].T.reshape(levels, rows, cols)

    def finish_sends(r):
        each(r, outgoing, lambda c: c.wait_send())

    send(0)
    receive(0)

    lane = lax.broadcasted_iota(jnp.int32, (KC, rows, cols), 2)

    def rows_at(buf, f, k0, d):
        return buf[f, pl.ds(1 + k0, KC), pl.ds(PAD + d, rows), :]

    def weights_body(i, carry):
        k0 = pl.multiple_of(i * KC, KC)
        kk = pl.ds(k0, KC)
        u0 = rows_at(b0, U, k0, 0)
        um2, um1, up1, _ = shift_x(u0, x0[U, kk], x0[U, kk], lane, cols)
        m0 = rows_at(b0, M, k0, 0)
        mm2, mm1, mp1, mp2 = shift_x(m0, x0[M, kk], x0[M, kk], lane, cols)
        v0 = rows_at(b0, V, k0, 0)
        vm1, vm2, vp1 = rows_at(b0, V, k0, -1), rows_at(b0, V, k0, -2), rows_at(b0, V, k0, 1)
        nm2, nm1 = rows_at(b0, M, k0, -2), rows_at(b0, M, k0, -1)
        np1, np2 = rows_at(b0, M, k0, 1), rows_at(b0, M, k0, 2)
        for base, (s_m2, s_m1, s_0, s_p1), (q_m2, q_m1, q_0, q_p1, q_p2) in (
            (0, (um2, um1, u0, up1), (mm2, mm1, m0, mp1, mp2)),
            (10, (vm2, vm1, v0, vp1), (nm2, nm1, m0, np1, np2)),
        ):
            a0 = coefficients(s_0)
            am1 = coefficients(s_m1)
            o0 = q_0 * q_p1
            om1 = q_m1 * q_0
            for k in range(4):
                w[base + k, kk] = o0 * a0[k]
                w[base + 4 + k, kk] = om1 * am1[k]
            w[base + 8, kk] = (q_p1 * q_p2) * coefficients(s_p1)[0]
            w[base + 9, kk] = (q_m2 * q_m1) * coefficients(s_m2)[3]
        m_up = b0[M, pl.ds(2 + k0, KC), inner, :]
        oz[pl.ds(1 + k0, KC)] = vertical_mix * (m0 * m_up)
        return carry

    lax.fori_loop(0, levels // KC, weights_body, 0)

    def step(src, xh, f, k0, forward):
        kk = pl.ds(k0, KC)
        c = rows_at(src, f, k0, 0)
        cm2, cm1, cp1, cp2 = shift_x(c, xh[f, kk], xh[f, kk], lane, cols)
        ym2, ym1 = rows_at(src, f, k0, -2), rows_at(src, f, k0, -1)
        yp1, yp2 = rows_at(src, f, k0, 1), rows_at(src, f, k0, 2)
        zm = src[f, pl.ds(k0, KC), inner, :]
        zp = src[f, pl.ds(2 + k0, KC), inner, :]
        oz_lo = oz[pl.ds(k0, KC)]
        oz_hi = oz[pl.ds(1 + k0, KC)]
        if forward:
            fxr = w[0, kk] * cm1 + w[1, kk] * c + w[2, kk] * cp1 + w[3, kk] * cp2
            fxl = w[4, kk] * cm2 + w[5, kk] * cm1 + w[6, kk] * c + w[7, kk] * cp1
            fyr = w[10, kk] * ym1 + w[11, kk] * c + w[12, kk] * yp1 + w[13, kk] * yp2
            fyl = w[14, kk] * ym2 + w[15, kk] * ym1 + w[16, kk] * c + w[17, kk] * yp1
            gl = oz_lo * (zm - c)
            gr = oz_hi * (c - zp)
            return c + (((fxl - fxr) + (fyl - fyr)) + (gl - gr))
        bx = (w[8, kk] * (cp2 - cp1) + w[1, kk] * (cp1 - c)
              + w[6, kk] * (c - cm1) + w[9, kk] * (cm1 - cm2))
        by = (w[18, kk] * (yp2 - yp1) + w[11, kk] * (yp1 - c)
              + w[16, kk] * (c - ym1) + w[19, kk] * (ym1 - ym2))
        bz = oz_hi * (zp - c) - oz_lo * (c - zm)
        return c + bx + by + bz


    def step1_loop(g):
        def body(i, carry):
            k0 = pl.multiple_of(i * KC, KC)
            for f in (2 * g, 2 * g + 1):
                b1[f, pl.ds(1 + k0, KC), inner, :] = step(b0, x0, f + 1, k0, g == 0)
            return carry

        lax.fori_loop(0, levels // KC, body, 0)

    def step2_loop(g):
        def body(i, carry):
            k0 = pl.multiple_of(i * KC, KC)
            for f in (2 * g, 2 * g + 1):
                o_all[f, pl.ds(k0, KC)] = step(b1, x1, f, k0, g == 0)
            return carry

        lax.fori_loop(0, levels // KC, body, 0)

    step1_loop(0)
    send(1)
    step1_loop(1)
    send(2)
    finish_sends(0)
    receive(1)
    step2_loop(0)
    receive(2)
    step2_loop(1)
    finish_sends(1)
    finish_sends(2)


def split_kernel(stacked, o_t, o_s, o_ct, o_cs, sem):
    copies = []
    for f, dst in enumerate((o_t, o_s, o_ct, o_cs)):
        cp = pltpu.make_async_copy(stacked.at[f], dst, sem.at[f])
        cp.start()
        copies.append(cp)
    for cp in copies:
        cp.wait()


def local(n_ew, n_ns, temp, salt, u_east, v_north, wet, cot_temp, cot_salt):
    levels, rows, cols = temp.shape
    f32 = jnp.float32
    any_spec = pl.BlockSpec(memory_space=pl.ANY)
    vmem_spec = pl.BlockSpec(memory_space=pltpu.VMEM)
    out = jax.ShapeDtypeStruct((levels, rows, cols), f32)
    call = pl.pallas_call(
        functools.partial(kernel, n_ew, n_ns, levels, rows, cols),
        out_shape=jax.ShapeDtypeStruct((N_TRACERS, levels, rows, cols), f32),
        in_specs=[any_spec] * 6 + [vmem_spec],
        out_specs=vmem_spec,
        scratch_shapes=[
            pltpu.VMEM((N_FIELDS, levels + 2, rows + 2 * PAD, cols), f32),
            pltpu.VMEM((X_FIELDS, levels, rows, cols), f32),
            pltpu.VMEM((X_FIELDS, cols, levels * rows), f32),
            pltpu.VMEM((X_FIELDS, cols, levels * rows), f32),
            pltpu.VMEM((N_TRACERS, levels + 2, rows + 2 * PAD, cols), f32),
            pltpu.VMEM((N_TRACERS, levels, rows, cols), f32),
            pltpu.VMEM((N_TRACERS, cols, levels * rows), f32),
            pltpu.VMEM((N_TRACERS, cols, levels * rows), f32),
            pltpu.VMEM((20, levels, rows, cols), f32),
            pltpu.VMEM((levels + 1, rows, cols), f32),
            pltpu.SemaphoreType.DMA((6,)),
            pltpu.SemaphoreType.DMA((3, 4)),
            pltpu.SemaphoreType.DMA((3, 4)),
        ],
        compiler_params=pltpu.CompilerParams(
            collective_id=0, has_side_effects=True, vmem_limit_bytes=56 * 1024 * 1024
        ),
    )
    stacked = call(temp, salt, cot_temp, cot_salt, u_east, v_north, wet)
    return pl.pallas_call(
        split_kernel,
        out_shape=(out,) * 4,
        in_specs=[vmem_spec],
        out_specs=(any_spec,) * 4,
        scratch_shapes=[pltpu.SemaphoreType.DMA((4,))],
    )(stacked)


def solution(mesh):
    spec = P(None, "ns", "ew")
    n_ew = mesh.shape["ew"]
    n_ns = mesh.shape["ns"]
    return jax.shard_map(
        functools.partial(local, n_ew, n_ns), mesh=mesh,
        in_specs=(spec,) * 7, out_specs=(spec,) * 4, check_vma=False,
    )
```

```python
import functools

import jax
import jax.numpy as jnp
from jax import lax
from jax.experimental import pallas as pl
from jax.experimental.pallas import tpu as pltpu
from jax.sharding import PartitionSpec as P

horizontal_mix = 0.05
vertical_mix = 0.2

PAD = 8
KC = 2
N_FIELDS = 7
X_FIELDS = 6
N_TRACERS = 4
U, M, V = 4, 5, 6
MESH = pl.DeviceIdType.MESH


def coefficients(speed):
    magnitude = jnp.abs(speed)
    return (
        (-speed - magnitude) / 12.0,
        (7.0 * speed + 3.0 * magnitude) / 12.0 + horizontal_mix,
        (7.0 * speed - 3.0 * magnitude) / 12.0 - horizontal_mix,
        (-speed + magnitude) / 12.0,
    )


def shift_x(c, left, right, lane, cols):
    cm1 = pltpu.roll(jnp.where(lane >= cols - 1, left, c), 1, 2)
    cm2 = pltpu.roll(jnp.where(lane >= cols - 2, left, c), 2, 2)
    cp1 = pltpu.roll(jnp.where(lane < 1, right, c), cols - 1, 2)
    cp2 = pltpu.roll(jnp.where(lane < 2, right, c), cols - 2, 2)
    return cm2, cm1, cp1, cp2


def kernel(n_ew, n_ns, levels, rows, cols,
           t_hbm, s_hbm, ct_hbm, cs_hbm, u_hbm, v_hbm, wet_ref,
           o_all,
           b0, x0, ts0, rt0, b1, x1, ts1, rt1, w, oz, load_sem, send_sem, recv_sem):
    ew = lax.axis_index("ew")
    ns = lax.axis_index("ns")
    east = (lax.rem(ew + 1, n_ew), ns)
    west = (lax.rem(ew + n_ew - 1, n_ew), ns)
    north = (ew, jnp.minimum(ns + 1, n_ns - 1))
    south = (ew, jnp.maximum(ns - 1, 0))
    has_north = ns < n_ns - 1
    has_south = ns > 0
    inner = pl.ds(PAD, rows)
    lev = pl.ds(1, levels)

    barrier = pltpu.get_barrier_semaphore()
    pl.semaphore_signal(barrier, 1, device_id=east, device_id_type=MESH)
    pl.semaphore_signal(barrier, 1, device_id=west, device_id_type=MESH)

    @pl.when(has_north)
    def _():
        pl.semaphore_signal(barrier, 1, device_id=north, device_id_type=MESH)

    @pl.when(has_south)
    def _():
        pl.semaphore_signal(barrier, 1, device_id=south, device_id_type=MESH)

    loads = []
    fields = ((0, t_hbm), (1, s_hbm), (2, ct_hbm), (3, cs_hbm), (U, u_hbm), (V, v_hbm))
    for j, (f, src) in enumerate(fields):
        cp = pltpu.make_async_copy(src, b0.at[f, lev, inner, :], load_sem.at[j])
        cp.start()
        loads.append(cp)

    for buf, nf in ((b0, N_FIELDS), (b1, N_TRACERS)):
        zl = jnp.zeros((nf, 1, rows + 2 * PAD, cols), jnp.float32)
        buf[:, pl.ds(0, 1), :, :] = zl
        buf[:, pl.ds(levels + 1, 1), :, :] = zl
        zr = jnp.zeros((nf, levels, 2, cols), jnp.float32)

        @pl.when(jnp.logical_not(has_south))
        def _():
            buf[:, lev, pl.ds(PAD - 2, 2), :] = zr

        @pl.when(jnp.logical_not(has_north))
        def _():
            buf[:, lev, pl.ds(PAD + rows, 2), :] = zr

    b0[M, lev, inner, :] = wet_ref[...].astype(jnp.float32)
    oz[pl.ds(0, 1), :, :] = jnp.zeros((1, rows, cols), jnp.float32)
    for cp in loads:
        cp.wait()

    peers = 2 + has_north.astype(jnp.int32) + has_south.astype(jnp.int32)
    pl.semaphore_wait(barrier, peers)

    def group(r):
        if r == 0:
            return b0, ts0, rt0, x0, pl.ds(M, 2), pl.ds(U, 2)
        if r == 1:
            return b0, ts0, rt0, x0, pl.ds(0, N_TRACERS), pl.ds(0, N_TRACERS)
        g = pl.ds(2 * (r - 2), 2)
        return b1, ts1, rt1, x1, g, g

    def edge_copy(r, d, dev):
        buf, ts, rt, _, fy, fx = group(r)
        if d == 0:
            src = buf.at[fy, lev, pl.ds(PAD + rows - 2, 2), :]
            dst = buf.at[fy, lev, pl.ds(PAD - 2, 2), :]
        elif d == 1:
            src = buf.at[fy, lev, pl.ds(PAD, 2), :]
            dst = buf.at[fy, lev, pl.ds(PAD + rows, 2), :]
        elif d == 2:
            src = ts.at[fx, pl.ds(cols - 2, 2), :]
            dst = rt.at[fx, pl.ds(cols - 2, 2), :]
        else:
            src = ts.at[fx, pl.ds(0, 2), :]
            dst = rt.at[fx, pl.ds(0, 2), :]
        return pltpu.make_async_remote_copy(
            src_ref=src, dst_ref=dst, send_sem=send_sem.at[r, d], recv_sem=recv_sem.at[r, d],
            device_id=dev, device_id_type=MESH,
        )

    def x_fields(r):
        if r == 0:
            return (U, M)
        if r == 1:
            return range(N_TRACERS)
        return range(2 * (r - 2), 2 * (r - 1))

    outgoing = ((0, north, has_north), (1, south, has_south), (2, east, None), (3, west, None))
    incoming = ((0, south, has_south), (1, north, has_north), (2, west, None), (3, east, None))

    def each(r, pairs, action):
        for d, dev, cond in pairs:
            if cond is None:
                action(edge_copy(r, d, dev))
            else:
                pl.when(cond)(lambda d=d, dev=dev: action(edge_copy(r, d, dev)))

    def send(r):
        buf, ts = group(r)[:2]
        for f in x_fields(r):
            ts[f] = buf[f, lev, inner, :].reshape(levels * rows, cols).T
        each(r, outgoing, lambda c: c.start())

    def receive(r):
        rt, x = group(r)[2:4]
        each(r, incoming, lambda c: c.wait_recv())
        for f in x_fields(r):
            x[f] = rt[f].T.reshape(levels, rows, cols)

    def finish_sends(r):
        each(r, outgoing, lambda c: c.wait_send())

    send(0)
    send(1)
    receive(0)

    lane = lax.broadcasted_iota(jnp.int32, (KC, rows, cols), 2)

    def rows_at(buf, f, k0, d):
        return buf[f, pl.ds(1 + k0, KC), pl.ds(PAD + d, rows), :]

    def weights_body(i, carry):
        k0 = pl.multiple_of(i * KC, KC)
        kk = pl.ds(k0, KC)
        u0 = rows_at(b0, U, k0, 0)
        um2, um1, up1, _ = shift_x(u0, x0[U, kk], x0[U, kk], lane, cols)
        m0 = rows_at(b0, M, k0, 0)
        mm2, mm1, mp1, mp2 = shift_x(m0, x0[M, kk], x0[M, kk], lane, cols)
        v0 = rows_at(b0, V, k0, 0)
        vm1, vm2, vp1 = rows_at(b0, V, k0, -1), rows_at(b0, V, k0, -2), rows_at(b0, V, k0, 1)
        nm2, nm1 = rows_at(b0, M, k0, -2), rows_at(b0, M, k0, -1)
        np1, np2 = rows_at(b0, M, k0, 1), rows_at(b0, M, k0, 2)
        for base, (s_m2, s_m1, s_0, s_p1), (q_m2, q_m1, q_0, q_p1, q_p2) in (
            (0, (um2, um1, u0, up1), (mm2, mm1, m0, mp1, mp2)),
            (10, (vm2, vm1, v0, vp1), (nm2, nm1, m0, np1, np2)),
        ):
            a0 = coefficients(s_0)
            am1 = coefficients(s_m1)
            o0 = q_0 * q_p1
            om1 = q_m1 * q_0
            for k in range(4):
                w[base + k, kk] = o0 * a0[k]
                w[base + 4 + k, kk] = om1 * am1[k]
            w[base + 8, kk] = (q_p1 * q_p2) * coefficients(s_p1)[0]
            w[base + 9, kk] = (q_m2 * q_m1) * coefficients(s_m2)[3]
        m_up = b0[M, pl.ds(2 + k0, KC), inner, :]
        oz[pl.ds(1 + k0, KC)] = vertical_mix * (m0 * m_up)
        return carry

    lax.fori_loop(0, levels // KC, weights_body, 0)

    def step(src, xh, f, k0, forward):
        kk = pl.ds(k0, KC)
        c = rows_at(src, f, k0, 0)
        cm2, cm1, cp1, cp2 = shift_x(c, xh[f, kk], xh[f, kk], lane, cols)
        ym2, ym1 = rows_at(src, f, k0, -2), rows_at(src, f, k0, -1)
        yp1, yp2 = rows_at(src, f, k0, 1), rows_at(src, f, k0, 2)
        zm = src[f, pl.ds(k0, KC), inner, :]
        zp = src[f, pl.ds(2 + k0, KC), inner, :]
        oz_lo = oz[pl.ds(k0, KC)]
        oz_hi = oz[pl.ds(1 + k0, KC)]
        if forward:
            fxr = w[0, kk] * cm1 + w[1, kk] * c + w[2, kk] * cp1 + w[3, kk] * cp2
            fxl = w[4, kk] * cm2 + w[5, kk] * cm1 + w[6, kk] * c + w[7, kk] * cp1
            fyr = w[10, kk] * ym1 + w[11, kk] * c + w[12, kk] * yp1 + w[13, kk] * yp2
            fyl = w[14, kk] * ym2 + w[15, kk] * ym1 + w[16, kk] * c + w[17, kk] * yp1
            gl = oz_lo * (zm - c)
            gr = oz_hi * (c - zp)
            return c + (((fxl - fxr) + (fyl - fyr)) + (gl - gr))
        bx = (w[8, kk] * (cp2 - cp1) + w[1, kk] * (cp1 - c)
              + w[6, kk] * (c - cm1) + w[9, kk] * (cm1 - cm2))
        by = (w[18, kk] * (yp2 - yp1) + w[11, kk] * (yp1 - c)
              + w[16, kk] * (c - ym1) + w[19, kk] * (ym1 - ym2))
        bz = oz_hi * (zp - c) - oz_lo * (c - zm)
        return c + bx + by + bz


    def step1_loop(g):
        def body(i, carry):
            k0 = pl.multiple_of(i * KC, KC)
            for f in (2 * g, 2 * g + 1):
                b1[f, pl.ds(1 + k0, KC), inner, :] = step(b0, x0, f, k0, g == 0)
            return carry

        lax.fori_loop(0, levels // KC, body, 0)

    def step2_loop(g):
        def body(i, carry):
            k0 = pl.multiple_of(i * KC, KC)
            for f in (2 * g, 2 * g + 1):
                o_all[f, pl.ds(k0, KC)] = step(b1, x1, f, k0, g == 0)
            return carry

        lax.fori_loop(0, levels // KC, body, 0)

    receive(1)
    step1_loop(0)
    send(2)
    step1_loop(1)
    send(3)
    finish_sends(0)
    finish_sends(1)
    receive(2)
    step2_loop(0)
    receive(3)
    step2_loop(1)
    finish_sends(2)
    finish_sends(3)


def split_kernel(stacked, o_t, o_s, o_ct, o_cs, sem):
    copies = []
    for f, dst in enumerate((o_t, o_s, o_ct, o_cs)):
        cp = pltpu.make_async_copy(stacked.at[f], dst, sem.at[f])
        cp.start()
        copies.append(cp)
    for cp in copies:
        cp.wait()


def local(n_ew, n_ns, temp, salt, u_east, v_north, wet, cot_temp, cot_salt):
    levels, rows, cols = temp.shape
    f32 = jnp.float32
    any_spec = pl.BlockSpec(memory_space=pl.ANY)
    vmem_spec = pl.BlockSpec(memory_space=pltpu.VMEM)
    out = jax.ShapeDtypeStruct((levels, rows, cols), f32)
    call = pl.pallas_call(
        functools.partial(kernel, n_ew, n_ns, levels, rows, cols),
        out_shape=jax.ShapeDtypeStruct((N_TRACERS, levels, rows, cols), f32),
        in_specs=[any_spec] * 6 + [vmem_spec],
        out_specs=vmem_spec,
        scratch_shapes=[
            pltpu.VMEM((N_FIELDS, levels + 2, rows + 2 * PAD, cols), f32),
            pltpu.VMEM((X_FIELDS, levels, rows, cols), f32),
            pltpu.VMEM((X_FIELDS, cols, levels * rows), f32),
            pltpu.VMEM((X_FIELDS, cols, levels * rows), f32),
            pltpu.VMEM((N_TRACERS, levels + 2, rows + 2 * PAD, cols), f32),
            pltpu.VMEM((N_TRACERS, levels, rows, cols), f32),
            pltpu.VMEM((N_TRACERS, cols, levels * rows), f32),
            pltpu.VMEM((N_TRACERS, cols, levels * rows), f32),
            pltpu.VMEM((20, levels, rows, cols), f32),
            pltpu.VMEM((levels + 1, rows, cols), f32),
            pltpu.SemaphoreType.DMA((6,)),
            pltpu.SemaphoreType.DMA((4, 4)),
            pltpu.SemaphoreType.DMA((4, 4)),
        ],
        compiler_params=pltpu.CompilerParams(
            collective_id=0, has_side_effects=True, vmem_limit_bytes=56 * 1024 * 1024
        ),
    )
    stacked = call(temp, salt, cot_temp, cot_salt, u_east, v_north, wet)
    return pl.pallas_call(
        split_kernel,
        out_shape=(out,) * 4,
        in_specs=[vmem_spec],
        out_specs=(any_spec,) * 4,
        scratch_shapes=[pltpu.SemaphoreType.DMA((4,))],
    )(stacked)


def solution(mesh):
    spec = P(None, "ns", "ew")
    n_ew = mesh.shape["ew"]
    n_ns = mesh.shape["ns"]
    return jax.shard_map(
        functools.partial(local, n_ew, n_ns), mesh=mesh,
        in_specs=(spec,) * 7, out_specs=(spec,) * 4, check_vma=False,
    )
```

```python
import functools

import jax
import jax.numpy as jnp
from jax import lax
from jax.experimental import pallas as pl
from jax.experimental.pallas import tpu as pltpu
from jax.sharding import PartitionSpec as P

horizontal_mix = 0.05
vertical_mix = 0.2

PAD = 8
KC = 2
N_FIELDS = 7
X_FIELDS = 6
N_TRACERS = 4
U, M, V = 4, 5, 6
MESH = pl.DeviceIdType.MESH


def coefficients(speed):
    magnitude = jnp.abs(speed)
    return (
        (-speed - magnitude) / 12.0,
        (7.0 * speed + 3.0 * magnitude) / 12.0 + horizontal_mix,
        (7.0 * speed - 3.0 * magnitude) / 12.0 - horizontal_mix,
        (-speed + magnitude) / 12.0,
    )


def shift_x(c, left, right, lane, cols):
    cm1 = pltpu.roll(jnp.where(lane >= cols - 1, left, c), 1, 2)
    cm2 = pltpu.roll(jnp.where(lane >= cols - 2, left, c), 2, 2)
    cp1 = pltpu.roll(jnp.where(lane < 1, right, c), cols - 1, 2)
    cp2 = pltpu.roll(jnp.where(lane < 2, right, c), cols - 2, 2)
    return cm2, cm1, cp1, cp2


def kernel(n_ew, n_ns, levels, rows, cols,
           t_hbm, s_hbm, ct_hbm, cs_hbm, u_hbm, v_hbm, wet_ref,
           o_all,
           b0, x0, ts0, rt0, b1, x1, ts1, rt1, w, load_sem, send_sem, recv_sem):
    ew = lax.axis_index("ew")
    ns = lax.axis_index("ns")
    east = (lax.rem(ew + 1, n_ew), ns)
    west = (lax.rem(ew + n_ew - 1, n_ew), ns)
    north = (ew, jnp.minimum(ns + 1, n_ns - 1))
    south = (ew, jnp.maximum(ns - 1, 0))
    has_north = ns < n_ns - 1
    has_south = ns > 0
    inner = pl.ds(PAD, rows)
    lev = pl.ds(1, levels)

    barrier = pltpu.get_barrier_semaphore()
    pl.semaphore_signal(barrier, 1, device_id=east, device_id_type=MESH)
    pl.semaphore_signal(barrier, 1, device_id=west, device_id_type=MESH)

    @pl.when(has_north)
    def _():
        pl.semaphore_signal(barrier, 1, device_id=north, device_id_type=MESH)

    @pl.when(has_south)
    def _():
        pl.semaphore_signal(barrier, 1, device_id=south, device_id_type=MESH)

    loads = []
    fields = ((0, t_hbm), (1, s_hbm), (2, ct_hbm), (3, cs_hbm), (U, u_hbm), (V, v_hbm))
    for j, (f, src) in enumerate(fields):
        cp = pltpu.make_async_copy(src, b0.at[f, lev, inner, :], load_sem.at[j])
        cp.start()
        loads.append(cp)

    for buf, nf in ((b0, N_FIELDS), (b1, N_TRACERS)):
        zl = jnp.zeros((nf, 1, rows + 2 * PAD, cols), jnp.float32)
        buf[:, pl.ds(0, 1), :, :] = zl
        buf[:, pl.ds(levels + 1, 1), :, :] = zl
        zr = jnp.zeros((nf, levels, 2, cols), jnp.float32)

        @pl.when(jnp.logical_not(has_south))
        def _():
            buf[:, lev, pl.ds(PAD - 2, 2), :] = zr

        @pl.when(jnp.logical_not(has_north))
        def _():
            buf[:, lev, pl.ds(PAD + rows, 2), :] = zr

    b0[M, lev, inner, :] = wet_ref[...].astype(jnp.float32)
    for cp in loads:
        cp.wait()

    peers = 2 + has_north.astype(jnp.int32) + has_south.astype(jnp.int32)
    pl.semaphore_wait(barrier, peers)

    def group(r):
        if r == 0:
            return b0, ts0, rt0, x0, pl.ds(M, 2), pl.ds(U, 2)
        if r == 1:
            return b0, ts0, rt0, x0, pl.ds(0, N_TRACERS), pl.ds(0, N_TRACERS)
        g = pl.ds(2 * (r - 2), 2)
        return b1, ts1, rt1, x1, g, g

    def edge_copy(r, d, dev):
        buf, ts, rt, _, fy, fx = group(r)
        if d == 0:
            src = buf.at[fy, lev, pl.ds(PAD + rows - 2, 2), :]
            dst = buf.at[fy, lev, pl.ds(PAD - 2, 2), :]
        elif d == 1:
            src = buf.at[fy, lev, pl.ds(PAD, 2), :]
            dst = buf.at[fy, lev, pl.ds(PAD + rows, 2), :]
        elif d == 2:
            src = ts.at[fx, pl.ds(cols - 2, 2), :]
            dst = rt.at[fx, pl.ds(cols - 2, 2), :]
        else:
            src = ts.at[fx, pl.ds(0, 2), :]
            dst = rt.at[fx, pl.ds(0, 2), :]
        return pltpu.make_async_remote_copy(
            src_ref=src, dst_ref=dst, send_sem=send_sem.at[r, d], recv_sem=recv_sem.at[r, d],
            device_id=dev, device_id_type=MESH,
        )

    def x_fields(r):
        if r == 0:
            return (U, M)
        if r == 1:
            return range(N_TRACERS)
        return range(2 * (r - 2), 2 * (r - 1))

    outgoing = ((0, north, has_north), (1, south, has_south), (2, east, None), (3, west, None))
    incoming = ((0, south, has_south), (1, north, has_north), (2, west, None), (3, east, None))

    def each(r, pairs, action):
        for d, dev, cond in pairs:
            if cond is None:
                action(edge_copy(r, d, dev))
            else:
                pl.when(cond)(lambda d=d, dev=dev: action(edge_copy(r, d, dev)))

    def send(r):
        buf, ts = group(r)[:2]
        for f in x_fields(r):
            ts[f] = buf[f, lev, inner, :].reshape(levels * rows, cols).T
        each(r, outgoing, lambda c: c.start())

    def receive(r):
        rt, x = group(r)[2:4]
        each(r, incoming, lambda c: c.wait_recv())
        for f in x_fields(r):
            x[f] = rt[f].T.reshape(levels, rows, cols)

    def finish_sends(r):
        each(r, outgoing, lambda c: c.wait_send())

    send(0)
    send(1)
    receive(0)

    lane = lax.broadcasted_iota(jnp.int32, (KC, rows, cols), 2)

    def rows_at(buf, f, k0, d):
        return buf[f, pl.ds(1 + k0, KC), pl.ds(PAD + d, rows), :]

    def weights_body(i, carry):
        k0 = pl.multiple_of(i * KC, KC)
        kk = pl.ds(k0, KC)
        u0 = rows_at(b0, U, k0, 0)
        um2, um1, up1, _ = shift_x(u0, x0[U, kk], x0[U, kk], lane, cols)
        m0 = rows_at(b0, M, k0, 0)
        mm2, mm1, mp1, mp2 = shift_x(m0, x0[M, kk], x0[M, kk], lane, cols)
        v0 = rows_at(b0, V, k0, 0)
        vm1, vm2, vp1 = rows_at(b0, V, k0, -1), rows_at(b0, V, k0, -2), rows_at(b0, V, k0, 1)
        nm2, nm1 = rows_at(b0, M, k0, -2), rows_at(b0, M, k0, -1)
        np1, np2 = rows_at(b0, M, k0, 1), rows_at(b0, M, k0, 2)
        centre = None
        for base, (s_m2, s_m1, s_0, s_p1), (q_m2, q_m1, q_0, q_p1, q_p2) in (
            (0, (um2, um1, u0, up1), (mm2, mm1, m0, mp1, mp2)),
            (4, (vm2, vm1, v0, vp1), (nm2, nm1, m0, np1, np2)),
        ):
            a0 = coefficients(s_0)
            am1 = coefficients(s_m1)
            o0 = q_0 * q_p1
            om1 = q_m1 * q_0
            here = [o0 * a0[k] for k in range(4)]
            back = [om1 * am1[k] for k in range(4)]
            ahead0 = (q_p1 * q_p2) * coefficients(s_p1)[0]
            behind3 = (q_m2 * q_m1) * coefficients(s_m2)[3]
            w[base + 0, kk] = back[0]
            w[base + 1, kk] = back[1] - here[0]
            w[base + 2, kk] = back[3] - here[2]
            w[base + 3, kk] = -here[3]
            w[8 + base + 0, kk] = -behind3
            w[8 + base + 1, kk] = behind3 - back[2]
            w[8 + base + 2, kk] = here[1] - ahead0
            w[8 + base + 3, kk] = ahead0
            mid = back[2] - here[1]
            centre = mid if centre is None else centre + mid
        m_dn = b0[M, pl.ds(k0, KC), inner, :]
        m_up = b0[M, pl.ds(2 + k0, KC), inner, :]
        z_lo = vertical_mix * (m_dn * m0)
        z_hi = vertical_mix * (m0 * m_up)
        w[16, kk] = z_lo
        w[17, kk] = z_hi
        w[18, kk] = 1.0 + centre - (z_lo + z_hi)
        return carry

    lax.fori_loop(0, levels // KC, weights_body, 0)

    def step(src, xh, f, k0, forward):
        kk = pl.ds(k0, KC)
        c = rows_at(src, f, k0, 0)
        cm2, cm1, cp1, cp2 = shift_x(c, xh[f, kk], xh[f, kk], lane, cols)
        ym2, ym1 = rows_at(src, f, k0, -2), rows_at(src, f, k0, -1)
        yp1, yp2 = rows_at(src, f, k0, 1), rows_at(src, f, k0, 2)
        zm = src[f, pl.ds(k0, KC), inner, :]
        zp = src[f, pl.ds(2 + k0, KC), inner, :]
        o = 0 if forward else 8
        sx = (w[o + 0, kk] * cm2 + w[o + 1, kk] * cm1) + (w[o + 2, kk] * cp1 + w[o + 3, kk] * cp2)
        sy = (w[o + 4, kk] * ym2 + w[o + 5, kk] * ym1) + (w[o + 6, kk] * yp1 + w[o + 7, kk] * yp2)
        sz = w[16, kk] * zm + w[17, kk] * zp
        return (w[18, kk] * c + sz) + (sx + sy)

    def step1_loop(g):
        def body(i, carry):
            k0 = pl.multiple_of(i * KC, KC)
            for f in (2 * g, 2 * g + 1):
                b1[f, pl.ds(1 + k0, KC), inner, :] = step(b0, x0, f, k0, g == 0)
            return carry

        lax.fori_loop(0, levels // KC, body, 0)

    def step2_loop(g):
        def body(i, carry):
            k0 = pl.multiple_of(i * KC, KC)
            for f in (2 * g, 2 * g + 1):
                o_all[f, pl.ds(k0, KC)] = step(b1, x1, f, k0, g == 0)
            return carry

        lax.fori_loop(0, levels // KC, body, 0)

    receive(1)
    step1_loop(0)
    send(2)
    step1_loop(1)
    send(3)
    finish_sends(0)
    finish_sends(1)
    receive(2)
    step2_loop(0)
    receive(3)
    step2_loop(1)
    finish_sends(2)
    finish_sends(3)


def split_kernel(stacked, o_t, o_s, o_ct, o_cs, sem):
    copies = []
    for f, dst in enumerate((o_t, o_s, o_ct, o_cs)):
        cp = pltpu.make_async_copy(stacked.at[f], dst, sem.at[f])
        cp.start()
        copies.append(cp)
    for cp in copies:
        cp.wait()


def local(n_ew, n_ns, temp, salt, u_east, v_north, wet, cot_temp, cot_salt):
    levels, rows, cols = temp.shape
    f32 = jnp.float32
    any_spec = pl.BlockSpec(memory_space=pl.ANY)
    vmem_spec = pl.BlockSpec(memory_space=pltpu.VMEM)
    out = jax.ShapeDtypeStruct((levels, rows, cols), f32)
    call = pl.pallas_call(
        functools.partial(kernel, n_ew, n_ns, levels, rows, cols),
        out_shape=jax.ShapeDtypeStruct((N_TRACERS, levels, rows, cols), f32),
        in_specs=[any_spec] * 6 + [vmem_spec],
        out_specs=vmem_spec,
        scratch_shapes=[
            pltpu.VMEM((N_FIELDS, levels + 2, rows + 2 * PAD, cols), f32),
            pltpu.VMEM((X_FIELDS, levels, rows, cols), f32),
            pltpu.VMEM((X_FIELDS, cols, levels * rows), f32),
            pltpu.VMEM((X_FIELDS, cols, levels * rows), f32),
            pltpu.VMEM((N_TRACERS, levels + 2, rows + 2 * PAD, cols), f32),
            pltpu.VMEM((N_TRACERS, levels, rows, cols), f32),
            pltpu.VMEM((N_TRACERS, cols, levels * rows), f32),
            pltpu.VMEM((N_TRACERS, cols, levels * rows), f32),
            pltpu.VMEM((19, levels, rows, cols), f32),
            pltpu.SemaphoreType.DMA((6,)),
            pltpu.SemaphoreType.DMA((4, 4)),
            pltpu.SemaphoreType.DMA((4, 4)),
        ],
        compiler_params=pltpu.CompilerParams(
            collective_id=0, has_side_effects=True, vmem_limit_bytes=56 * 1024 * 1024
        ),
    )
    stacked = call(temp, salt, cot_temp, cot_salt, u_east, v_north, wet)
    return pl.pallas_call(
        split_kernel,
        out_shape=(out,) * 4,
        in_specs=[vmem_spec],
        out_specs=(any_spec,) * 4,
        scratch_shapes=[pltpu.SemaphoreType.DMA((4,))],
    )(stacked)


def solution(mesh):
    spec = P(None, "ns", "ew")
    n_ew = mesh.shape["ew"]
    n_ns = mesh.shape["ns"]
    return jax.shard_map(
        functools.partial(local, n_ew, n_ns), mesh=mesh,
        in_specs=(spec,) * 7, out_specs=(spec,) * 4, check_vma=False,
    )
```

```python
import functools

import jax
import jax.numpy as jnp
from jax import lax
from jax.experimental import pallas as pl
from jax.experimental.pallas import tpu as pltpu
from jax.sharding import PartitionSpec as P

horizontal_mix = 0.05
vertical_mix = 0.2

PAD = 8
KC = 2
N_FIELDS = 7
X_FIELDS = 6
N_TRACERS = 4
U, M, V = 4, 5, 6
MESH = pl.DeviceIdType.MESH


def coefficients(speed):
    magnitude = jnp.abs(speed)
    return (
        (-speed - magnitude) / 12.0,
        (7.0 * speed + 3.0 * magnitude) / 12.0 + horizontal_mix,
        (7.0 * speed - 3.0 * magnitude) / 12.0 - horizontal_mix,
        (-speed + magnitude) / 12.0,
    )


def shift_x(c, left, right, lane, cols):
    cm1 = pltpu.roll(jnp.where(lane >= cols - 1, left, c), 1, 2)
    cm2 = pltpu.roll(jnp.where(lane >= cols - 2, left, c), 2, 2)
    cp1 = pltpu.roll(jnp.where(lane < 1, right, c), cols - 1, 2)
    cp2 = pltpu.roll(jnp.where(lane < 2, right, c), cols - 2, 2)
    return cm2, cm1, cp1, cp2


def kernel(n_ew, n_ns, levels, rows, cols,
           t_hbm, s_hbm, ct_hbm, cs_hbm, u_hbm, v_hbm, wet_ref,
           o_all,
           b0, x0, ts0, rt0, b1, x1, ts1, rt1, w, load_sem, send_sem, recv_sem):
    ew = lax.axis_index("ew")
    ns = lax.axis_index("ns")
    east = (lax.rem(ew + 1, n_ew), ns)
    west = (lax.rem(ew + n_ew - 1, n_ew), ns)
    north = (ew, jnp.minimum(ns + 1, n_ns - 1))
    south = (ew, jnp.maximum(ns - 1, 0))
    has_north = ns < n_ns - 1
    has_south = ns > 0
    inner = pl.ds(PAD, rows)
    lev = pl.ds(1, levels)

    barrier = pltpu.get_barrier_semaphore()
    pl.semaphore_signal(barrier, 1, device_id=east, device_id_type=MESH)
    pl.semaphore_signal(barrier, 1, device_id=west, device_id_type=MESH)

    @pl.when(has_north)
    def _():
        pl.semaphore_signal(barrier, 1, device_id=north, device_id_type=MESH)

    @pl.when(has_south)
    def _():
        pl.semaphore_signal(barrier, 1, device_id=south, device_id_type=MESH)

    loads = []
    fields = ((0, t_hbm), (1, s_hbm), (2, ct_hbm), (3, cs_hbm), (U, u_hbm), (V, v_hbm))
    for j, (f, src) in enumerate(fields):
        cp = pltpu.make_async_copy(src, b0.at[f, lev, inner, :], load_sem.at[j])
        cp.start()
        loads.append(cp)

    for buf, nf in ((b0, N_FIELDS), (b1, N_TRACERS)):
        zl = jnp.zeros((nf, 1, rows + 2 * PAD, cols), jnp.float32)
        buf[:, pl.ds(0, 1), :, :] = zl
        buf[:, pl.ds(levels + 1, 1), :, :] = zl
        zr = jnp.zeros((nf, levels, 2, cols), jnp.float32)

        @pl.when(jnp.logical_not(has_south))
        def _():
            buf[:, lev, pl.ds(PAD - 2, 2), :] = zr

        @pl.when(jnp.logical_not(has_north))
        def _():
            buf[:, lev, pl.ds(PAD + rows, 2), :] = zr

    b0[M, lev, inner, :] = wet_ref[...].astype(jnp.float32)
    for cp in loads:
        cp.wait()

    peers = 2 + has_north.astype(jnp.int32) + has_south.astype(jnp.int32)
    pl.semaphore_wait(barrier, peers)

    def group(r):
        if r == 0:
            return b0, ts0, rt0, x0, pl.ds(M, 2), pl.ds(U, 2)
        if r <= N_TRACERS:
            g = pl.ds(r - 1, 1)
            return b0, ts0, rt0, x0, g, g
        g = pl.ds(r - 1 - N_TRACERS, 1)
        return b1, ts1, rt1, x1, g, g

    def edge_copy(r, d, dev):
        buf, ts, rt, _, fy, fx = group(r)
        if d == 0:
            src = buf.at[fy, lev, pl.ds(PAD + rows - 2, 2), :]
            dst = buf.at[fy, lev, pl.ds(PAD - 2, 2), :]
        elif d == 1:
            src = buf.at[fy, lev, pl.ds(PAD, 2), :]
            dst = buf.at[fy, lev, pl.ds(PAD + rows, 2), :]
        elif d == 2:
            src = ts.at[fx, pl.ds(cols - 2, 2), :]
            dst = rt.at[fx, pl.ds(cols - 2, 2), :]
        else:
            src = ts.at[fx, pl.ds(0, 2), :]
            dst = rt.at[fx, pl.ds(0, 2), :]
        return pltpu.make_async_remote_copy(
            src_ref=src, dst_ref=dst, send_sem=send_sem.at[r, d], recv_sem=recv_sem.at[r, d],
            device_id=dev, device_id_type=MESH,
        )

    def x_fields(r):
        if r == 0:
            return (U, M)
        if r <= N_TRACERS:
            return (r - 1,)
        return (r - 1 - N_TRACERS,)

    outgoing = ((0, north, has_north), (1, south, has_south), (2, east, None), (3, west, None))
    incoming = ((0, south, has_south), (1, north, has_north), (2, west, None), (3, east, None))

    def each(r, pairs, action):
        for d, dev, cond in pairs:
            if cond is None:
                action(edge_copy(r, d, dev))
            else:
                pl.when(cond)(lambda d=d, dev=dev: action(edge_copy(r, d, dev)))

    def send(r):
        buf, ts = group(r)[:2]
        for f in x_fields(r):
            ts[f] = buf[f, lev, inner, :].reshape(levels * rows, cols).T
        each(r, outgoing, lambda c: c.start())

    def receive(r):
        rt, x = group(r)[2:4]
        each(r, incoming, lambda c: c.wait_recv())
        for f in x_fields(r):
            x[f] = rt[f].T.reshape(levels, rows, cols)

    def finish_sends(r):
        each(r, outgoing, lambda c: c.wait_send())

    for r in range(1 + N_TRACERS):
        send(r)
    receive(0)

    lane = lax.broadcasted_iota(jnp.int32, (KC, rows, cols), 2)

    def rows_at(buf, f, k0, d):
        return buf[f, pl.ds(1 + k0, KC), pl.ds(PAD + d, rows), :]

    def weights_body(i, carry):
        k0 = pl.multiple_of(i * KC, KC)
        kk = pl.ds(k0, KC)
        u0 = rows_at(b0, U, k0, 0)
        um2, um1, up1, _ = shift_x(u0, x0[U, kk], x0[U, kk], lane, cols)
        m0 = rows_at(b0, M, k0, 0)
        mm2, mm1, mp1, mp2 = shift_x(m0, x0[M, kk], x0[M, kk], lane, cols)
        v0 = rows_at(b0, V, k0, 0)
        vm1, vm2, vp1 = rows_at(b0, V, k0, -1), rows_at(b0, V, k0, -2), rows_at(b0, V, k0, 1)
        nm2, nm1 = rows_at(b0, M, k0, -2), rows_at(b0, M, k0, -1)
        np1, np2 = rows_at(b0, M, k0, 1), rows_at(b0, M, k0, 2)
        centre = None
        for base, (s_m2, s_m1, s_0, s_p1), (q_m2, q_m1, q_0, q_p1, q_p2) in (
            (0, (um2, um1, u0, up1), (mm2, mm1, m0, mp1, mp2)),
            (4, (vm2, vm1, v0, vp1), (nm2, nm1, m0, np1, np2)),
        ):
            a0 = coefficients(s_0)
            am1 = coefficients(s_m1)
            o0 = q_0 * q_p1
            om1 = q_m1 * q_0
            here = [o0 * a0[k] for k in range(4)]
            back = [om1 * am1[k] for k in range(4)]
            ahead0 = (q_p1 * q_p2) * coefficients(s_p1)[0]
            behind3 = (q_m2 * q_m1) * coefficients(s_m2)[3]
            w[base + 0, kk] = back[0]
            w[base + 1, kk] = back[1] - here[0]
            w[base + 2, kk] = back[3] - here[2]
            w[base + 3, kk] = -here[3]
            w[8 + base + 0, kk] = -behind3
            w[8 + base + 1, kk] = behind3 - back[2]
            w[8 + base + 2, kk] = here[1] - ahead0
            w[8 + base + 3, kk] = ahead0
            mid = back[2] - here[1]
            centre = mid if centre is None else centre + mid
        m_dn = b0[M, pl.ds(k0, KC), inner, :]
        m_up = b0[M, pl.ds(2 + k0, KC), inner, :]
        z_lo = vertical_mix * (m_dn * m0)
        z_hi = vertical_mix * (m0 * m_up)
        w[16, kk] = z_lo
        w[17, kk] = z_hi
        w[18, kk] = 1.0 + centre - (z_lo + z_hi)
        return carry

    lax.fori_loop(0, levels // KC, weights_body, 0)

    def step(src, xh, f, k0, forward):
        kk = pl.ds(k0, KC)
        c = rows_at(src, f, k0, 0)
        cm2, cm1, cp1, cp2 = shift_x(c, xh[f, kk], xh[f, kk], lane, cols)
        ym2, ym1 = rows_at(src, f, k0, -2), rows_at(src, f, k0, -1)
        yp1, yp2 = rows_at(src, f, k0, 1), rows_at(src, f, k0, 2)
        zm = src[f, pl.ds(k0, KC), inner, :]
        zp = src[f, pl.ds(2 + k0, KC), inner, :]
        o = 0 if forward else 8
        sx = (w[o + 0, kk] * cm2 + w[o + 1, kk] * cm1) + (w[o + 2, kk] * cp1 + w[o + 3, kk] * cp2)
        sy = (w[o + 4, kk] * ym2 + w[o + 5, kk] * ym1) + (w[o + 6, kk] * yp1 + w[o + 7, kk] * yp2)
        sz = w[16, kk] * zm + w[17, kk] * zp
        return (w[18, kk] * c + sz) + (sx + sy)

    def step1_loop(f):
        def body(i, carry):
            k0 = pl.multiple_of(i * KC, KC)
            b1[f, pl.ds(1 + k0, KC), inner, :] = step(b0, x0, f, k0, f < 2)
            return carry

        lax.fori_loop(0, levels // KC, body, 0)

    def step2_loop(f):
        def body(i, carry):
            k0 = pl.multiple_of(i * KC, KC)
            o_all[f, pl.ds(k0, KC)] = step(b1, x1, f, k0, f < 2)
            return carry

        lax.fori_loop(0, levels // KC, body, 0)

    for f in range(N_TRACERS):
        receive(1 + f)
        step1_loop(f)
        send(1 + N_TRACERS + f)
    for r in range(1 + N_TRACERS):
        finish_sends(r)
    for f in range(N_TRACERS):
        receive(1 + N_TRACERS + f)
        step2_loop(f)
    for f in range(N_TRACERS):
        finish_sends(1 + N_TRACERS + f)


def split_kernel(stacked, o_t, o_s, o_ct, o_cs, sem):
    copies = []
    for f, dst in enumerate((o_t, o_s, o_ct, o_cs)):
        cp = pltpu.make_async_copy(stacked.at[f], dst, sem.at[f])
        cp.start()
        copies.append(cp)
    for cp in copies:
        cp.wait()


def local(n_ew, n_ns, temp, salt, u_east, v_north, wet, cot_temp, cot_salt):
    levels, rows, cols = temp.shape
    f32 = jnp.float32
    any_spec = pl.BlockSpec(memory_space=pl.ANY)
    vmem_spec = pl.BlockSpec(memory_space=pltpu.VMEM)
    out = jax.ShapeDtypeStruct((levels, rows, cols), f32)
    call = pl.pallas_call(
        functools.partial(kernel, n_ew, n_ns, levels, rows, cols),
        out_shape=jax.ShapeDtypeStruct((N_TRACERS, levels, rows, cols), f32),
        in_specs=[any_spec] * 6 + [vmem_spec],
        out_specs=vmem_spec,
        scratch_shapes=[
            pltpu.VMEM((N_FIELDS, levels + 2, rows + 2 * PAD, cols), f32),
            pltpu.VMEM((X_FIELDS, levels, rows, cols), f32),
            pltpu.VMEM((X_FIELDS, cols, levels * rows), f32),
            pltpu.VMEM((X_FIELDS, cols, levels * rows), f32),
            pltpu.VMEM((N_TRACERS, levels + 2, rows + 2 * PAD, cols), f32),
            pltpu.VMEM((N_TRACERS, levels, rows, cols), f32),
            pltpu.VMEM((N_TRACERS, cols, levels * rows), f32),
            pltpu.VMEM((N_TRACERS, cols, levels * rows), f32),
            pltpu.VMEM((19, levels, rows, cols), f32),
            pltpu.SemaphoreType.DMA((6,)),
            pltpu.SemaphoreType.DMA((1 + 2 * N_TRACERS, 4)),
            pltpu.SemaphoreType.DMA((1 + 2 * N_TRACERS, 4)),
        ],
        compiler_params=pltpu.CompilerParams(
            collective_id=0, has_side_effects=True, vmem_limit_bytes=56 * 1024 * 1024
        ),
    )
    stacked = call(temp, salt, cot_temp, cot_salt, u_east, v_north, wet)
    return pl.pallas_call(
        split_kernel,
        out_shape=(out,) * 4,
        in_specs=[vmem_spec],
        out_specs=(any_spec,) * 4,
        scratch_shapes=[pltpu.SemaphoreType.DMA((4,))],
    )(stacked)


def solution(mesh):
    spec = P(None, "ns", "ew")
    n_ew = mesh.shape["ew"]
    n_ns = mesh.shape["ns"]
    return jax.shard_map(
        functools.partial(local, n_ew, n_ns), mesh=mesh,
        in_specs=(spec,) * 7, out_specs=(spec,) * 4, check_vma=False,
    )
```

```python
import functools

import jax
import jax.numpy as jnp
from jax import lax
from jax.experimental import pallas as pl
from jax.experimental.pallas import tpu as pltpu
from jax.sharding import PartitionSpec as P

horizontal_mix = 0.05
vertical_mix = 0.2

PAD = 8
KC = 2
N_FIELDS = 7
X_FIELDS = 6
N_TRACERS = 4
U, M, V = 4, 5, 6
MESH = pl.DeviceIdType.MESH


def coefficients(speed):
    magnitude = jnp.abs(speed)
    return (
        (-speed - magnitude) / 12.0,
        (7.0 * speed + 3.0 * magnitude) / 12.0 + horizontal_mix,
        (7.0 * speed - 3.0 * magnitude) / 12.0 - horizontal_mix,
        (-speed + magnitude) / 12.0,
    )


def shift_x(c, left, right, lane, cols):
    cm1 = pltpu.roll(jnp.where(lane >= cols - 1, left, c), 1, 2)
    cm2 = pltpu.roll(jnp.where(lane >= cols - 2, left, c), 2, 2)
    cp1 = pltpu.roll(jnp.where(lane < 1, right, c), cols - 1, 2)
    cp2 = pltpu.roll(jnp.where(lane < 2, right, c), cols - 2, 2)
    return cm2, cm1, cp1, cp2


def kernel(n_ew, n_ns, levels, rows, cols,
           t_hbm, s_hbm, ct_hbm, cs_hbm, u_hbm, v_hbm, wet_ref,
           o_all,
           b0, x0, ts0, rt0, b1, x1, ts1, rt1, w, load_sem, send_sem, recv_sem):
    ew = lax.axis_index("ew")
    ns = lax.axis_index("ns")
    east = (lax.rem(ew + 1, n_ew), ns)
    west = (lax.rem(ew + n_ew - 1, n_ew), ns)
    north = (ew, jnp.minimum(ns + 1, n_ns - 1))
    south = (ew, jnp.maximum(ns - 1, 0))
    has_north = ns < n_ns - 1
    has_south = ns > 0
    inner = pl.ds(PAD, rows)
    lev = pl.ds(1, levels)

    barrier = pltpu.get_barrier_semaphore()
    pl.semaphore_signal(barrier, 1, device_id=east, device_id_type=MESH)
    pl.semaphore_signal(barrier, 1, device_id=west, device_id_type=MESH)

    @pl.when(has_north)
    def _():
        pl.semaphore_signal(barrier, 1, device_id=north, device_id_type=MESH)

    @pl.when(has_south)
    def _():
        pl.semaphore_signal(barrier, 1, device_id=south, device_id_type=MESH)

    loads = []
    fields = ((0, t_hbm), (1, s_hbm), (2, ct_hbm), (3, cs_hbm), (U, u_hbm), (V, v_hbm))
    for j, (f, src) in enumerate(fields):
        cp = pltpu.make_async_copy(src, b0.at[f, lev, inner, :], load_sem.at[j])
        cp.start()
        loads.append(cp)

    for buf, nf in ((b0, N_FIELDS), (b1, N_TRACERS)):
        zl = jnp.zeros((nf, 1, rows + 2 * PAD, cols), jnp.float32)
        buf[:, pl.ds(0, 1), :, :] = zl
        buf[:, pl.ds(levels + 1, 1), :, :] = zl
        zr = jnp.zeros((nf, levels, 2, cols), jnp.float32)

        @pl.when(jnp.logical_not(has_south))
        def _():
            buf[:, lev, pl.ds(PAD - 2, 2), :] = zr

        @pl.when(jnp.logical_not(has_north))
        def _():
            buf[:, lev, pl.ds(PAD + rows, 2), :] = zr

    b0[M, lev, inner, :] = wet_ref[...].astype(jnp.float32)
    for cp in loads:
        cp.wait()

    peers = 2 + has_north.astype(jnp.int32) + has_south.astype(jnp.int32)
    pl.semaphore_wait(barrier, peers)

    def group(r):
        if r == 0:
            return b0, ts0, rt0, x0, pl.ds(M, 2), pl.ds(U, 2)
        if r == 1:
            return b0, ts0, rt0, x0, pl.ds(0, N_TRACERS), pl.ds(0, N_TRACERS)
        g = pl.ds(2 * (r - 2), 2)
        return b1, ts1, rt1, x1, g, g

    def edge_copy(r, d, dev):
        buf, ts, rt, _, fy, fx = group(r)
        if d == 0:
            src = buf.at[fy, lev, pl.ds(PAD + rows - 2, 2), :]
            dst = buf.at[fy, lev, pl.ds(PAD - 2, 2), :]
        elif d == 1:
            src = buf.at[fy, lev, pl.ds(PAD, 2), :]
            dst = buf.at[fy, lev, pl.ds(PAD + rows, 2), :]
        elif d == 2:
            src = ts.at[fx, pl.ds(cols - 2, 2), :]
            dst = rt.at[fx, pl.ds(cols - 2, 2), :]
        else:
            src = ts.at[fx, pl.ds(0, 2), :]
            dst = rt.at[fx, pl.ds(0, 2), :]
        return pltpu.make_async_remote_copy(
            src_ref=src, dst_ref=dst, send_sem=send_sem.at[r, d], recv_sem=recv_sem.at[r, d],
            device_id=dev, device_id_type=MESH,
        )

    def x_fields(r):
        if r == 0:
            return (U, M)
        if r == 1:
            return range(N_TRACERS)
        return range(2 * (r - 2), 2 * (r - 1))

    outgoing = ((0, north, has_north), (1, south, has_south), (2, east, None), (3, west, None))
    incoming = ((0, south, has_south), (1, north, has_north), (2, west, None), (3, east, None))

    def each(r, pairs, action):
        for d, dev, cond in pairs:
            if cond is None:
                action(edge_copy(r, d, dev))
            else:
                pl.when(cond)(lambda d=d, dev=dev: action(edge_copy(r, d, dev)))

    def send_rows(r):
        each(r, outgoing[:2], lambda c: c.start())

    def send_columns(r):
        buf, ts = group(r)[:2]
        for f in x_fields(r):
            ts[f] = buf[f, lev, inner, :].reshape(levels * rows, cols).T
        each(r, outgoing[2:], lambda c: c.start())

    def send(r):
        send_rows(r)
        send_columns(r)

    def receive(r):
        rt, x = group(r)[2:4]
        each(r, incoming, lambda c: c.wait_recv())
        for f in x_fields(r):
            x[f] = rt[f].T.reshape(levels, rows, cols)

    def finish_sends(r):
        each(r, outgoing, lambda c: c.wait_send())

    send_rows(0)
    send_rows(1)
    send_columns(0)
    send_columns(1)
    receive(0)

    lane = lax.broadcasted_iota(jnp.int32, (KC, rows, cols), 2)

    def rows_at(buf, f, k0, d):
        return buf[f, pl.ds(1 + k0, KC), pl.ds(PAD + d, rows), :]

    def weights_body(i, carry):
        k0 = pl.multiple_of(i * KC, KC)
        kk = pl.ds(k0, KC)
        u0 = rows_at(b0, U, k0, 0)
        um2, um1, up1, _ = shift_x(u0, x0[U, kk], x0[U, kk], lane, cols)
        m0 = rows_at(b0, M, k0, 0)
        mm2, mm1, mp1, mp2 = shift_x(m0, x0[M, kk], x0[M, kk], lane, cols)
        v0 = rows_at(b0, V, k0, 0)
        vm1, vm2, vp1 = rows_at(b0, V, k0, -1), rows_at(b0, V, k0, -2), rows_at(b0, V, k0, 1)
        nm2, nm1 = rows_at(b0, M, k0, -2), rows_at(b0, M, k0, -1)
        np1, np2 = rows_at(b0, M, k0, 1), rows_at(b0, M, k0, 2)
        centre = None
        for base, (s_m2, s_m1, s_0, s_p1), (q_m2, q_m1, q_0, q_p1, q_p2) in (
            (0, (um2, um1, u0, up1), (mm2, mm1, m0, mp1, mp2)),
            (4, (vm2, vm1, v0, vp1), (nm2, nm1, m0, np1, np2)),
        ):
            a0 = coefficients(s_0)
            am1 = coefficients(s_m1)
            o0 = q_0 * q_p1
            om1 = q_m1 * q_0
            here = [o0 * a0[k] for k in range(4)]
            back = [om1 * am1[k] for k in range(4)]
            ahead0 = (q_p1 * q_p2) * coefficients(s_p1)[0]
            behind3 = (q_m2 * q_m1) * coefficients(s_m2)[3]
            w[base + 0, kk] = back[0]
            w[base + 1, kk] = back[1] - here[0]
            w[base + 2, kk] = back[3] - here[2]
            w[base + 3, kk] = -here[3]
            w[8 + base + 0, kk] = -behind3
            w[8 + base + 1, kk] = behind3 - back[2]
            w[8 + base + 2, kk] = here[1] - ahead0
            w[8 + base + 3, kk] = ahead0
            mid = back[2] - here[1]
            centre = mid if centre is None else centre + mid
        m_dn = b0[M, pl.ds(k0, KC), inner, :]
        m_up = b0[M, pl.ds(2 + k0, KC), inner, :]
        z_lo = vertical_mix * (m_dn * m0)
        z_hi = vertical_mix * (m0 * m_up)
        w[16, kk] = z_lo
        w[17, kk] = z_hi
        w[18, kk] = 1.0 + centre - (z_lo + z_hi)
        return carry

    lax.fori_loop(0, levels // KC, weights_body, 0)

    def step(src, xh, f, k0, forward):
        kk = pl.ds(k0, KC)
        c = rows_at(src, f, k0, 0)
        cm2, cm1, cp1, cp2 = shift_x(c, xh[f, kk], xh[f, kk], lane, cols)
        ym2, ym1 = rows_at(src, f, k0, -2), rows_at(src, f, k0, -1)
        yp1, yp2 = rows_at(src, f, k0, 1), rows_at(src, f, k0, 2)
        zm = src[f, pl.ds(k0, KC), inner, :]
        zp = src[f, pl.ds(2 + k0, KC), inner, :]
        o = 0 if forward else 8
        sx = (w[o + 0, kk] * cm2 + w[o + 1, kk] * cm1) + (w[o + 2, kk] * cp1 + w[o + 3, kk] * cp2)
        sy = (w[o + 4, kk] * ym2 + w[o + 5, kk] * ym1) + (w[o + 6, kk] * yp1 + w[o + 7, kk] * yp2)
        sz = w[16, kk] * zm + w[17, kk] * zp
        return (w[18, kk] * c + sz) + (sx + sy)

    def step1_loop(g):
        def body(i, carry):
            k0 = pl.multiple_of(i * KC, KC)
            for f in (2 * g, 2 * g + 1):
                b1[f, pl.ds(1 + k0, KC), inner, :] = step(b0, x0, f, k0, g == 0)
            return carry

        lax.fori_loop(0, levels // KC, body, 0)

    def step2_loop(g):
        def body(i, carry):
            k0 = pl.multiple_of(i * KC, KC)
            for f in (2 * g, 2 * g + 1):
                o_all[f, pl.ds(k0, KC)] = step(b1, x1, f, k0, g == 0)
            return carry

        lax.fori_loop(0, levels // KC, body, 0)

    receive(1)
    step1_loop(0)
    send(2)
    step1_loop(1)
    send(3)
    finish_sends(0)
    finish_sends(1)
    receive(2)
    step2_loop(0)
    receive(3)
    step2_loop(1)
    finish_sends(2)
    finish_sends(3)


def split_kernel(stacked, o_t, o_s, o_ct, o_cs, sem):
    copies = []
    for f, dst in enumerate((o_t, o_s, o_ct, o_cs)):
        cp = pltpu.make_async_copy(stacked.at[f], dst, sem.at[f])
        cp.start()
        copies.append(cp)
    for cp in copies:
        cp.wait()


def local(n_ew, n_ns, temp, salt, u_east, v_north, wet, cot_temp, cot_salt):
    levels, rows, cols = temp.shape
    f32 = jnp.float32
    any_spec = pl.BlockSpec(memory_space=pl.ANY)
    vmem_spec = pl.BlockSpec(memory_space=pltpu.VMEM)
    out = jax.ShapeDtypeStruct((levels, rows, cols), f32)
    call = pl.pallas_call(
        functools.partial(kernel, n_ew, n_ns, levels, rows, cols),
        out_shape=jax.ShapeDtypeStruct((N_TRACERS, levels, rows, cols), f32),
        in_specs=[any_spec] * 6 + [vmem_spec],
        out_specs=vmem_spec,
        scratch_shapes=[
            pltpu.VMEM((N_FIELDS, levels + 2, rows + 2 * PAD, cols), f32),
            pltpu.VMEM((X_FIELDS, levels, rows, cols), f32),
            pltpu.VMEM((X_FIELDS, cols, levels * rows), f32),
            pltpu.VMEM((X_FIELDS, cols, levels * rows), f32),
            pltpu.VMEM((N_TRACERS, levels + 2, rows + 2 * PAD, cols), f32),
            pltpu.VMEM((N_TRACERS, levels, rows, cols), f32),
            pltpu.VMEM((N_TRACERS, cols, levels * rows), f32),
            pltpu.VMEM((N_TRACERS, cols, levels * rows), f32),
            pltpu.VMEM((19, levels, rows, cols), f32),
            pltpu.SemaphoreType.DMA((6,)),
            pltpu.SemaphoreType.DMA((4, 4)),
            pltpu.SemaphoreType.DMA((4, 4)),
        ],
        compiler_params=pltpu.CompilerParams(
            collective_id=0, has_side_effects=True, vmem_limit_bytes=56 * 1024 * 1024
        ),
    )
    stacked = call(temp, salt, cot_temp, cot_salt, u_east, v_north, wet)
    return pl.pallas_call(
        split_kernel,
        out_shape=(out,) * 4,
        in_specs=[vmem_spec],
        out_specs=(any_spec,) * 4,
        scratch_shapes=[pltpu.SemaphoreType.DMA((4,))],
    )(stacked)


def solution(mesh):
    spec = P(None, "ns", "ew")
    n_ew = mesh.shape["ew"]
    n_ns = mesh.shape["ns"]
    return jax.shard_map(
        functools.partial(local, n_ew, n_ns), mesh=mesh,
        in_specs=(spec,) * 7, out_specs=(spec,) * 4, check_vma=False,
    )
```

```python
import functools

import jax
import jax.numpy as jnp
from jax import lax
from jax.experimental import pallas as pl
from jax.experimental.pallas import tpu as pltpu
from jax.sharding import PartitionSpec as P

horizontal_mix = 0.05
vertical_mix = 0.2

PAD = 8
KC = 2
N_FIELDS = 7
X_FIELDS = 6
N_TRACERS = 4
U, M, V = 4, 5, 6
MESH = pl.DeviceIdType.MESH


def coefficients(speed):
    magnitude = jnp.abs(speed)
    return (
        (-speed - magnitude) / 12.0,
        (7.0 * speed + 3.0 * magnitude) / 12.0 + horizontal_mix,
        (7.0 * speed - 3.0 * magnitude) / 12.0 - horizontal_mix,
        (-speed + magnitude) / 12.0,
    )


def shift_x(c, left, right, lane, cols):
    cm1 = pltpu.roll(jnp.where(lane >= cols - 1, left, c), 1, 2)
    cm2 = pltpu.roll(jnp.where(lane >= cols - 2, left, c), 2, 2)
    cp1 = pltpu.roll(jnp.where(lane < 1, right, c), cols - 1, 2)
    cp2 = pltpu.roll(jnp.where(lane < 2, right, c), cols - 2, 2)
    return cm2, cm1, cp1, cp2


def kernel(n_ew, n_ns, levels, rows, cols,
           t_hbm, s_hbm, ct_hbm, cs_hbm, u_hbm, v_hbm, wet_ref,
           o_all,
           b0, x0, ts0, rt0, b1, x1, ts1, rt1, w, load_sem, send_sem, recv_sem):
    ew = lax.axis_index("ew")
    ns = lax.axis_index("ns")
    east = (lax.rem(ew + 1, n_ew), ns)
    west = (lax.rem(ew + n_ew - 1, n_ew), ns)
    north = (ew, jnp.minimum(ns + 1, n_ns - 1))
    south = (ew, jnp.maximum(ns - 1, 0))
    has_north = ns < n_ns - 1
    has_south = ns > 0
    inner = pl.ds(PAD, rows)
    lev = pl.ds(1, levels)

    barrier = pltpu.get_barrier_semaphore()
    pl.semaphore_signal(barrier, 1, device_id=east, device_id_type=MESH)
    pl.semaphore_signal(barrier, 1, device_id=west, device_id_type=MESH)

    @pl.when(has_north)
    def _():
        pl.semaphore_signal(barrier, 1, device_id=north, device_id_type=MESH)

    @pl.when(has_south)
    def _():
        pl.semaphore_signal(barrier, 1, device_id=south, device_id_type=MESH)

    loads = []
    fields = ((0, t_hbm), (1, s_hbm), (2, ct_hbm), (3, cs_hbm), (U, u_hbm), (V, v_hbm))
    for j, (f, src) in enumerate(fields):
        cp = pltpu.make_async_copy(src, b0.at[f, lev, inner, :], load_sem.at[j])
        cp.start()
        loads.append(cp)

    for buf, nf in ((b0, N_FIELDS), (b1, N_TRACERS)):
        zl = jnp.zeros((nf, 1, rows + 2 * PAD, cols), jnp.float32)
        buf[:, pl.ds(0, 1), :, :] = zl
        buf[:, pl.ds(levels + 1, 1), :, :] = zl
        zr = jnp.zeros((nf, levels, 2, cols), jnp.float32)

        @pl.when(jnp.logical_not(has_south))
        def _():
            buf[:, lev, pl.ds(PAD - 2, 2), :] = zr

        @pl.when(jnp.logical_not(has_north))
        def _():
            buf[:, lev, pl.ds(PAD + rows, 2), :] = zr

    b0[M, lev, inner, :] = wet_ref[...].astype(jnp.float32)
    for cp in loads:
        cp.wait()

    peers = 2 + has_north.astype(jnp.int32) + has_south.astype(jnp.int32)
    pl.semaphore_wait(barrier, peers)

    def group(r):
        if r == 0:
            return b0, ts0, rt0, x0, pl.ds(M, 2), pl.ds(U, 2)
        if r == 1:
            return b0, ts0, rt0, x0, pl.ds(0, N_TRACERS), pl.ds(0, N_TRACERS)
        g = pl.ds(2 * (r - 2), 2)
        return b1, ts1, rt1, x1, g, g

    def edge_copy(r, d, dev):
        buf, ts, rt, _, fy, fx = group(r)
        if d == 0:
            src = buf.at[fy, lev, pl.ds(PAD + rows - 2, 2), :]
            dst = buf.at[fy, lev, pl.ds(PAD - 2, 2), :]
        elif d == 1:
            src = buf.at[fy, lev, pl.ds(PAD, 2), :]
            dst = buf.at[fy, lev, pl.ds(PAD + rows, 2), :]
        elif d == 2:
            src = ts.at[fx, pl.ds(cols - 2, 2), :]
            dst = rt.at[fx, pl.ds(cols - 2, 2), :]
        else:
            src = ts.at[fx, pl.ds(0, 2), :]
            dst = rt.at[fx, pl.ds(0, 2), :]
        return pltpu.make_async_remote_copy(
            src_ref=src, dst_ref=dst, send_sem=send_sem.at[r, d], recv_sem=recv_sem.at[r, d],
            device_id=dev, device_id_type=MESH,
        )

    def x_fields(r):
        if r == 0:
            return (U, M)
        if r == 1:
            return range(N_TRACERS)
        return range(2 * (r - 2), 2 * (r - 1))

    outgoing = ((0, north, has_north), (1, south, has_south), (2, east, None), (3, west, None))
    incoming = ((0, south, has_south), (1, north, has_north), (2, west, None), (3, east, None))

    def each(r, pairs, action):
        for d, dev, cond in pairs:
            if cond is None:
                action(edge_copy(r, d, dev))
            else:
                pl.when(cond)(lambda d=d, dev=dev: action(edge_copy(r, d, dev)))

    def send_rows(r):
        each(r, outgoing[:2], lambda c: c.start())

    def send_columns(r):
        buf, ts = group(r)[:2]
        for f in x_fields(r):
            ts[f] = buf[f, lev, inner, :].reshape(levels * rows, cols).T
        each(r, outgoing[2:], lambda c: c.start())

    def send(r):
        send_rows(r)
        send_columns(r)

    def receive(r):
        rt, x = group(r)[2:4]
        each(r, incoming, lambda c: c.wait_recv())
        for f in x_fields(r):
            x[f] = rt[f].T.reshape(levels, rows, cols)

    def finish_sends(r):
        each(r, outgoing, lambda c: c.wait_send())

    send_rows(0)
    send_rows(1)
    send_columns(0)
    send_columns(1)
    receive(0)

    lane = lax.broadcasted_iota(jnp.int32, (KC, rows, cols), 2)

    def rows_at(buf, f, k0, d):
        return buf[f, pl.ds(1 + k0, KC), pl.ds(PAD + d, rows), :]

    def weights_body(i, carry):
        k0 = pl.multiple_of(i * KC, KC)
        kk = pl.ds(k0, KC)
        u0 = rows_at(b0, U, k0, 0)
        um2, um1, up1, _ = shift_x(u0, x0[U, kk], x0[U, kk], lane, cols)
        m0 = rows_at(b0, M, k0, 0)
        mm2, mm1, mp1, mp2 = shift_x(m0, x0[M, kk], x0[M, kk], lane, cols)
        v0 = rows_at(b0, V, k0, 0)
        vm1, vm2, vp1 = rows_at(b0, V, k0, -1), rows_at(b0, V, k0, -2), rows_at(b0, V, k0, 1)
        nm2, nm1 = rows_at(b0, M, k0, -2), rows_at(b0, M, k0, -1)
        np1, np2 = rows_at(b0, M, k0, 1), rows_at(b0, M, k0, 2)
        centre = None
        for base, (s_m2, s_m1, s_0, s_p1), (q_m2, q_m1, q_0, q_p1, q_p2) in (
            (0, (um2, um1, u0, up1), (mm2, mm1, m0, mp1, mp2)),
            (4, (vm2, vm1, v0, vp1), (nm2, nm1, m0, np1, np2)),
        ):
            a0 = coefficients(s_0)
            am1 = coefficients(s_m1)
            o0 = q_0 * q_p1
            om1 = q_m1 * q_0
            here = [o0 * a0[k] for k in range(4)]
            back = [om1 * am1[k] for k in range(4)]
            ahead0 = (q_p1 * q_p2) * coefficients(s_p1)[0]
            behind3 = (q_m2 * q_m1) * coefficients(s_m2)[3]
            w[base + 0, kk] = back[0]
            w[base + 1, kk] = back[1] - here[0]
            w[base + 2, kk] = back[3] - here[2]
            w[base + 3, kk] = -here[3]
            w[8 + base + 0, kk] = -behind3
            w[8 + base + 1, kk] = behind3 - back[2]
            w[8 + base + 2, kk] = here[1] - ahead0
            w[8 + base + 3, kk] = ahead0
            mid = back[2] - here[1]
            centre = mid if centre is None else centre + mid
        m_dn = b0[M, pl.ds(k0, KC), inner, :]
        m_up = b0[M, pl.ds(2 + k0, KC), inner, :]
        z_lo = vertical_mix * (m_dn * m0)
        z_hi = vertical_mix * (m0 * m_up)
        w[16, kk] = z_lo
        w[17, kk] = z_hi
        w[18, kk] = 1.0 + centre - (z_lo + z_hi)
        return carry

    lax.fori_loop(0, levels // KC, weights_body, 0)

    def step(src, xh, f, k0, forward):
        kk = pl.ds(k0, KC)
        c = rows_at(src, f, k0, 0)
        cm2, cm1, cp1, cp2 = shift_x(c, xh[f, kk], xh[f, kk], lane, cols)
        ym2, ym1 = rows_at(src, f, k0, -2), rows_at(src, f, k0, -1)
        yp1, yp2 = rows_at(src, f, k0, 1), rows_at(src, f, k0, 2)
        zm = src[f, pl.ds(k0, KC), inner, :]
        zp = src[f, pl.ds(2 + k0, KC), inner, :]
        o = 0 if forward else 8
        sx = (w[o + 0, kk] * cm2 + w[o + 1, kk] * cm1) + (w[o + 2, kk] * cp1 + w[o + 3, kk] * cp2)
        sy = (w[o + 4, kk] * ym2 + w[o + 5, kk] * ym1) + (w[o + 6, kk] * yp1 + w[o + 7, kk] * yp2)
        sz = w[16, kk] * zm + w[17, kk] * zp
        return (w[18, kk] * c + sz) + (sx + sy)

    def step1_loop(g):
        def body(i, carry):
            k0 = pl.multiple_of(i * KC, KC)
            for f in (2 * g, 2 * g + 1):
                b1[f, pl.ds(1 + k0, KC), inner, :] = step(b0, x0, f, k0, g == 0)
            return carry

        lax.fori_loop(0, levels // KC, body, 0)

    def step2_loop(g):
        def body(i, carry):
            k0 = pl.multiple_of(i * KC, KC)
            for f in (2 * g, 2 * g + 1):
                o_all[f, pl.ds(k0, KC)] = step(b1, x1, f, k0, g == 0)
            return carry

        lax.fori_loop(0, levels // KC, body, 0)

    receive(1)
    step1_loop(0)
    send(2)
    step1_loop(1)
    send(3)
    finish_sends(0)
    finish_sends(1)
    receive(2)
    step2_loop(0)
    receive(3)
    step2_loop(1)
    finish_sends(2)
    finish_sends(3)


def split_kernel(stacked, o_t, o_s, o_ct, o_cs, sem):
    copies = []
    for f, dst in enumerate((o_t, o_s, o_ct, o_cs)):
        cp = pltpu.make_async_copy(stacked.at[f], dst, sem.at[f])
        cp.start()
        copies.append(cp)
    for cp in copies:
        cp.wait()


def local(n_ew, n_ns, temp, salt, u_east, v_north, wet, cot_temp, cot_salt):
    levels, rows, cols = temp.shape
    f32 = jnp.float32
    any_spec = pl.BlockSpec(memory_space=pl.ANY)
    vmem_spec = pl.BlockSpec(memory_space=pltpu.VMEM)
    out = jax.ShapeDtypeStruct((levels, rows, cols), f32)
    call = pl.pallas_call(
        functools.partial(kernel, n_ew, n_ns, levels, rows, cols),
        out_shape=jax.ShapeDtypeStruct((N_TRACERS, levels, rows, cols), f32),
        in_specs=[any_spec] * 6 + [vmem_spec],
        out_specs=vmem_spec,
        scratch_shapes=[
            pltpu.VMEM((N_FIELDS, levels + 2, rows + 2 * PAD, cols), f32),
            pltpu.VMEM((X_FIELDS, levels, rows, cols), f32),
            pltpu.VMEM((X_FIELDS, cols, levels * rows), f32),
            pltpu.VMEM((X_FIELDS, cols, levels * rows), f32),
            pltpu.VMEM((N_TRACERS, levels + 2, rows + 2 * PAD, cols), f32),
            pltpu.VMEM((N_TRACERS, levels, rows, cols), f32),
            pltpu.VMEM((N_TRACERS, cols, levels * rows), f32),
            pltpu.VMEM((N_TRACERS, cols, levels * rows), f32),
            pltpu.VMEM((19, levels, rows, cols), f32),
            pltpu.SemaphoreType.DMA((6,)),
            pltpu.SemaphoreType.DMA((4, 4)),
            pltpu.SemaphoreType.DMA((4, 4)),
        ],
        compiler_params=pltpu.CompilerParams(
            collective_id=0, has_side_effects=True, vmem_limit_bytes=56 * 1024 * 1024
        ),
    )
    stacked = call(temp, salt, cot_temp, cot_salt, u_east, v_north, wet)
    return pl.pallas_call(
        split_kernel,
        out_shape=(out,) * 4,
        in_specs=[any_spec],
        out_specs=(any_spec,) * 4,
        scratch_shapes=[pltpu.SemaphoreType.DMA((4,))],
    )(stacked)


def solution(mesh):
    spec = P(None, "ns", "ew")
    n_ew = mesh.shape["ew"]
    n_ns = mesh.shape["ns"]
    return jax.shard_map(
        functools.partial(local, n_ew, n_ns), mesh=mesh,
        in_specs=(spec,) * 7, out_specs=(spec,) * 4, check_vma=False,
    )
```

```python
import functools

import jax
import jax.numpy as jnp
from jax import lax
from jax.experimental import pallas as pl
from jax.experimental.pallas import tpu as pltpu
from jax.sharding import PartitionSpec as P

horizontal_mix = 0.05
vertical_mix = 0.2

PAD = 8
KC = 8
N_FIELDS = 7
X_FIELDS = 6
N_TRACERS = 4
U, M, V = 4, 5, 6
MESH = pl.DeviceIdType.MESH


def coefficients(speed):
    magnitude = jnp.abs(speed)
    return (
        (-speed - magnitude) / 12.0,
        (7.0 * speed + 3.0 * magnitude) / 12.0 + horizontal_mix,
        (7.0 * speed - 3.0 * magnitude) / 12.0 - horizontal_mix,
        (-speed + magnitude) / 12.0,
    )


def shift_x(c, left, right, lane, cols):
    cm1 = pltpu.roll(jnp.where(lane >= cols - 1, left, c), 1, 2)
    cm2 = pltpu.roll(jnp.where(lane >= cols - 2, left, c), 2, 2)
    cp1 = pltpu.roll(jnp.where(lane < 1, right, c), cols - 1, 2)
    cp2 = pltpu.roll(jnp.where(lane < 2, right, c), cols - 2, 2)
    return cm2, cm1, cp1, cp2


def kernel(n_ew, n_ns, levels, rows, cols,
           t_hbm, s_hbm, ct_hbm, cs_hbm, u_hbm, v_hbm, wet_ref,
           o_all,
           b0, x0, ts0, rt0, b1, x1, ts1, rt1, w, load_sem, send_sem, recv_sem):
    ew = lax.axis_index("ew")
    ns = lax.axis_index("ns")
    east = (lax.rem(ew + 1, n_ew), ns)
    west = (lax.rem(ew + n_ew - 1, n_ew), ns)
    north = (ew, jnp.minimum(ns + 1, n_ns - 1))
    south = (ew, jnp.maximum(ns - 1, 0))
    has_north = ns < n_ns - 1
    has_south = ns > 0
    inner = pl.ds(PAD, rows)
    lev = pl.ds(1, levels)

    barrier = pltpu.get_barrier_semaphore()
    pl.semaphore_signal(barrier, 1, device_id=east, device_id_type=MESH)
    pl.semaphore_signal(barrier, 1, device_id=west, device_id_type=MESH)

    @pl.when(has_north)
    def _():
        pl.semaphore_signal(barrier, 1, device_id=north, device_id_type=MESH)

    @pl.when(has_south)
    def _():
        pl.semaphore_signal(barrier, 1, device_id=south, device_id_type=MESH)

    loads = []
    fields = ((0, t_hbm), (1, s_hbm), (2, ct_hbm), (3, cs_hbm), (U, u_hbm), (V, v_hbm))
    for j, (f, src) in enumerate(fields):
        cp = pltpu.make_async_copy(src, b0.at[f, lev, inner, :], load_sem.at[j])
        cp.start()
        loads.append(cp)

    for buf, nf in ((b0, N_FIELDS), (b1, N_TRACERS)):
        zl = jnp.zeros((nf, 1, rows + 2 * PAD, cols), jnp.float32)
        buf[:, pl.ds(0, 1), :, :] = zl
        buf[:, pl.ds(levels + 1, 1), :, :] = zl
        zr = jnp.zeros((nf, levels, 2, cols), jnp.float32)

        @pl.when(jnp.logical_not(has_south))
        def _():
            buf[:, lev, pl.ds(PAD - 2, 2), :] = zr

        @pl.when(jnp.logical_not(has_north))
        def _():
            buf[:, lev, pl.ds(PAD + rows, 2), :] = zr

    b0[M, lev, inner, :] = wet_ref[...].astype(jnp.float32)
    for cp in loads:
        cp.wait()

    peers = 2 + has_north.astype(jnp.int32) + has_south.astype(jnp.int32)
    pl.semaphore_wait(barrier, peers)

    def group(r):
        if r == 0:
            return b0, ts0, rt0, x0, pl.ds(M, 2), pl.ds(U, 2)
        if r == 1:
            return b0, ts0, rt0, x0, pl.ds(0, N_TRACERS), pl.ds(0, N_TRACERS)
        g = pl.ds(2 * (r - 2), 2)
        return b1, ts1, rt1, x1, g, g

    def edge_copy(r, d, dev):
        buf, ts, rt, _, fy, fx = group(r)
        if d == 0:
            src = buf.at[fy, lev, pl.ds(PAD + rows - 2, 2), :]
            dst = buf.at[fy, lev, pl.ds(PAD - 2, 2), :]
        elif d == 1:
            src = buf.at[fy, lev, pl.ds(PAD, 2), :]
            dst = buf.at[fy, lev, pl.ds(PAD + rows, 2), :]
        elif d == 2:
            src = ts.at[fx, pl.ds(cols - 2, 2), :]
            dst = rt.at[fx, pl.ds(cols - 2, 2), :]
        else:
            src = ts.at[fx, pl.ds(0, 2), :]
            dst = rt.at[fx, pl.ds(0, 2), :]
        return pltpu.make_async_remote_copy(
            src_ref=src, dst_ref=dst, send_sem=send_sem.at[r, d], recv_sem=recv_sem.at[r, d],
            device_id=dev, device_id_type=MESH,
        )

    def x_fields(r):
        if r == 0:
            return (U, M)
        if r == 1:
            return range(N_TRACERS)
        return range(2 * (r - 2), 2 * (r - 1))

    outgoing = ((0, north, has_north), (1, south, has_south), (2, east, None), (3, west, None))
    incoming = ((0, south, has_south), (1, north, has_north), (2, west, None), (3, east, None))

    def each(r, pairs, action):
        for d, dev, cond in pairs:
            if cond is None:
                action(edge_copy(r, d, dev))
            else:
                pl.when(cond)(lambda d=d, dev=dev: action(edge_copy(r, d, dev)))

    def send_rows(r):
        each(r, outgoing[:2], lambda c: c.start())

    def send_columns(r):
        buf, ts = group(r)[:2]
        for f in x_fields(r):
            ts[f] = buf[f, lev, inner, :].reshape(levels * rows, cols).T
        each(r, outgoing[2:], lambda c: c.start())

    def send(r):
        send_rows(r)
        send_columns(r)

    def receive(r):
        rt, x = group(r)[2:4]
        each(r, incoming, lambda c: c.wait_recv())
        for f in x_fields(r):
            x[f] = rt[f].T.reshape(levels, rows, cols)

    def finish_sends(r):
        each(r, outgoing, lambda c: c.wait_send())

    send_rows(0)
    send_rows(1)
    send_columns(0)
    send_columns(1)
    receive(0)

    lane = lax.broadcasted_iota(jnp.int32, (KC, rows, cols), 2)

    def rows_at(buf, f, k0, d):
        return buf[f, pl.ds(1 + k0, KC), pl.ds(PAD + d, rows), :]

    def weights_body(i, carry):
        k0 = pl.multiple_of(i * KC, KC)
        kk = pl.ds(k0, KC)
        u0 = rows_at(b0, U, k0, 0)
        um2, um1, up1, _ = shift_x(u0, x0[U, kk], x0[U, kk], lane, cols)
        m0 = rows_at(b0, M, k0, 0)
        mm2, mm1, mp1, mp2 = shift_x(m0, x0[M, kk], x0[M, kk], lane, cols)
        v0 = rows_at(b0, V, k0, 0)
        vm1, vm2, vp1 = rows_at(b0, V, k0, -1), rows_at(b0, V, k0, -2), rows_at(b0, V, k0, 1)
        nm2, nm1 = rows_at(b0, M, k0, -2), rows_at(b0, M, k0, -1)
        np1, np2 = rows_at(b0, M, k0, 1), rows_at(b0, M, k0, 2)
        centre = None
        for base, (s_m2, s_m1, s_0, s_p1), (q_m2, q_m1, q_0, q_p1, q_p2) in (
            (0, (um2, um1, u0, up1), (mm2, mm1, m0, mp1, mp2)),
            (4, (vm2, vm1, v0, vp1), (nm2, nm1, m0, np1, np2)),
        ):
            a0 = coefficients(s_0)
            am1 = coefficients(s_m1)
            o0 = q_0 * q_p1
            om1 = q_m1 * q_0
            here = [o0 * a0[k] for k in range(4)]
            back = [om1 * am1[k] for k in range(4)]
            ahead0 = (q_p1 * q_p2) * coefficients(s_p1)[0]
            behind3 = (q_m2 * q_m1) * coefficients(s_m2)[3]
            w[base + 0, kk] = back[0]
            w[base + 1, kk] = back[1] - here[0]
            w[base + 2, kk] = back[3] - here[2]
            w[base + 3, kk] = -here[3]
            w[8 + base + 0, kk] = -behind3
            w[8 + base + 1, kk] = behind3 - back[2]
            w[8 + base + 2, kk] = here[1] - ahead0
            w[8 + base + 3, kk] = ahead0
            mid = back[2] - here[1]
            centre = mid if centre is None else centre + mid
        m_dn = b0[M, pl.ds(k0, KC), inner, :]
        m_up = b0[M, pl.ds(2 + k0, KC), inner, :]
        z_lo = vertical_mix * (m_dn * m0)
        z_hi = vertical_mix * (m0 * m_up)
        w[16, kk] = z_lo
        w[17, kk] = z_hi
        w[18, kk] = 1.0 + centre - (z_lo + z_hi)
        return carry

    lax.fori_loop(0, levels // KC, weights_body, 0)

    def step(src, xh, f, k0, forward):
        kk = pl.ds(k0, KC)
        c = rows_at(src, f, k0, 0)
        cm2, cm1, cp1, cp2 = shift_x(c, xh[f, kk], xh[f, kk], lane, cols)
        ym2, ym1 = rows_at(src, f, k0, -2), rows_at(src, f, k0, -1)
        yp1, yp2 = rows_at(src, f, k0, 1), rows_at(src, f, k0, 2)
        zm = src[f, pl.ds(k0, KC), inner, :]
        zp = src[f, pl.ds(2 + k0, KC), inner, :]
        o = 0 if forward else 8
        sx = (w[o + 0, kk] * cm2 + w[o + 1, kk] * cm1) + (w[o + 2, kk] * cp1 + w[o + 3, kk] * cp2)
        sy = (w[o + 4, kk] * ym2 + w[o + 5, kk] * ym1) + (w[o + 6, kk] * yp1 + w[o + 7, kk] * yp2)
        sz = w[16, kk] * zm + w[17, kk] * zp
        return (w[18, kk] * c + sz) + (sx + sy)

    def step1_loop(g):
        def body(i, carry):
            k0 = pl.multiple_of(i * KC, KC)
            for f in (2 * g, 2 * g + 1):
                b1[f, pl.ds(1 + k0, KC), inner, :] = step(b0, x0, f, k0, g == 0)
            return carry

        lax.fori_loop(0, levels // KC, body, 0)

    def step2_loop(g):
        def body(i, carry):
            k0 = pl.multiple_of(i * KC, KC)
            for f in (2 * g, 2 * g + 1):
                o_all[f, pl.ds(k0, KC)] = step(b1, x1, f, k0, g == 0)
            return carry

        lax.fori_loop(0, levels // KC, body, 0)

    receive(1)
    step1_loop(0)
    send(2)
    step1_loop(1)
    send(3)
    finish_sends(0)
    finish_sends(1)
    receive(2)
    step2_loop(0)
    receive(3)
    step2_loop(1)
    finish_sends(2)
    finish_sends(3)


def split_kernel(stacked, o_t, o_s, o_ct, o_cs, sem):
    copies = []
    for f, dst in enumerate((o_t, o_s, o_ct, o_cs)):
        cp = pltpu.make_async_copy(stacked.at[f], dst, sem.at[f])
        cp.start()
        copies.append(cp)
    for cp in copies:
        cp.wait()


def local(n_ew, n_ns, temp, salt, u_east, v_north, wet, cot_temp, cot_salt):
    levels, rows, cols = temp.shape
    f32 = jnp.float32
    any_spec = pl.BlockSpec(memory_space=pl.ANY)
    vmem_spec = pl.BlockSpec(memory_space=pltpu.VMEM)
    out = jax.ShapeDtypeStruct((levels, rows, cols), f32)
    call = pl.pallas_call(
        functools.partial(kernel, n_ew, n_ns, levels, rows, cols),
        out_shape=jax.ShapeDtypeStruct((N_TRACERS, levels, rows, cols), f32),
        in_specs=[any_spec] * 6 + [vmem_spec],
        out_specs=vmem_spec,
        scratch_shapes=[
            pltpu.VMEM((N_FIELDS, levels + 2, rows + 2 * PAD, cols), f32),
            pltpu.VMEM((X_FIELDS, levels, rows, cols), f32),
            pltpu.VMEM((X_FIELDS, cols, levels * rows), f32),
            pltpu.VMEM((X_FIELDS, cols, levels * rows), f32),
            pltpu.VMEM((N_TRACERS, levels + 2, rows + 2 * PAD, cols), f32),
            pltpu.VMEM((N_TRACERS, levels, rows, cols), f32),
            pltpu.VMEM((N_TRACERS, cols, levels * rows), f32),
            pltpu.VMEM((N_TRACERS, cols, levels * rows), f32),
            pltpu.VMEM((19, levels, rows, cols), f32),
            pltpu.SemaphoreType.DMA((6,)),
            pltpu.SemaphoreType.DMA((4, 4)),
            pltpu.SemaphoreType.DMA((4, 4)),
        ],
        compiler_params=pltpu.CompilerParams(
            collective_id=0, has_side_effects=True, vmem_limit_bytes=56 * 1024 * 1024
        ),
    )
    stacked = call(temp, salt, cot_temp, cot_salt, u_east, v_north, wet)
    return pl.pallas_call(
        split_kernel,
        out_shape=(out,) * 4,
        in_specs=[vmem_spec],
        out_specs=(any_spec,) * 4,
        scratch_shapes=[pltpu.SemaphoreType.DMA((4,))],
    )(stacked)


def solution(mesh):
    spec = P(None, "ns", "ew")
    n_ew = mesh.shape["ew"]
    n_ns = mesh.shape["ns"]
    return jax.shard_map(
        functools.partial(local, n_ew, n_ns), mesh=mesh,
        in_specs=(spec,) * 7, out_specs=(spec,) * 4, check_vma=False,
    )
```

```python
import functools

import jax
import jax.numpy as jnp
from jax import lax
from jax.experimental import pallas as pl
from jax.experimental.pallas import tpu as pltpu
from jax.sharding import PartitionSpec as P

horizontal_mix = 0.05
vertical_mix = 0.2

PAD = 8
KC = 8
N_FIELDS = 7
X_FIELDS = 6
N_TRACERS = 4
U, M, V = 4, 5, 6
MESH = pl.DeviceIdType.MESH


def coefficients(speed):
    magnitude = jnp.abs(speed)
    return (
        (-speed - magnitude) / 12.0,
        (7.0 * speed + 3.0 * magnitude) / 12.0 + horizontal_mix,
        (7.0 * speed - 3.0 * magnitude) / 12.0 - horizontal_mix,
        (-speed + magnitude) / 12.0,
    )


def shift_x(c, left, right, lane, cols):
    cm1 = pltpu.roll(jnp.where(lane >= cols - 1, left, c), 1, 2)
    cm2 = pltpu.roll(jnp.where(lane >= cols - 2, left, c), 2, 2)
    cp1 = pltpu.roll(jnp.where(lane < 1, right, c), cols - 1, 2)
    cp2 = pltpu.roll(jnp.where(lane < 2, right, c), cols - 2, 2)
    return cm2, cm1, cp1, cp2


def kernel(n_ew, n_ns, levels, rows, cols,
           t_hbm, s_hbm, ct_hbm, cs_hbm, u_hbm, v_hbm, wet_ref,
           o_all,
           b0, x0, ts0, rt0, b1, x1, ts1, rt1, w, load_sem, send_sem, recv_sem):
    ew = lax.axis_index("ew")
    ns = lax.axis_index("ns")
    east = (lax.rem(ew + 1, n_ew), ns)
    west = (lax.rem(ew + n_ew - 1, n_ew), ns)
    north = (ew, jnp.minimum(ns + 1, n_ns - 1))
    south = (ew, jnp.maximum(ns - 1, 0))
    has_north = ns < n_ns - 1
    has_south = ns > 0
    inner = pl.ds(PAD, rows)
    lev = pl.ds(1, levels)

    barrier = pltpu.get_barrier_semaphore()
    pl.semaphore_signal(barrier, 1, device_id=east, device_id_type=MESH)
    pl.semaphore_signal(barrier, 1, device_id=west, device_id_type=MESH)

    @pl.when(has_north)
    def _():
        pl.semaphore_signal(barrier, 1, device_id=north, device_id_type=MESH)

    @pl.when(has_south)
    def _():
        pl.semaphore_signal(barrier, 1, device_id=south, device_id_type=MESH)

    loads = []
    fields = ((0, t_hbm), (1, s_hbm), (2, ct_hbm), (3, cs_hbm), (U, u_hbm), (V, v_hbm))
    for j, (f, src) in enumerate(fields):
        cp = pltpu.make_async_copy(src, b0.at[f, lev, inner, :], load_sem.at[j])
        cp.start()
        loads.append(cp)

    for buf, nf in ((b0, N_FIELDS), (b1, N_TRACERS)):
        zl = jnp.zeros((nf, 1, rows + 2 * PAD, cols), jnp.float32)
        buf[:, pl.ds(0, 1), :, :] = zl
        buf[:, pl.ds(levels + 1, 1), :, :] = zl
        zr = jnp.zeros((nf, levels, 2, cols), jnp.float32)

        @pl.when(jnp.logical_not(has_south))
        def _():
            buf[:, lev, pl.ds(PAD - 2, 2), :] = zr

        @pl.when(jnp.logical_not(has_north))
        def _():
            buf[:, lev, pl.ds(PAD + rows, 2), :] = zr

    b0[M, lev, inner, :] = wet_ref[...].astype(jnp.float32)
    for cp in loads:
        cp.wait()

    peers = 2 + has_north.astype(jnp.int32) + has_south.astype(jnp.int32)
    pl.semaphore_wait(barrier, peers)

    def group(r):
        if r == 0:
            return b0, ts0, rt0, x0, pl.ds(M, 2), pl.ds(U, 2)
        if r == 1:
            return b0, ts0, rt0, x0, pl.ds(0, N_TRACERS), pl.ds(0, N_TRACERS)
        g = pl.ds(2 * (r - 2), 2)
        return b1, ts1, rt1, x1, g, g

    def edge_copy(r, d, dev):
        buf, ts, rt, _, fy, fx = group(r)
        if d == 0:
            src = buf.at[fy, lev, pl.ds(PAD + rows - 2, 2), :]
            dst = buf.at[fy, lev, pl.ds(PAD - 2, 2), :]
        elif d == 1:
            src = buf.at[fy, lev, pl.ds(PAD, 2), :]
            dst = buf.at[fy, lev, pl.ds(PAD + rows, 2), :]
        elif d == 2:
            src = ts.at[fx, pl.ds(cols - 2, 2), :]
            dst = rt.at[fx, pl.ds(cols - 2, 2), :]
        else:
            src = ts.at[fx, pl.ds(0, 2), :]
            dst = rt.at[fx, pl.ds(0, 2), :]
        return pltpu.make_async_remote_copy(
            src_ref=src, dst_ref=dst, send_sem=send_sem.at[r, d], recv_sem=recv_sem.at[r, d],
            device_id=dev, device_id_type=MESH,
        )

    def x_fields(r):
        if r == 0:
            return (U, M)
        if r == 1:
            return range(N_TRACERS)
        return range(2 * (r - 2), 2 * (r - 1))

    outgoing = ((0, north, has_north), (1, south, has_south), (2, east, None), (3, west, None))
    incoming = ((0, south, has_south), (1, north, has_north), (2, west, None), (3, east, None))

    def each(r, pairs, action):
        for d, dev, cond in pairs:
            if cond is None:
                action(edge_copy(r, d, dev))
            else:
                pl.when(cond)(lambda d=d, dev=dev: action(edge_copy(r, d, dev)))

    def send_rows(r):
        each(r, outgoing[:2], lambda c: c.start())

    def send_columns(r):
        buf, ts = group(r)[:2]
        for f in x_fields(r):
            ts[f] = buf[f, lev, inner, :].reshape(levels * rows, cols).T
        each(r, outgoing[2:], lambda c: c.start())

    def send(r):
        send_rows(r)
        send_columns(r)

    def receive(r):
        rt, x = group(r)[2:4]
        each(r, incoming, lambda c: c.wait_recv())
        for f in x_fields(r):
            x[f] = rt[f].T.reshape(levels, rows, cols)

    def finish_sends(r):
        each(r, outgoing, lambda c: c.wait_send())

    send_rows(0)
    send_rows(1)
    send_columns(0)
    send_columns(1)
    receive(0)

    lane = lax.broadcasted_iota(jnp.int32, (KC, rows, cols), 2)

    def rows_at(buf, f, k0, d):
        return buf[f, pl.ds(1 + k0, KC), pl.ds(PAD + d, rows), :]

    def weights_body(i, carry):
        k0 = pl.multiple_of(i * KC, KC)
        kk = pl.ds(k0, KC)
        u0 = rows_at(b0, U, k0, 0)
        um2, um1, up1, _ = shift_x(u0, x0[U, kk], x0[U, kk], lane, cols)
        m0 = rows_at(b0, M, k0, 0)
        mm2, mm1, mp1, mp2 = shift_x(m0, x0[M, kk], x0[M, kk], lane, cols)
        v0 = rows_at(b0, V, k0, 0)
        vm1, vm2, vp1 = rows_at(b0, V, k0, -1), rows_at(b0, V, k0, -2), rows_at(b0, V, k0, 1)
        nm2, nm1 = rows_at(b0, M, k0, -2), rows_at(b0, M, k0, -1)
        np1, np2 = rows_at(b0, M, k0, 1), rows_at(b0, M, k0, 2)
        centre = None
        for base, (s_m2, s_m1, s_0, s_p1), (q_m2, q_m1, q_0, q_p1, q_p2) in (
            (0, (um2, um1, u0, up1), (mm2, mm1, m0, mp1, mp2)),
            (4, (vm2, vm1, v0, vp1), (nm2, nm1, m0, np1, np2)),
        ):
            a0 = coefficients(s_0)
            am1 = coefficients(s_m1)
            o0 = q_0 * q_p1
            om1 = q_m1 * q_0
            here = [o0 * a0[k] for k in range(4)]
            back = [om1 * am1[k] for k in range(4)]
            ahead0 = (q_p1 * q_p2) * coefficients(s_p1)[0]
            behind3 = (q_m2 * q_m1) * coefficients(s_m2)[3]
            w[base + 0, kk] = back[0]
            w[base + 1, kk] = back[1] - here[0]
            w[base + 2, kk] = back[3] - here[2]
            w[base + 3, kk] = -here[3]
            w[8 + base + 0, kk] = -behind3
            w[8 + base + 1, kk] = behind3 - back[2]
            w[8 + base + 2, kk] = here[1] - ahead0
            w[8 + base + 3, kk] = ahead0
            mid = back[2] - here[1]
            centre = mid if centre is None else centre + mid
        m_dn = b0[M, pl.ds(k0, KC), inner, :]
        m_up = b0[M, pl.ds(2 + k0, KC), inner, :]
        z_lo = vertical_mix * (m_dn * m0)
        z_hi = vertical_mix * (m0 * m_up)
        w[16, kk] = z_lo
        w[17, kk] = z_hi
        w[18, kk] = 1.0 + centre - (z_lo + z_hi)
        return carry

    lax.fori_loop(0, levels // KC, weights_body, 0, unroll=True)

    def step(src, xh, f, k0, forward):
        kk = pl.ds(k0, KC)
        c = rows_at(src, f, k0, 0)
        cm2, cm1, cp1, cp2 = shift_x(c, xh[f, kk], xh[f, kk], lane, cols)
        ym2, ym1 = rows_at(src, f, k0, -2), rows_at(src, f, k0, -1)
        yp1, yp2 = rows_at(src, f, k0, 1), rows_at(src, f, k0, 2)
        zm = src[f, pl.ds(k0, KC), inner, :]
        zp = src[f, pl.ds(2 + k0, KC), inner, :]
        o = 0 if forward else 8
        sx = (w[o + 0, kk] * cm2 + w[o + 1, kk] * cm1) + (w[o + 2, kk] * cp1 + w[o + 3, kk] * cp2)
        sy = (w[o + 4, kk] * ym2 + w[o + 5, kk] * ym1) + (w[o + 6, kk] * yp1 + w[o + 7, kk] * yp2)
        sz = w[16, kk] * zm + w[17, kk] * zp
        return (w[18, kk] * c + sz) + (sx + sy)

    def step1_loop(g):
        def body(i, carry):
            k0 = pl.multiple_of(i * KC, KC)
            for f in (2 * g, 2 * g + 1):
                b1[f, pl.ds(1 + k0, KC), inner, :] = step(b0, x0, f, k0, g == 0)
            return carry

        lax.fori_loop(0, levels // KC, body, 0, unroll=True)

    def step2_loop(g):
        def body(i, carry):
            k0 = pl.multiple_of(i * KC, KC)
            for f in (2 * g, 2 * g + 1):
                o_all[f, pl.ds(k0, KC)] = step(b1, x1, f, k0, g == 0)
            return carry

        lax.fori_loop(0, levels // KC, body, 0, unroll=True)

    receive(1)
    step1_loop(0)
    send(2)
    step1_loop(1)
    send(3)
    finish_sends(0)
    finish_sends(1)
    receive(2)
    step2_loop(0)
    receive(3)
    step2_loop(1)
    finish_sends(2)
    finish_sends(3)


def split_kernel(stacked, o_t, o_s, o_ct, o_cs, sem):
    copies = []
    for f, dst in enumerate((o_t, o_s, o_ct, o_cs)):
        cp = pltpu.make_async_copy(stacked.at[f], dst, sem.at[f])
        cp.start()
        copies.append(cp)
    for cp in copies:
        cp.wait()


def local(n_ew, n_ns, temp, salt, u_east, v_north, wet, cot_temp, cot_salt):
    levels, rows, cols = temp.shape
    f32 = jnp.float32
    any_spec = pl.BlockSpec(memory_space=pl.ANY)
    vmem_spec = pl.BlockSpec(memory_space=pltpu.VMEM)
    out = jax.ShapeDtypeStruct((levels, rows, cols), f32)
    call = pl.pallas_call(
        functools.partial(kernel, n_ew, n_ns, levels, rows, cols),
        out_shape=jax.ShapeDtypeStruct((N_TRACERS, levels, rows, cols), f32),
        in_specs=[any_spec] * 6 + [vmem_spec],
        out_specs=vmem_spec,
        scratch_shapes=[
            pltpu.VMEM((N_FIELDS, levels + 2, rows + 2 * PAD, cols), f32),
            pltpu.VMEM((X_FIELDS, levels, rows, cols), f32),
            pltpu.VMEM((X_FIELDS, cols, levels * rows), f32),
            pltpu.VMEM((X_FIELDS, cols, levels * rows), f32),
            pltpu.VMEM((N_TRACERS, levels + 2, rows + 2 * PAD, cols), f32),
            pltpu.VMEM((N_TRACERS, levels, rows, cols), f32),
            pltpu.VMEM((N_TRACERS, cols, levels * rows), f32),
            pltpu.VMEM((N_TRACERS, cols, levels * rows), f32),
            pltpu.VMEM((19, levels, rows, cols), f32),
            pltpu.SemaphoreType.DMA((6,)),
            pltpu.SemaphoreType.DMA((4, 4)),
            pltpu.SemaphoreType.DMA((4, 4)),
        ],
        compiler_params=pltpu.CompilerParams(
            collective_id=0, has_side_effects=True, vmem_limit_bytes=56 * 1024 * 1024
        ),
    )
    stacked = call(temp, salt, cot_temp, cot_salt, u_east, v_north, wet)
    return pl.pallas_call(
        split_kernel,
        out_shape=(out,) * 4,
        in_specs=[vmem_spec],
        out_specs=(any_spec,) * 4,
        scratch_shapes=[pltpu.SemaphoreType.DMA((4,))],
    )(stacked)


def solution(mesh):
    spec = P(None, "ns", "ew")
    n_ew = mesh.shape["ew"]
    n_ns = mesh.shape["ns"]
    return jax.shard_map(
        functools.partial(local, n_ew, n_ns), mesh=mesh,
        in_specs=(spec,) * 7, out_specs=(spec,) * 4, check_vma=False,
    )
```

```python
import functools

import jax
import jax.numpy as jnp
from jax import lax
from jax.experimental import pallas as pl
from jax.experimental.pallas import tpu as pltpu
from jax.sharding import PartitionSpec as P

horizontal_mix = 0.05
vertical_mix = 0.2

PAD = 8
KC = 8
N_FIELDS = 7
X_FIELDS = 6
N_TRACERS = 4
U, M, V = 4, 5, 6
MESH = pl.DeviceIdType.MESH


def coefficients(speed):
    magnitude = jnp.abs(speed)
    return (
        (-speed - magnitude) / 12.0,
        (7.0 * speed + 3.0 * magnitude) / 12.0 + horizontal_mix,
        (7.0 * speed - 3.0 * magnitude) / 12.0 - horizontal_mix,
        (-speed + magnitude) / 12.0,
    )


def shift_x(c, left, right, lane, cols):
    cm1 = pltpu.roll(jnp.where(lane >= cols - 1, left, c), 1, 2)
    cm2 = pltpu.roll(jnp.where(lane >= cols - 2, left, c), 2, 2)
    cp1 = pltpu.roll(jnp.where(lane < 1, right, c), cols - 1, 2)
    cp2 = pltpu.roll(jnp.where(lane < 2, right, c), cols - 2, 2)
    return cm2, cm1, cp1, cp2


def kernel(n_ew, n_ns, levels, rows, cols,
           t_hbm, s_hbm, ct_hbm, cs_hbm, u_hbm, v_hbm, wet_ref,
           o_all,
           b0, x0, ts0, rt0, b1, x1, ts1, rt1, w, load_sem, send_sem, recv_sem):
    ew = lax.axis_index("ew")
    ns = lax.axis_index("ns")
    east = (lax.rem(ew + 1, n_ew), ns)
    west = (lax.rem(ew + n_ew - 1, n_ew), ns)
    north = (ew, jnp.minimum(ns + 1, n_ns - 1))
    south = (ew, jnp.maximum(ns - 1, 0))
    has_north = ns < n_ns - 1
    has_south = ns > 0
    inner = pl.ds(PAD, rows)
    lev = pl.ds(1, levels)

    barrier = pltpu.get_barrier_semaphore()
    pl.semaphore_signal(barrier, 1, device_id=east, device_id_type=MESH)
    pl.semaphore_signal(barrier, 1, device_id=west, device_id_type=MESH)

    @pl.when(has_north)
    def _():
        pl.semaphore_signal(barrier, 1, device_id=north, device_id_type=MESH)

    @pl.when(has_south)
    def _():
        pl.semaphore_signal(barrier, 1, device_id=south, device_id_type=MESH)

    loads = []
    fields = ((0, t_hbm), (1, s_hbm), (2, ct_hbm), (3, cs_hbm), (U, u_hbm), (V, v_hbm))
    for j, (f, src) in enumerate(fields):
        cp = pltpu.make_async_copy(src, b0.at[f, lev, inner, :], load_sem.at[j])
        cp.start()
        loads.append(cp)

    for buf, nf in ((b0, N_FIELDS), (b1, N_TRACERS)):
        zl = jnp.zeros((nf, 1, rows + 2 * PAD, cols), jnp.float32)
        buf[:, pl.ds(0, 1), :, :] = zl
        buf[:, pl.ds(levels + 1, 1), :, :] = zl
        zr = jnp.zeros((nf, levels, 2, cols), jnp.float32)

        @pl.when(jnp.logical_not(has_south))
        def _():
            buf[:, lev, pl.ds(PAD - 2, 2), :] = zr

        @pl.when(jnp.logical_not(has_north))
        def _():
            buf[:, lev, pl.ds(PAD + rows, 2), :] = zr

    b0[M, lev, inner, :] = wet_ref[...].astype(jnp.float32)
    for cp in loads:
        cp.wait()

    peers = 2 + has_north.astype(jnp.int32) + has_south.astype(jnp.int32)
    pl.semaphore_wait(barrier, peers)

    def group(r):
        if r == 0:
            return b0, ts0, rt0, x0, pl.ds(M, 2), pl.ds(U, 2)
        g = pl.ds(2 * ((r - 1) % 2), 2)
        if r <= 2:
            return b0, ts0, rt0, x0, g, g
        return b1, ts1, rt1, x1, g, g

    def edge_copy(r, d, dev):
        buf, ts, rt, _, fy, fx = group(r)
        if d == 0:
            src = buf.at[fy, lev, pl.ds(PAD + rows - 2, 2), :]
            dst = buf.at[fy, lev, pl.ds(PAD - 2, 2), :]
        elif d == 1:
            src = buf.at[fy, lev, pl.ds(PAD, 2), :]
            dst = buf.at[fy, lev, pl.ds(PAD + rows, 2), :]
        elif d == 2:
            src = ts.at[fx, pl.ds(cols - 2, 2), :]
            dst = rt.at[fx, pl.ds(cols - 2, 2), :]
        else:
            src = ts.at[fx, pl.ds(0, 2), :]
            dst = rt.at[fx, pl.ds(0, 2), :]
        return pltpu.make_async_remote_copy(
            src_ref=src, dst_ref=dst, send_sem=send_sem.at[r, d], recv_sem=recv_sem.at[r, d],
            device_id=dev, device_id_type=MESH,
        )

    def x_fields(r):
        if r == 0:
            return (U, M)
        g = (r - 1) % 2
        return range(2 * g, 2 * g + 2)

    outgoing = ((0, north, has_north), (1, south, has_south), (2, east, None), (3, west, None))
    incoming = ((0, south, has_south), (1, north, has_north), (2, west, None), (3, east, None))

    def each(r, pairs, action):
        for d, dev, cond in pairs:
            if cond is None:
                action(edge_copy(r, d, dev))
            else:
                pl.when(cond)(lambda d=d, dev=dev: action(edge_copy(r, d, dev)))

    def send_rows(r):
        each(r, outgoing[:2], lambda c: c.start())

    def send_columns(r):
        buf, ts = group(r)[:2]
        for f in x_fields(r):
            ts[f] = buf[f, lev, inner, :].reshape(levels * rows, cols).T
        each(r, outgoing[2:], lambda c: c.start())

    def send(r):
        send_rows(r)
        send_columns(r)

    def receive(r):
        rt, x = group(r)[2:4]
        each(r, incoming, lambda c: c.wait_recv())
        for f in x_fields(r):
            x[f] = rt[f].T.reshape(levels, rows, cols)

    def finish_sends(r):
        each(r, outgoing, lambda c: c.wait_send())

    for r in range(3):
        send_rows(r)
    for r in range(3):
        send_columns(r)
    receive(0)

    lane = lax.broadcasted_iota(jnp.int32, (KC, rows, cols), 2)

    def rows_at(buf, f, k0, d):
        return buf[f, pl.ds(1 + k0, KC), pl.ds(PAD + d, rows), :]

    def weights_body(i, carry):
        k0 = pl.multiple_of(i * KC, KC)
        kk = pl.ds(k0, KC)
        u0 = rows_at(b0, U, k0, 0)
        um2, um1, up1, _ = shift_x(u0, x0[U, kk], x0[U, kk], lane, cols)
        m0 = rows_at(b0, M, k0, 0)
        mm2, mm1, mp1, mp2 = shift_x(m0, x0[M, kk], x0[M, kk], lane, cols)
        v0 = rows_at(b0, V, k0, 0)
        vm1, vm2, vp1 = rows_at(b0, V, k0, -1), rows_at(b0, V, k0, -2), rows_at(b0, V, k0, 1)
        nm2, nm1 = rows_at(b0, M, k0, -2), rows_at(b0, M, k0, -1)
        np1, np2 = rows_at(b0, M, k0, 1), rows_at(b0, M, k0, 2)
        centre = None
        for base, (s_m2, s_m1, s_0, s_p1), (q_m2, q_m1, q_0, q_p1, q_p2) in (
            (0, (um2, um1, u0, up1), (mm2, mm1, m0, mp1, mp2)),
            (4, (vm2, vm1, v0, vp1), (nm2, nm1, m0, np1, np2)),
        ):
            a0 = coefficients(s_0)
            am1 = coefficients(s_m1)
            o0 = q_0 * q_p1
            om1 = q_m1 * q_0
            here = [o0 * a0[k] for k in range(4)]
            back = [om1 * am1[k] for k in range(4)]
            ahead0 = (q_p1 * q_p2) * coefficients(s_p1)[0]
            behind3 = (q_m2 * q_m1) * coefficients(s_m2)[3]
            w[base + 0, kk] = back[0]
            w[base + 1, kk] = back[1] - here[0]
            w[base + 2, kk] = back[3] - here[2]
            w[base + 3, kk] = -here[3]
            w[8 + base + 0, kk] = -behind3
            w[8 + base + 1, kk] = behind3 - back[2]
            w[8 + base + 2, kk] = here[1] - ahead0
            w[8 + base + 3, kk] = ahead0
            mid = back[2] - here[1]
            centre = mid if centre is None else centre + mid
        m_dn = b0[M, pl.ds(k0, KC), inner, :]
        m_up = b0[M, pl.ds(2 + k0, KC), inner, :]
        z_lo = vertical_mix * (m_dn * m0)
        z_hi = vertical_mix * (m0 * m_up)
        w[16, kk] = z_lo
        w[17, kk] = z_hi
        w[18, kk] = 1.0 + centre - (z_lo + z_hi)
        return carry

    lax.fori_loop(0, levels // KC, weights_body, 0, unroll=True)

    def step(src, xh, f, k0, forward):
        kk = pl.ds(k0, KC)
        c = rows_at(src, f, k0, 0)
        cm2, cm1, cp1, cp2 = shift_x(c, xh[f, kk], xh[f, kk], lane, cols)
        ym2, ym1 = rows_at(src, f, k0, -2), rows_at(src, f, k0, -1)
        yp1, yp2 = rows_at(src, f, k0, 1), rows_at(src, f, k0, 2)
        zm = src[f, pl.ds(k0, KC), inner, :]
        zp = src[f, pl.ds(2 + k0, KC), inner, :]
        o = 0 if forward else 8
        sx = (w[o + 0, kk] * cm2 + w[o + 1, kk] * cm1) + (w[o + 2, kk] * cp1 + w[o + 3, kk] * cp2)
        sy = (w[o + 4, kk] * ym2 + w[o + 5, kk] * ym1) + (w[o + 6, kk] * yp1 + w[o + 7, kk] * yp2)
        sz = w[16, kk] * zm + w[17, kk] * zp
        return (w[18, kk] * c + sz) + (sx + sy)

    def step1_loop(g):
        def body(i, carry):
            k0 = pl.multiple_of(i * KC, KC)
            for f in (2 * g, 2 * g + 1):
                b1[f, pl.ds(1 + k0, KC), inner, :] = step(b0, x0, f, k0, g == 0)
            return carry

        lax.fori_loop(0, levels // KC, body, 0, unroll=True)

    def step2_loop(g):
        def body(i, carry):
            k0 = pl.multiple_of(i * KC, KC)
            for f in (2 * g, 2 * g + 1):
                o_all[f, pl.ds(k0, KC)] = step(b1, x1, f, k0, g == 0)
            return carry

        lax.fori_loop(0, levels // KC, body, 0, unroll=True)

    receive(1)
    step1_loop(0)
    send(3)
    receive(2)
    step1_loop(1)
    send(4)
    for r in range(3):
        finish_sends(r)
    receive(3)
    step2_loop(0)
    receive(4)
    step2_loop(1)
    finish_sends(3)
    finish_sends(4)


def split_kernel(stacked, o_t, o_s, o_ct, o_cs, sem):
    copies = []
    for f, dst in enumerate((o_t, o_s, o_ct, o_cs)):
        cp = pltpu.make_async_copy(stacked.at[f], dst, sem.at[f])
        cp.start()
        copies.append(cp)
    for cp in copies:
        cp.wait()


def local(n_ew, n_ns, temp, salt, u_east, v_north, wet, cot_temp, cot_salt):
    levels, rows, cols = temp.shape
    f32 = jnp.float32
    any_spec = pl.BlockSpec(memory_space=pl.ANY)
    vmem_spec = pl.BlockSpec(memory_space=pltpu.VMEM)
    out = jax.ShapeDtypeStruct((levels, rows, cols), f32)
    call = pl.pallas_call(
        functools.partial(kernel, n_ew, n_ns, levels, rows, cols),
        out_shape=jax.ShapeDtypeStruct((N_TRACERS, levels, rows, cols), f32),
        in_specs=[any_spec] * 6 + [vmem_spec],
        out_specs=vmem_spec,
        scratch_shapes=[
            pltpu.VMEM((N_FIELDS, levels + 2, rows + 2 * PAD, cols), f32),
            pltpu.VMEM((X_FIELDS, levels, rows, cols), f32),
            pltpu.VMEM((X_FIELDS, cols, levels * rows), f32),
            pltpu.VMEM((X_FIELDS, cols, levels * rows), f32),
            pltpu.VMEM((N_TRACERS, levels + 2, rows + 2 * PAD, cols), f32),
            pltpu.VMEM((N_TRACERS, levels, rows, cols), f32),
            pltpu.VMEM((N_TRACERS, cols, levels * rows), f32),
            pltpu.VMEM((N_TRACERS, cols, levels * rows), f32),
            pltpu.VMEM((19, levels, rows, cols), f32),
            pltpu.SemaphoreType.DMA((6,)),
            pltpu.SemaphoreType.DMA((5, 4)),
            pltpu.SemaphoreType.DMA((5, 4)),
        ],
        compiler_params=pltpu.CompilerParams(
            collective_id=0, has_side_effects=True, vmem_limit_bytes=56 * 1024 * 1024
        ),
    )
    stacked = call(temp, salt, cot_temp, cot_salt, u_east, v_north, wet)
    return pl.pallas_call(
        split_kernel,
        out_shape=(out,) * 4,
        in_specs=[vmem_spec],
        out_specs=(any_spec,) * 4,
        scratch_shapes=[pltpu.SemaphoreType.DMA((4,))],
    )(stacked)


def solution(mesh):
    spec = P(None, "ns", "ew")
    n_ew = mesh.shape["ew"]
    n_ns = mesh.shape["ns"]
    return jax.shard_map(
        functools.partial(local, n_ew, n_ns), mesh=mesh,
        in_specs=(spec,) * 7, out_specs=(spec,) * 4, check_vma=False,
    )
```

```python
import functools

import jax
import jax.numpy as jnp
from jax import lax
from jax.experimental import pallas as pl
from jax.experimental.pallas import tpu as pltpu
from jax.sharding import PartitionSpec as P

horizontal_mix = 0.05
vertical_mix = 0.2

PAD = 8
KC = 8
N_FIELDS = 7
X_FIELDS = 6
N_TRACERS = 4
U, M, V = 4, 5, 6
MESH = pl.DeviceIdType.MESH


def coefficients(speed):
    magnitude = jnp.abs(speed)
    return (
        (-speed - magnitude) / 12.0,
        (7.0 * speed + 3.0 * magnitude) / 12.0 + horizontal_mix,
        (7.0 * speed - 3.0 * magnitude) / 12.0 - horizontal_mix,
        (-speed + magnitude) / 12.0,
    )


def shift_x(c, left, right, lane, cols):
    cm1 = pltpu.roll(jnp.where(lane >= cols - 1, left, c), 1, 2)
    cm2 = pltpu.roll(jnp.where(lane >= cols - 2, left, c), 2, 2)
    cp1 = pltpu.roll(jnp.where(lane < 1, right, c), cols - 1, 2)
    cp2 = pltpu.roll(jnp.where(lane < 2, right, c), cols - 2, 2)
    return cm2, cm1, cp1, cp2


def kernel(n_ew, n_ns, levels, rows, cols,
           t_hbm, s_hbm, ct_hbm, cs_hbm, u_hbm, v_hbm, wet_ref,
           o_all,
           b0, x0, ts0, rt0, b1, x1, ts1, rt1, w, res, load_sem, send_sem, recv_sem, out_sem):
    ew = lax.axis_index("ew")
    ns = lax.axis_index("ns")
    east = (lax.rem(ew + 1, n_ew), ns)
    west = (lax.rem(ew + n_ew - 1, n_ew), ns)
    north = (ew, jnp.minimum(ns + 1, n_ns - 1))
    south = (ew, jnp.maximum(ns - 1, 0))
    has_north = ns < n_ns - 1
    has_south = ns > 0
    inner = pl.ds(PAD, rows)
    lev = pl.ds(1, levels)

    barrier = pltpu.get_barrier_semaphore()
    pl.semaphore_signal(barrier, 1, device_id=east, device_id_type=MESH)
    pl.semaphore_signal(barrier, 1, device_id=west, device_id_type=MESH)

    @pl.when(has_north)
    def _():
        pl.semaphore_signal(barrier, 1, device_id=north, device_id_type=MESH)

    @pl.when(has_south)
    def _():
        pl.semaphore_signal(barrier, 1, device_id=south, device_id_type=MESH)

    loads = []
    fields = ((0, t_hbm), (1, s_hbm), (2, ct_hbm), (3, cs_hbm), (U, u_hbm), (V, v_hbm))
    for j, (f, src) in enumerate(fields):
        cp = pltpu.make_async_copy(src, b0.at[f, lev, inner, :], load_sem.at[j])
        cp.start()
        loads.append(cp)

    for buf, nf in ((b0, N_FIELDS), (b1, N_TRACERS)):
        zl = jnp.zeros((nf, 1, rows + 2 * PAD, cols), jnp.float32)
        buf[:, pl.ds(0, 1), :, :] = zl
        buf[:, pl.ds(levels + 1, 1), :, :] = zl
        zr = jnp.zeros((nf, levels, 2, cols), jnp.float32)

        @pl.when(jnp.logical_not(has_south))
        def _():
            buf[:, lev, pl.ds(PAD - 2, 2), :] = zr

        @pl.when(jnp.logical_not(has_north))
        def _():
            buf[:, lev, pl.ds(PAD + rows, 2), :] = zr

    b0[M, lev, inner, :] = wet_ref[...].astype(jnp.float32)
    for cp in loads:
        cp.wait()

    peers = 2 + has_north.astype(jnp.int32) + has_south.astype(jnp.int32)
    pl.semaphore_wait(barrier, peers)

    def group(r):
        if r == 0:
            return b0, ts0, rt0, x0, pl.ds(M, 2), pl.ds(U, 2)
        g = pl.ds(2 * ((r - 1) % 2), 2)
        if r <= 2:
            return b0, ts0, rt0, x0, g, g
        return b1, ts1, rt1, x1, g, g

    def edge_copy(r, d, dev):
        buf, ts, rt, _, fy, fx = group(r)
        if d == 0:
            src = buf.at[fy, lev, pl.ds(PAD + rows - 2, 2), :]
            dst = buf.at[fy, lev, pl.ds(PAD - 2, 2), :]
        elif d == 1:
            src = buf.at[fy, lev, pl.ds(PAD, 2), :]
            dst = buf.at[fy, lev, pl.ds(PAD + rows, 2), :]
        elif d == 2:
            src = ts.at[fx, pl.ds(cols - 2, 2), :]
            dst = rt.at[fx, pl.ds(cols - 2, 2), :]
        else:
            src = ts.at[fx, pl.ds(0, 2), :]
            dst = rt.at[fx, pl.ds(0, 2), :]
        return pltpu.make_async_remote_copy(
            src_ref=src, dst_ref=dst, send_sem=send_sem.at[r, d], recv_sem=recv_sem.at[r, d],
            device_id=dev, device_id_type=MESH,
        )

    def x_fields(r):
        if r == 0:
            return (U, M)
        g = (r - 1) % 2
        return range(2 * g, 2 * g + 2)

    outgoing = ((0, north, has_north), (1, south, has_south), (2, east, None), (3, west, None))
    incoming = ((0, south, has_south), (1, north, has_north), (2, west, None), (3, east, None))

    def each(r, pairs, action):
        for d, dev, cond in pairs:
            if cond is None:
                action(edge_copy(r, d, dev))
            else:
                pl.when(cond)(lambda d=d, dev=dev: action(edge_copy(r, d, dev)))

    def send_rows(r):
        each(r, outgoing[:2], lambda c: c.start())

    def send_columns(r):
        buf, ts = group(r)[:2]
        for f in x_fields(r):
            ts[f] = buf[f, lev, inner, :].reshape(levels * rows, cols).T
        each(r, outgoing[2:], lambda c: c.start())

    def send(r):
        send_rows(r)
        send_columns(r)

    def receive(r):
        rt, x = group(r)[2:4]
        each(r, incoming, lambda c: c.wait_recv())
        for f in x_fields(r):
            x[f] = rt[f].T.reshape(levels, rows, cols)

    def finish_sends(r):
        each(r, outgoing, lambda c: c.wait_send())

    for r in range(3):
        send_rows(r)
    for r in range(3):
        send_columns(r)
    receive(0)

    lane = lax.broadcasted_iota(jnp.int32, (KC, rows, cols), 2)

    def rows_at(buf, f, k0, d):
        return buf[f, pl.ds(1 + k0, KC), pl.ds(PAD + d, rows), :]

    def weights_body(i, carry):
        k0 = pl.multiple_of(i * KC, KC)
        kk = pl.ds(k0, KC)
        u0 = rows_at(b0, U, k0, 0)
        um2, um1, up1, _ = shift_x(u0, x0[U, kk], x0[U, kk], lane, cols)
        m0 = rows_at(b0, M, k0, 0)
        mm2, mm1, mp1, mp2 = shift_x(m0, x0[M, kk], x0[M, kk], lane, cols)
        v0 = rows_at(b0, V, k0, 0)
        vm1, vm2, vp1 = rows_at(b0, V, k0, -1), rows_at(b0, V, k0, -2), rows_at(b0, V, k0, 1)
        nm2, nm1 = rows_at(b0, M, k0, -2), rows_at(b0, M, k0, -1)
        np1, np2 = rows_at(b0, M, k0, 1), rows_at(b0, M, k0, 2)
        centre = None
        for base, (s_m2, s_m1, s_0, s_p1), (q_m2, q_m1, q_0, q_p1, q_p2) in (
            (0, (um2, um1, u0, up1), (mm2, mm1, m0, mp1, mp2)),
            (4, (vm2, vm1, v0, vp1), (nm2, nm1, m0, np1, np2)),
        ):
            a0 = coefficients(s_0)
            am1 = coefficients(s_m1)
            o0 = q_0 * q_p1
            om1 = q_m1 * q_0
            here = [o0 * a0[k] for k in range(4)]
            back = [om1 * am1[k] for k in range(4)]
            ahead0 = (q_p1 * q_p2) * coefficients(s_p1)[0]
            behind3 = (q_m2 * q_m1) * coefficients(s_m2)[3]
            w[base + 0, kk] = back[0]
            w[base + 1, kk] = back[1] - here[0]
            w[base + 2, kk] = back[3] - here[2]
            w[base + 3, kk] = -here[3]
            w[8 + base + 0, kk] = -behind3
            w[8 + base + 1, kk] = behind3 - back[2]
            w[8 + base + 2, kk] = here[1] - ahead0
            w[8 + base + 3, kk] = ahead0
            mid = back[2] - here[1]
            centre = mid if centre is None else centre + mid
        m_dn = b0[M, pl.ds(k0, KC), inner, :]
        m_up = b0[M, pl.ds(2 + k0, KC), inner, :]
        z_lo = vertical_mix * (m_dn * m0)
        z_hi = vertical_mix * (m0 * m_up)
        w[16, kk] = z_lo
        w[17, kk] = z_hi
        w[18, kk] = 1.0 + centre - (z_lo + z_hi)
        return carry

    lax.fori_loop(0, levels // KC, weights_body, 0, unroll=True)

    def step(src, xh, f, k0, forward):
        kk = pl.ds(k0, KC)
        c = rows_at(src, f, k0, 0)
        cm2, cm1, cp1, cp2 = shift_x(c, xh[f, kk], xh[f, kk], lane, cols)
        ym2, ym1 = rows_at(src, f, k0, -2), rows_at(src, f, k0, -1)
        yp1, yp2 = rows_at(src, f, k0, 1), rows_at(src, f, k0, 2)
        zm = src[f, pl.ds(k0, KC), inner, :]
        zp = src[f, pl.ds(2 + k0, KC), inner, :]
        o = 0 if forward else 8
        sx = (w[o + 0, kk] * cm2 + w[o + 1, kk] * cm1) + (w[o + 2, kk] * cp1 + w[o + 3, kk] * cp2)
        sy = (w[o + 4, kk] * ym2 + w[o + 5, kk] * ym1) + (w[o + 6, kk] * yp1 + w[o + 7, kk] * yp2)
        sz = w[16, kk] * zm + w[17, kk] * zp
        return (w[18, kk] * c + sz) + (sx + sy)

    def step1_loop(g):
        def body(i, carry):
            k0 = pl.multiple_of(i * KC, KC)
            for f in (2 * g, 2 * g + 1):
                b1[f, pl.ds(1 + k0, KC), inner, :] = step(b0, x0, f, k0, g == 0)
            return carry

        lax.fori_loop(0, levels // KC, body, 0, unroll=True)

    def step2_loop(g):
        def body(i, carry):
            k0 = pl.multiple_of(i * KC, KC)
            for f in (2 * g, 2 * g + 1):
                res[f, pl.ds(k0, KC)] = step(b1, x1, f, k0, g == 0)
            return carry

        lax.fori_loop(0, levels // KC, body, 0, unroll=True)

    receive(1)
    step1_loop(0)
    send(3)
    receive(2)
    step1_loop(1)
    send(4)
    for r in range(3):
        finish_sends(r)
    def store(g):
        copies = []
        for f in (2 * g, 2 * g + 1):
            cp = pltpu.make_async_copy(res.at[f], o_all.at[f], out_sem.at[f])
            cp.start()
            copies.append(cp)
        return copies

    receive(3)
    step2_loop(0)
    stored = store(0)
    receive(4)
    step2_loop(1)
    stored += store(1)
    finish_sends(3)
    finish_sends(4)
    for cp in stored:
        cp.wait()


def split_kernel(stacked, o_t, o_s, o_ct, o_cs, held, in_sem, out_sem):
    ins = []
    for f in range(N_TRACERS):
        cp = pltpu.make_async_copy(stacked.at[f], held.at[f], in_sem.at[f])
        cp.start()
        ins.append(cp)
    outs = []
    for f, dst in enumerate((o_t, o_s, o_ct, o_cs)):
        ins[f].wait()
        cp = pltpu.make_async_copy(held.at[f], dst, out_sem.at[f])
        cp.start()
        outs.append(cp)
    for cp in outs:
        cp.wait()


def local(n_ew, n_ns, temp, salt, u_east, v_north, wet, cot_temp, cot_salt):
    levels, rows, cols = temp.shape
    f32 = jnp.float32
    any_spec = pl.BlockSpec(memory_space=pl.ANY)
    vmem_spec = pl.BlockSpec(memory_space=pltpu.VMEM)
    out = jax.ShapeDtypeStruct((levels, rows, cols), f32)
    call = pl.pallas_call(
        functools.partial(kernel, n_ew, n_ns, levels, rows, cols),
        out_shape=jax.ShapeDtypeStruct((N_TRACERS, levels, rows, cols), f32),
        in_specs=[any_spec] * 6 + [vmem_spec],
        out_specs=any_spec,
        scratch_shapes=[
            pltpu.VMEM((N_FIELDS, levels + 2, rows + 2 * PAD, cols), f32),
            pltpu.VMEM((X_FIELDS, levels, rows, cols), f32),
            pltpu.VMEM((X_FIELDS, cols, levels * rows), f32),
            pltpu.VMEM((X_FIELDS, cols, levels * rows), f32),
            pltpu.VMEM((N_TRACERS, levels + 2, rows + 2 * PAD, cols), f32),
            pltpu.VMEM((N_TRACERS, levels, rows, cols), f32),
            pltpu.VMEM((N_TRACERS, cols, levels * rows), f32),
            pltpu.VMEM((N_TRACERS, cols, levels * rows), f32),
            pltpu.VMEM((19, levels, rows, cols), f32),
            pltpu.VMEM((N_TRACERS, levels, rows, cols), f32),
            pltpu.SemaphoreType.DMA((6,)),
            pltpu.SemaphoreType.DMA((5, 4)),
            pltpu.SemaphoreType.DMA((5, 4)),
            pltpu.SemaphoreType.DMA((N_TRACERS,)),
        ],
        compiler_params=pltpu.CompilerParams(
            collective_id=0, has_side_effects=True, vmem_limit_bytes=56 * 1024 * 1024
        ),
    )
    stacked = call(temp, salt, cot_temp, cot_salt, u_east, v_north, wet)
    return pl.pallas_call(
        split_kernel,
        out_shape=(out,) * 4,
        in_specs=[any_spec],
        out_specs=(any_spec,) * 4,
        scratch_shapes=[
            pltpu.VMEM((N_TRACERS, levels, rows, cols), f32),
            pltpu.SemaphoreType.DMA((N_TRACERS,)),
            pltpu.SemaphoreType.DMA((N_TRACERS,)),
        ],
    )(stacked)


def solution(mesh):
    spec = P(None, "ns", "ew")
    n_ew = mesh.shape["ew"]
    n_ns = mesh.shape["ns"]
    return jax.shard_map(
        functools.partial(local, n_ew, n_ns), mesh=mesh,
        in_specs=(spec,) * 7, out_specs=(spec,) * 4, check_vma=False,
    )
```

```python
import functools

import jax
import jax.numpy as jnp
from jax import lax
from jax.experimental import pallas as pl
from jax.experimental.pallas import tpu as pltpu
from jax.sharding import PartitionSpec as P

horizontal_mix = 0.05
vertical_mix = 0.2

PAD = 8
KC = 8
N_FIELDS = 7
X_FIELDS = 6
N_TRACERS = 4
U, M, V = 4, 5, 6
MESH = pl.DeviceIdType.MESH


def coefficients(speed):
    magnitude = jnp.abs(speed)
    return (
        (-speed - magnitude) / 12.0,
        (7.0 * speed + 3.0 * magnitude) / 12.0 + horizontal_mix,
        (7.0 * speed - 3.0 * magnitude) / 12.0 - horizontal_mix,
        (-speed + magnitude) / 12.0,
    )


def shift_x(c, left, right, lane, cols):
    cm1 = pltpu.roll(jnp.where(lane >= cols - 1, left, c), 1, 2)
    cm2 = pltpu.roll(jnp.where(lane >= cols - 2, left, c), 2, 2)
    cp1 = pltpu.roll(jnp.where(lane < 1, right, c), cols - 1, 2)
    cp2 = pltpu.roll(jnp.where(lane < 2, right, c), cols - 2, 2)
    return cm2, cm1, cp1, cp2


def kernel(n_ew, n_ns, levels, rows, cols,
           t_hbm, s_hbm, ct_hbm, cs_hbm, u_hbm, v_hbm, wet_ref,
           o_all,
           b0, x0, ts0, rt0, b1, x1, ts1, rt1, w, res, wet_vmem, load_sem, send_sem, recv_sem, out_sem):
    ew = lax.axis_index("ew")
    ns = lax.axis_index("ns")
    east = (lax.rem(ew + 1, n_ew), ns)
    west = (lax.rem(ew + n_ew - 1, n_ew), ns)
    north = (ew, jnp.minimum(ns + 1, n_ns - 1))
    south = (ew, jnp.maximum(ns - 1, 0))
    has_north = ns < n_ns - 1
    has_south = ns > 0
    inner = pl.ds(PAD, rows)
    lev = pl.ds(1, levels)

    barrier = pltpu.get_barrier_semaphore()
    pl.semaphore_signal(barrier, 1, device_id=east, device_id_type=MESH)
    pl.semaphore_signal(barrier, 1, device_id=west, device_id_type=MESH)

    @pl.when(has_north)
    def _():
        pl.semaphore_signal(barrier, 1, device_id=north, device_id_type=MESH)

    @pl.when(has_south)
    def _():
        pl.semaphore_signal(barrier, 1, device_id=south, device_id_type=MESH)

    loads = []
    fields = ((0, t_hbm), (1, s_hbm), (2, ct_hbm), (3, cs_hbm), (U, u_hbm), (V, v_hbm))
    for j, (f, src) in enumerate(fields):
        cp = pltpu.make_async_copy(src, b0.at[f, lev, inner, :], load_sem.at[j])
        cp.start()
        loads.append(cp)
    wet_load = pltpu.make_async_copy(wet_ref, wet_vmem, load_sem.at[len(fields)])
    wet_load.start()

    for buf, nf in ((b0, N_FIELDS), (b1, N_TRACERS)):
        zl = jnp.zeros((nf, 1, rows + 2 * PAD, cols), jnp.float32)
        buf[:, pl.ds(0, 1), :, :] = zl
        buf[:, pl.ds(levels + 1, 1), :, :] = zl
        zr = jnp.zeros((nf, levels, 2, cols), jnp.float32)

        @pl.when(jnp.logical_not(has_south))
        def _():
            buf[:, lev, pl.ds(PAD - 2, 2), :] = zr

        @pl.when(jnp.logical_not(has_north))
        def _():
            buf[:, lev, pl.ds(PAD + rows, 2), :] = zr

    wet_load.wait()
    b0[M, lev, inner, :] = wet_vmem[...].astype(jnp.float32)
    for cp in loads:
        cp.wait()

    peers = 2 + has_north.astype(jnp.int32) + has_south.astype(jnp.int32)
    pl.semaphore_wait(barrier, peers)

    def group(r):
        if r == 0:
            return b0, ts0, rt0, x0, pl.ds(M, 2), pl.ds(U, 2)
        g = pl.ds(2 * ((r - 1) % 2), 2)
        if r <= 2:
            return b0, ts0, rt0, x0, g, g
        return b1, ts1, rt1, x1, g, g

    def edge_copy(r, d, dev):
        buf, ts, rt, _, fy, fx = group(r)
        if d == 0:
            src = buf.at[fy, lev, pl.ds(PAD + rows - 2, 2), :]
            dst = buf.at[fy, lev, pl.ds(PAD - 2, 2), :]
        elif d == 1:
            src = buf.at[fy, lev, pl.ds(PAD, 2), :]
            dst = buf.at[fy, lev, pl.ds(PAD + rows, 2), :]
        elif d == 2:
            src = ts.at[fx, pl.ds(cols - 2, 2), :]
            dst = rt.at[fx, pl.ds(cols - 2, 2), :]
        else:
            src = ts.at[fx, pl.ds(0, 2), :]
            dst = rt.at[fx, pl.ds(0, 2), :]
        return pltpu.make_async_remote_copy(
            src_ref=src, dst_ref=dst, send_sem=send_sem.at[r, d], recv_sem=recv_sem.at[r, d],
            device_id=dev, device_id_type=MESH,
        )

    def x_fields(r):
        if r == 0:
            return (U, M)
        g = (r - 1) % 2
        return range(2 * g, 2 * g + 2)

    outgoing = ((0, north, has_north), (1, south, has_south), (2, east, None), (3, west, None))
    incoming = ((0, south, has_south), (1, north, has_north), (2, west, None), (3, east, None))

    def each(r, pairs, action):
        for d, dev, cond in pairs:
            if cond is None:
                action(edge_copy(r, d, dev))
            else:
                pl.when(cond)(lambda d=d, dev=dev: action(edge_copy(r, d, dev)))

    def send_rows(r):
        each(r, outgoing[:2], lambda c: c.start())

    def send_columns(r):
        buf, ts = group(r)[:2]
        for f in x_fields(r):
            ts[f] = buf[f, lev, inner, :].reshape(levels * rows, cols).T
        each(r, outgoing[2:], lambda c: c.start())

    def send(r):
        send_rows(r)
        send_columns(r)

    def receive(r):
        rt, x = group(r)[2:4]
        each(r, incoming, lambda c: c.wait_recv())
        for f in x_fields(r):
            x[f] = rt[f].T.reshape(levels, rows, cols)

    def finish_sends(r):
        each(r, outgoing, lambda c: c.wait_send())

    for r in range(3):
        send_rows(r)
    for r in range(3):
        send_columns(r)
    receive(0)

    lane = lax.broadcasted_iota(jnp.int32, (KC, rows, cols), 2)

    def rows_at(buf, f, k0, d):
        return buf[f, pl.ds(1 + k0, KC), pl.ds(PAD + d, rows), :]

    def weights_body(i, carry):
        k0 = pl.multiple_of(i * KC, KC)
        kk = pl.ds(k0, KC)
        u0 = rows_at(b0, U, k0, 0)
        um2, um1, up1, _ = shift_x(u0, x0[U, kk], x0[U, kk], lane, cols)
        m0 = rows_at(b0, M, k0, 0)
        mm2, mm1, mp1, mp2 = shift_x(m0, x0[M, kk], x0[M, kk], lane, cols)
        v0 = rows_at(b0, V, k0, 0)
        vm1, vm2, vp1 = rows_at(b0, V, k0, -1), rows_at(b0, V, k0, -2), rows_at(b0, V, k0, 1)
        nm2, nm1 = rows_at(b0, M, k0, -2), rows_at(b0, M, k0, -1)
        np1, np2 = rows_at(b0, M, k0, 1), rows_at(b0, M, k0, 2)
        centre = None
        for base, (s_m2, s_m1, s_0, s_p1), (q_m2, q_m1, q_0, q_p1, q_p2) in (
            (0, (um2, um1, u0, up1), (mm2, mm1, m0, mp1, mp2)),
            (4, (vm2, vm1, v0, vp1), (nm2, nm1, m0, np1, np2)),
        ):
            a0 = coefficients(s_0)
            am1 = coefficients(s_m1)
            o0 = q_0 * q_p1
            om1 = q_m1 * q_0
            here = [o0 * a0[k] for k in range(4)]
            back = [om1 * am1[k] for k in range(4)]
            ahead0 = (q_p1 * q_p2) * coefficients(s_p1)[0]
            behind3 = (q_m2 * q_m1) * coefficients(s_m2)[3]
            w[base + 0, kk] = back[0]
            w[base + 1, kk] = back[1] - here[0]
            w[base + 2, kk] = back[3] - here[2]
            w[base + 3, kk] = -here[3]
            w[8 + base + 0, kk] = -behind3
            w[8 + base + 1, kk] = behind3 - back[2]
            w[8 + base + 2, kk] = here[1] - ahead0
            w[8 + base + 3, kk] = ahead0
            mid = back[2] - here[1]
            centre = mid if centre is None else centre + mid
        m_dn = b0[M, pl.ds(k0, KC), inner, :]
        m_up = b0[M, pl.ds(2 + k0, KC), inner, :]
        z_lo = vertical_mix * (m_dn * m0)
        z_hi = vertical_mix * (m0 * m_up)
        w[16, kk] = z_lo
        w[17, kk] = z_hi
        w[18, kk] = 1.0 + centre - (z_lo + z_hi)
        return carry

    lax.fori_loop(0, levels // KC, weights_body, 0, unroll=True)

    def step(src, xh, f, k0, forward):
        kk = pl.ds(k0, KC)
        c = rows_at(src, f, k0, 0)
        cm2, cm1, cp1, cp2 = shift_x(c, xh[f, kk], xh[f, kk], lane, cols)
        ym2, ym1 = rows_at(src, f, k0, -2), rows_at(src, f, k0, -1)
        yp1, yp2 = rows_at(src, f, k0, 1), rows_at(src, f, k0, 2)
        zm = src[f, pl.ds(k0, KC), inner, :]
        zp = src[f, pl.ds(2 + k0, KC), inner, :]
        o = 0 if forward else 8
        sx = (w[o + 0, kk] * cm2 + w[o + 1, kk] * cm1) + (w[o + 2, kk] * cp1 + w[o + 3, kk] * cp2)
        sy = (w[o + 4, kk] * ym2 + w[o + 5, kk] * ym1) + (w[o + 6, kk] * yp1 + w[o + 7, kk] * yp2)
        sz = w[16, kk] * zm + w[17, kk] * zp
        return (w[18, kk] * c + sz) + (sx + sy)

    def step1_loop(g):
        def body(i, carry):
            k0 = pl.multiple_of(i * KC, KC)
            for f in (2 * g, 2 * g + 1):
                b1[f, pl.ds(1 + k0, KC), inner, :] = step(b0, x0, f, k0, g == 0)
            return carry

        lax.fori_loop(0, levels // KC, body, 0, unroll=True)

    def step2_loop(g):
        def body(i, carry):
            k0 = pl.multiple_of(i * KC, KC)
            for f in (2 * g, 2 * g + 1):
                res[f, pl.ds(k0, KC)] = step(b1, x1, f, k0, g == 0)
            return carry

        lax.fori_loop(0, levels // KC, body, 0, unroll=True)

    receive(1)
    step1_loop(0)
    send(3)
    receive(2)
    step1_loop(1)
    send(4)
    for r in range(3):
        finish_sends(r)
    def store(g):
        copies = []
        for f in (2 * g, 2 * g + 1):
            cp = pltpu.make_async_copy(res.at[f], o_all.at[f], out_sem.at[f])
            cp.start()
            copies.append(cp)
        return copies

    receive(3)
    step2_loop(0)
    stored = store(0)
    receive(4)
    step2_loop(1)
    stored += store(1)
    finish_sends(3)
    finish_sends(4)
    for cp in stored:
        cp.wait()


def split_kernel(stacked, o_t, o_s, o_ct, o_cs, held, in_sem, out_sem):
    ins = []
    for f in range(N_TRACERS):
        cp = pltpu.make_async_copy(stacked.at[f], held.at[f], in_sem.at[f])
        cp.start()
        ins.append(cp)
    outs = []
    for f, dst in enumerate((o_t, o_s, o_ct, o_cs)):
        ins[f].wait()
        cp = pltpu.make_async_copy(held.at[f], dst, out_sem.at[f])
        cp.start()
        outs.append(cp)
    for cp in outs:
        cp.wait()


def local(n_ew, n_ns, temp, salt, u_east, v_north, wet, cot_temp, cot_salt):
    levels, rows, cols = temp.shape
    f32 = jnp.float32
    any_spec = pl.BlockSpec(memory_space=pl.ANY)
    vmem_spec = pl.BlockSpec(memory_space=pltpu.VMEM)
    out = jax.ShapeDtypeStruct((levels, rows, cols), f32)
    call = pl.pallas_call(
        functools.partial(kernel, n_ew, n_ns, levels, rows, cols),
        out_shape=jax.ShapeDtypeStruct((N_TRACERS, levels, rows, cols), f32),
        in_specs=[any_spec] * 7,
        out_specs=any_spec,
        scratch_shapes=[
            pltpu.VMEM((N_FIELDS, levels + 2, rows + 2 * PAD, cols), f32),
            pltpu.VMEM((X_FIELDS, levels, rows, cols), f32),
            pltpu.VMEM((X_FIELDS, cols, levels * rows), f32),
            pltpu.VMEM((X_FIELDS, cols, levels * rows), f32),
            pltpu.VMEM((N_TRACERS, levels + 2, rows + 2 * PAD, cols), f32),
            pltpu.VMEM((N_TRACERS, levels, rows, cols), f32),
            pltpu.VMEM((N_TRACERS, cols, levels * rows), f32),
            pltpu.VMEM((N_TRACERS, cols, levels * rows), f32),
            pltpu.VMEM((19, levels, rows, cols), f32),
            pltpu.VMEM((N_TRACERS, levels, rows, cols), f32),
            pltpu.VMEM((levels, rows, cols), jnp.int32),
            pltpu.SemaphoreType.DMA((7,)),
            pltpu.SemaphoreType.DMA((5, 4)),
            pltpu.SemaphoreType.DMA((5, 4)),
            pltpu.SemaphoreType.DMA((N_TRACERS,)),
        ],
        compiler_params=pltpu.CompilerParams(
            collective_id=0, has_side_effects=True, vmem_limit_bytes=56 * 1024 * 1024
        ),
    )
    stacked = call(temp, salt, cot_temp, cot_salt, u_east, v_north, wet)
    return pl.pallas_call(
        split_kernel,
        out_shape=(out,) * 4,
        in_specs=[any_spec],
        out_specs=(any_spec,) * 4,
        scratch_shapes=[
            pltpu.VMEM((N_TRACERS, levels, rows, cols), f32),
            pltpu.SemaphoreType.DMA((N_TRACERS,)),
            pltpu.SemaphoreType.DMA((N_TRACERS,)),
        ],
    )(stacked)


def solution(mesh):
    spec = P(None, "ns", "ew")
    n_ew = mesh.shape["ew"]
    n_ns = mesh.shape["ns"]
    return jax.shard_map(
        functools.partial(local, n_ew, n_ns), mesh=mesh,
        in_specs=(spec,) * 7, out_specs=(spec,) * 4, check_vma=False,
    )
```

```python
import functools

import jax
import jax.numpy as jnp
from jax import lax
from jax.experimental import pallas as pl
from jax.experimental.pallas import tpu as pltpu
from jax.sharding import PartitionSpec as P

horizontal_mix = 0.05
vertical_mix = 0.2

PAD = 8
KC = 8
N_FIELDS = 7
X_FIELDS = 6
N_TRACERS = 4
U, M, V = 4, 5, 6
MESH = pl.DeviceIdType.MESH


def coefficients(speed):
    magnitude = jnp.abs(speed)
    return (
        (-speed - magnitude) / 12.0,
        (7.0 * speed + 3.0 * magnitude) / 12.0 + horizontal_mix,
        (7.0 * speed - 3.0 * magnitude) / 12.0 - horizontal_mix,
        (-speed + magnitude) / 12.0,
    )


def shift_x(c, left, right, lane, cols):
    cm1 = pltpu.roll(jnp.where(lane >= cols - 1, left, c), 1, 2)
    cm2 = pltpu.roll(jnp.where(lane >= cols - 2, left, c), 2, 2)
    cp1 = pltpu.roll(jnp.where(lane < 1, right, c), cols - 1, 2)
    cp2 = pltpu.roll(jnp.where(lane < 2, right, c), cols - 2, 2)
    return cm2, cm1, cp1, cp2


def kernel(n_ew, n_ns, levels, rows, cols,
           t_hbm, s_hbm, ct_hbm, cs_hbm, u_hbm, v_hbm, wet_ref,
           o_all,
           b0, x0, ts0, rt0, b1, x1, ts1, rt1, w, res, wet_vmem, load_sem, send_sem, recv_sem, out_sem):
    ew = lax.axis_index("ew")
    ns = lax.axis_index("ns")
    east = (lax.rem(ew + 1, n_ew), ns)
    west = (lax.rem(ew + n_ew - 1, n_ew), ns)
    north = (ew, jnp.minimum(ns + 1, n_ns - 1))
    south = (ew, jnp.maximum(ns - 1, 0))
    has_north = ns < n_ns - 1
    has_south = ns > 0
    inner = pl.ds(PAD, rows)
    lev = pl.ds(1, levels)

    barrier = pltpu.get_barrier_semaphore()
    pl.semaphore_signal(barrier, 1, device_id=east, device_id_type=MESH)
    pl.semaphore_signal(barrier, 1, device_id=west, device_id_type=MESH)

    @pl.when(has_north)
    def _():
        pl.semaphore_signal(barrier, 1, device_id=north, device_id_type=MESH)

    @pl.when(has_south)
    def _():
        pl.semaphore_signal(barrier, 1, device_id=south, device_id_type=MESH)

    loads = []
    fields = ((0, t_hbm), (1, s_hbm), (2, ct_hbm), (3, cs_hbm), (U, u_hbm), (V, v_hbm))
    for j, (f, src) in enumerate(fields):
        cp = pltpu.make_async_copy(src, b0.at[f, lev, inner, :], load_sem.at[j])
        cp.start()
        loads.append(cp)
    wet_load = pltpu.make_async_copy(wet_ref, wet_vmem, load_sem.at[len(fields)])
    wet_load.start()

    for buf, nf in ((b0, N_FIELDS), (b1, N_TRACERS)):
        zl = jnp.zeros((nf, 1, rows + 2 * PAD, cols), jnp.float32)
        buf[:, pl.ds(0, 1), :, :] = zl
        buf[:, pl.ds(levels + 1, 1), :, :] = zl
        zr = jnp.zeros((nf, levels, 2, cols), jnp.float32)

        @pl.when(jnp.logical_not(has_south))
        def _():
            buf[:, lev, pl.ds(PAD - 2, 2), :] = zr

        @pl.when(jnp.logical_not(has_north))
        def _():
            buf[:, lev, pl.ds(PAD + rows, 2), :] = zr

    wet_load.wait()
    b0[M, lev, inner, :] = wet_vmem[...].astype(jnp.float32)
    for cp in loads:
        cp.wait()

    peers = 2 + has_north.astype(jnp.int32) + has_south.astype(jnp.int32)
    pl.semaphore_wait(barrier, peers)

    def group(r):
        if r == 0:
            return b0, ts0, rt0, x0, pl.ds(M, 2), pl.ds(U, 2)
        g = pl.ds(2 * ((r - 1) % 2), 2)
        if r <= 2:
            return b0, ts0, rt0, x0, g, g
        return b1, ts1, rt1, x1, g, g

    def edge_copy(r, d, dev):
        buf, ts, rt, _, fy, fx = group(r)
        if d == 0:
            src = buf.at[fy, lev, pl.ds(PAD + rows - 2, 2), :]
            dst = buf.at[fy, lev, pl.ds(PAD - 2, 2), :]
        elif d == 1:
            src = buf.at[fy, lev, pl.ds(PAD, 2), :]
            dst = buf.at[fy, lev, pl.ds(PAD + rows, 2), :]
        elif d == 2:
            src = ts.at[fx, pl.ds(cols - 2, 2), :]
            dst = rt.at[fx, pl.ds(cols - 2, 2), :]
        else:
            src = ts.at[fx, pl.ds(0, 2), :]
            dst = rt.at[fx, pl.ds(0, 2), :]
        return pltpu.make_async_remote_copy(
            src_ref=src, dst_ref=dst, send_sem=send_sem.at[r, d], recv_sem=recv_sem.at[r, d],
            device_id=dev, device_id_type=MESH,
        )

    def x_fields(r):
        if r == 0:
            return (U, M)
        g = (r - 1) % 2
        return range(2 * g, 2 * g + 2)

    outgoing = ((0, north, has_north), (1, south, has_south), (2, east, None), (3, west, None))
    incoming = ((0, south, has_south), (1, north, has_north), (2, west, None), (3, east, None))

    def each(r, pairs, action):
        for d, dev, cond in pairs:
            if cond is None:
                action(edge_copy(r, d, dev))
            else:
                pl.when(cond)(lambda d=d, dev=dev: action(edge_copy(r, d, dev)))

    def send_rows(r):
        each(r, outgoing[:2], lambda c: c.start())

    def send_columns(r):
        buf, ts = group(r)[:2]
        for f in x_fields(r):
            ts[f] = buf[f, lev, inner, :].reshape(levels * rows, cols).T
        each(r, outgoing[2:], lambda c: c.start())

    def send(r):
        send_rows(r)
        send_columns(r)

    def receive(r):
        rt, x = group(r)[2:4]
        each(r, incoming, lambda c: c.wait_recv())
        for f in x_fields(r):
            x[f] = rt[f].T.reshape(levels, rows, cols)

    def finish_sends(r):
        each(r, outgoing, lambda c: c.wait_send())

    for r in range(3):
        send_rows(r)
    for r in range(3):
        send_columns(r)
    receive(0)

    lane = lax.broadcasted_iota(jnp.int32, (KC, rows, cols), 2)

    def rows_at(buf, f, k0, d):
        return buf[f, pl.ds(1 + k0, KC), pl.ds(PAD + d, rows), :]

    def weights_body(i, carry):
        k0 = pl.multiple_of(i * KC, KC)
        kk = pl.ds(k0, KC)
        u0 = rows_at(b0, U, k0, 0)
        um2, um1, up1, _ = shift_x(u0, x0[U, kk], x0[U, kk], lane, cols)
        m0 = rows_at(b0, M, k0, 0)
        mm2, mm1, mp1, mp2 = shift_x(m0, x0[M, kk], x0[M, kk], lane, cols)
        v0 = rows_at(b0, V, k0, 0)
        vm1, vm2, vp1 = rows_at(b0, V, k0, -1), rows_at(b0, V, k0, -2), rows_at(b0, V, k0, 1)
        nm2, nm1 = rows_at(b0, M, k0, -2), rows_at(b0, M, k0, -1)
        np1, np2 = rows_at(b0, M, k0, 1), rows_at(b0, M, k0, 2)
        centre = None
        for base, (s_m2, s_m1, s_0, s_p1), (q_m2, q_m1, q_0, q_p1, q_p2) in (
            (0, (um2, um1, u0, up1), (mm2, mm1, m0, mp1, mp2)),
            (4, (vm2, vm1, v0, vp1), (nm2, nm1, m0, np1, np2)),
        ):
            a0 = coefficients(s_0)
            am1 = coefficients(s_m1)
            o0 = q_0 * q_p1
            om1 = q_m1 * q_0
            here = [o0 * a0[k] for k in range(4)]
            back = [om1 * am1[k] for k in range(4)]
            ahead0 = (q_p1 * q_p2) * coefficients(s_p1)[0]
            behind3 = (q_m2 * q_m1) * coefficients(s_m2)[3]
            w[base + 0, kk] = back[0]
            w[base + 1, kk] = back[1] - here[0]
            w[base + 2, kk] = back[3] - here[2]
            w[base + 3, kk] = -here[3]
            w[8 + base + 0, kk] = -behind3
            w[8 + base + 1, kk] = behind3 - back[2]
            w[8 + base + 2, kk] = here[1] - ahead0
            w[8 + base + 3, kk] = ahead0
            mid = back[2] - here[1]
            centre = mid if centre is None else centre + mid
        m_dn = b0[M, pl.ds(k0, KC), inner, :]
        m_up = b0[M, pl.ds(2 + k0, KC), inner, :]
        z_lo = vertical_mix * (m_dn * m0)
        z_hi = vertical_mix * (m0 * m_up)
        w[16, kk] = z_lo
        w[17, kk] = z_hi
        w[18, kk] = 1.0 + centre - (z_lo + z_hi)
        return carry

    lax.fori_loop(0, levels // KC, weights_body, 0, unroll=True)

    def step(src, xh, f, k0, forward):
        kk = pl.ds(k0, KC)
        c = rows_at(src, f, k0, 0)
        cm2, cm1, cp1, cp2 = shift_x(c, xh[f, kk], xh[f, kk], lane, cols)
        ym2, ym1 = rows_at(src, f, k0, -2), rows_at(src, f, k0, -1)
        yp1, yp2 = rows_at(src, f, k0, 1), rows_at(src, f, k0, 2)
        zm = src[f, pl.ds(k0, KC), inner, :]
        zp = src[f, pl.ds(2 + k0, KC), inner, :]
        o = 0 if forward else 8
        sx = (w[o + 0, kk] * cm2 + w[o + 1, kk] * cm1) + (w[o + 2, kk] * cp1 + w[o + 3, kk] * cp2)
        sy = (w[o + 4, kk] * ym2 + w[o + 5, kk] * ym1) + (w[o + 6, kk] * yp1 + w[o + 7, kk] * yp2)
        sz = w[16, kk] * zm + w[17, kk] * zp
        return (w[18, kk] * c + sz) + (sx + sy)

    def step1_loop(g):
        def body(i, carry):
            k0 = pl.multiple_of(i * KC, KC)
            for f in (2 * g, 2 * g + 1):
                b1[f, pl.ds(1 + k0, KC), inner, :] = step(b0, x0, f, k0, g == 0)
            return carry

        lax.fori_loop(0, levels // KC, body, 0, unroll=True)

    def out_copy(f, i):
        chunk = pl.ds(pl.multiple_of(i * KC, KC), KC)
        return pltpu.make_async_copy(res.at[f, chunk], o_all.at[f, chunk], out_sem.at[f, i])

    def step2_loop(g):
        def body(i, carry):
            k0 = pl.multiple_of(i * KC, KC)
            for f in (2 * g, 2 * g + 1):
                res[f, pl.ds(k0, KC)] = step(b1, x1, f, k0, g == 0)
                out_copy(f, i).start()
            return carry

        lax.fori_loop(0, levels // KC, body, 0, unroll=True)

    receive(1)
    step1_loop(0)
    send(3)
    receive(2)
    step1_loop(1)
    send(4)
    for r in range(3):
        finish_sends(r)
    receive(3)
    step2_loop(0)
    receive(4)
    step2_loop(1)
    finish_sends(3)
    finish_sends(4)
    for f in range(N_TRACERS):
        for i in range(levels // KC):
            out_copy(f, i).wait()


def split_kernel(stacked, o_t, o_s, o_ct, o_cs, held, in_sem, out_sem):
    ins = []
    for f in range(N_TRACERS):
        cp = pltpu.make_async_copy(stacked.at[f], held.at[f], in_sem.at[f])
        cp.start()
        ins.append(cp)
    outs = []
    for f, dst in enumerate((o_t, o_s, o_ct, o_cs)):
        ins[f].wait()
        cp = pltpu.make_async_copy(held.at[f], dst, out_sem.at[f])
        cp.start()
        outs.append(cp)
    for cp in outs:
        cp.wait()


def local(n_ew, n_ns, temp, salt, u_east, v_north, wet, cot_temp, cot_salt):
    levels, rows, cols = temp.shape
    f32 = jnp.float32
    any_spec = pl.BlockSpec(memory_space=pl.ANY)
    vmem_spec = pl.BlockSpec(memory_space=pltpu.VMEM)
    out = jax.ShapeDtypeStruct((levels, rows, cols), f32)
    call = pl.pallas_call(
        functools.partial(kernel, n_ew, n_ns, levels, rows, cols),
        out_shape=jax.ShapeDtypeStruct((N_TRACERS, levels, rows, cols), f32),
        in_specs=[any_spec] * 7,
        out_specs=any_spec,
        scratch_shapes=[
            pltpu.VMEM((N_FIELDS, levels + 2, rows + 2 * PAD, cols), f32),
            pltpu.VMEM((X_FIELDS, levels, rows, cols), f32),
            pltpu.VMEM((X_FIELDS, cols, levels * rows), f32),
            pltpu.VMEM((X_FIELDS, cols, levels * rows), f32),
            pltpu.VMEM((N_TRACERS, levels + 2, rows + 2 * PAD, cols), f32),
            pltpu.VMEM((N_TRACERS, levels, rows, cols), f32),
            pltpu.VMEM((N_TRACERS, cols, levels * rows), f32),
            pltpu.VMEM((N_TRACERS, cols, levels * rows), f32),
            pltpu.VMEM((19, levels, rows, cols), f32),
            pltpu.VMEM((N_TRACERS, levels, rows, cols), f32),
            pltpu.VMEM((levels, rows, cols), jnp.int32),
            pltpu.SemaphoreType.DMA((7,)),
            pltpu.SemaphoreType.DMA((5, 4)),
            pltpu.SemaphoreType.DMA((5, 4)),
            pltpu.SemaphoreType.DMA((N_TRACERS, levels // KC)),
        ],
        compiler_params=pltpu.CompilerParams(
            collective_id=0, has_side_effects=True, vmem_limit_bytes=56 * 1024 * 1024
        ),
    )
    stacked = call(temp, salt, cot_temp, cot_salt, u_east, v_north, wet)
    return pl.pallas_call(
        split_kernel,
        out_shape=(out,) * 4,
        in_specs=[any_spec],
        out_specs=(any_spec,) * 4,
        scratch_shapes=[
            pltpu.VMEM((N_TRACERS, levels, rows, cols), f32),
            pltpu.SemaphoreType.DMA((N_TRACERS,)),
            pltpu.SemaphoreType.DMA((N_TRACERS,)),
        ],
    )(stacked)


def solution(mesh):
    spec = P(None, "ns", "ew")
    n_ew = mesh.shape["ew"]
    n_ns = mesh.shape["ns"]
    return jax.shard_map(
        functools.partial(local, n_ew, n_ns), mesh=mesh,
        in_specs=(spec,) * 7, out_specs=(spec,) * 4, check_vma=False,
    )
```

```python
import functools

import jax
import jax.numpy as jnp
from jax import lax
from jax.experimental import pallas as pl
from jax.experimental.pallas import tpu as pltpu
from jax.sharding import PartitionSpec as P

horizontal_mix = 0.05
vertical_mix = 0.2

PAD = 8
KC = 8
N_FIELDS = 7
X_FIELDS = 6
N_TRACERS = 4
U, M, V = 4, 5, 6
MESH = pl.DeviceIdType.MESH


def coefficients(speed):
    magnitude = jnp.abs(speed)
    return (
        (-speed - magnitude) / 12.0,
        (7.0 * speed + 3.0 * magnitude) / 12.0 + horizontal_mix,
        (7.0 * speed - 3.0 * magnitude) / 12.0 - horizontal_mix,
        (-speed + magnitude) / 12.0,
    )


def shift_x(c, left, right, lane, cols):
    cm1 = pltpu.roll(jnp.where(lane >= cols - 1, left, c), 1, 2)
    cm2 = pltpu.roll(jnp.where(lane >= cols - 2, left, c), 2, 2)
    cp1 = pltpu.roll(jnp.where(lane < 1, right, c), cols - 1, 2)
    cp2 = pltpu.roll(jnp.where(lane < 2, right, c), cols - 2, 2)
    return cm2, cm1, cp1, cp2


def kernel(n_ew, n_ns, levels, rows, cols,
           t_hbm, s_hbm, ct_hbm, cs_hbm, u_hbm, v_hbm, wet_ref,
           o_all,
           b0, x0, ts0, rt0, b1, x1, ts1, rt1, w, res, wet_vmem, load_sem, send_sem, recv_sem, out_sem):
    ew = lax.axis_index("ew")
    ns = lax.axis_index("ns")
    east = (lax.rem(ew + 1, n_ew), ns)
    west = (lax.rem(ew + n_ew - 1, n_ew), ns)
    north = (ew, jnp.minimum(ns + 1, n_ns - 1))
    south = (ew, jnp.maximum(ns - 1, 0))
    has_north = ns < n_ns - 1
    has_south = ns > 0
    inner = pl.ds(PAD, rows)
    lev = pl.ds(1, levels)

    barrier = pltpu.get_barrier_semaphore()
    pl.semaphore_signal(barrier, 1, device_id=east, device_id_type=MESH)
    pl.semaphore_signal(barrier, 1, device_id=west, device_id_type=MESH)

    @pl.when(has_north)
    def _():
        pl.semaphore_signal(barrier, 1, device_id=north, device_id_type=MESH)

    @pl.when(has_south)
    def _():
        pl.semaphore_signal(barrier, 1, device_id=south, device_id_type=MESH)

    loads = []
    fields = ((0, t_hbm), (1, s_hbm), (2, ct_hbm), (3, cs_hbm), (U, u_hbm), (V, v_hbm))
    for j, (f, src) in enumerate(fields):
        cp = pltpu.make_async_copy(src, b0.at[f, lev, inner, :], load_sem.at[j])
        cp.start()
        loads.append(cp)
    wet_load = pltpu.make_async_copy(wet_ref, wet_vmem, load_sem.at[len(fields)])
    wet_load.start()

    for buf, nf in ((b0, N_FIELDS), (b1, N_TRACERS)):
        zl = jnp.zeros((nf, 1, rows + 2 * PAD, cols), jnp.float32)
        buf[:, pl.ds(0, 1), :, :] = zl
        buf[:, pl.ds(levels + 1, 1), :, :] = zl
        zr = jnp.zeros((nf, levels, 2, cols), jnp.float32)

        @pl.when(jnp.logical_not(has_south))
        def _():
            buf[:, lev, pl.ds(PAD - 2, 2), :] = zr

        @pl.when(jnp.logical_not(has_north))
        def _():
            buf[:, lev, pl.ds(PAD + rows, 2), :] = zr

    wet_load.wait()
    b0[M, lev, inner, :] = wet_vmem[...].astype(jnp.float32)
    for cp in loads:
        cp.wait()

    peers = 2 + has_north.astype(jnp.int32) + has_south.astype(jnp.int32)
    pl.semaphore_wait(barrier, peers)

    def group(r):
        if r == 0:
            return b0, ts0, rt0, x0, pl.ds(M, 2), pl.ds(U, 2)
        g = pl.ds(2 * ((r - 1) % 2), 2)
        if r <= 2:
            return b0, ts0, rt0, x0, g, g
        return b1, ts1, rt1, x1, g, g

    def edge_copy(r, d, dev):
        buf, ts, rt, _, fy, fx = group(r)
        if d == 0:
            src = buf.at[fy, lev, pl.ds(PAD + rows - 2, 2), :]
            dst = buf.at[fy, lev, pl.ds(PAD - 2, 2), :]
        elif d == 1:
            src = buf.at[fy, lev, pl.ds(PAD, 2), :]
            dst = buf.at[fy, lev, pl.ds(PAD + rows, 2), :]
        elif d == 2:
            src = ts.at[fx, pl.ds(cols - 2, 2), :]
            dst = rt.at[fx, pl.ds(cols - 2, 2), :]
        else:
            src = ts.at[fx, pl.ds(0, 2), :]
            dst = rt.at[fx, pl.ds(0, 2), :]
        return pltpu.make_async_remote_copy(
            src_ref=src, dst_ref=dst, send_sem=send_sem.at[r, d], recv_sem=recv_sem.at[r, d],
            device_id=dev, device_id_type=MESH,
        )

    def x_fields(r):
        if r == 0:
            return (U, M)
        g = (r - 1) % 2
        return range(2 * g, 2 * g + 2)

    outgoing = ((0, north, has_north), (1, south, has_south), (2, east, None), (3, west, None))
    incoming = ((0, south, has_south), (1, north, has_north), (2, west, None), (3, east, None))

    def each(r, pairs, action):
        for d, dev, cond in pairs:
            if cond is None:
                action(edge_copy(r, d, dev))
            else:
                pl.when(cond)(lambda d=d, dev=dev: action(edge_copy(r, d, dev)))

    def send_rows(r):
        each(r, outgoing[:2], lambda c: c.start())

    def send_columns(r):
        buf, ts = group(r)[:2]
        for f in x_fields(r):
            ts[f] = buf[f, lev, inner, :].reshape(levels * rows, cols).T
        each(r, outgoing[2:], lambda c: c.start())

    def send(r):
        send_rows(r)
        send_columns(r)

    def receive(r):
        rt, x = group(r)[2:4]
        each(r, incoming, lambda c: c.wait_recv())
        for f in x_fields(r):
            x[f] = rt[f].T.reshape(levels, rows, cols)

    def finish_sends(r):
        each(r, outgoing, lambda c: c.wait_send())

    for r in range(3):
        send_rows(r)
    for r in range(3):
        send_columns(r)
    receive(0)

    lane = lax.broadcasted_iota(jnp.int32, (KC, rows, cols), 2)

    def rows_at(buf, f, k0, d):
        return buf[f, pl.ds(1 + k0, KC), pl.ds(PAD + d, rows), :]

    def weights_body(i, carry):
        k0 = pl.multiple_of(i * KC, KC)
        kk = pl.ds(k0, KC)
        u0 = rows_at(b0, U, k0, 0)
        um2, um1, up1, _ = shift_x(u0, x0[U, kk], x0[U, kk], lane, cols)
        m0 = rows_at(b0, M, k0, 0)
        mm2, mm1, mp1, mp2 = shift_x(m0, x0[M, kk], x0[M, kk], lane, cols)
        v0 = rows_at(b0, V, k0, 0)
        vm1, vm2, vp1 = rows_at(b0, V, k0, -1), rows_at(b0, V, k0, -2), rows_at(b0, V, k0, 1)
        nm2, nm1 = rows_at(b0, M, k0, -2), rows_at(b0, M, k0, -1)
        np1, np2 = rows_at(b0, M, k0, 1), rows_at(b0, M, k0, 2)
        centre = None
        for base, (s_m2, s_m1, s_0, s_p1), (q_m2, q_m1, q_0, q_p1, q_p2) in (
            (0, (um2, um1, u0, up1), (mm2, mm1, m0, mp1, mp2)),
            (4, (vm2, vm1, v0, vp1), (nm2, nm1, m0, np1, np2)),
        ):
            a0 = coefficients(s_0)
            am1 = coefficients(s_m1)
            o0 = q_0 * q_p1
            om1 = q_m1 * q_0
            here = [o0 * a0[k] for k in range(4)]
            back = [om1 * am1[k] for k in range(4)]
            ahead0 = (q_p1 * q_p2) * coefficients(s_p1)[0]
            behind3 = (q_m2 * q_m1) * coefficients(s_m2)[3]
            w[base + 0, kk] = back[0]
            w[base + 1, kk] = back[1] - here[0]
            w[base + 2, kk] = back[3] - here[2]
            w[base + 3, kk] = -here[3]
            w[8 + base + 0, kk] = -behind3
            w[8 + base + 1, kk] = behind3 - back[2]
            w[8 + base + 2, kk] = here[1] - ahead0
            w[8 + base + 3, kk] = ahead0
            mid = back[2] - here[1]
            centre = mid if centre is None else centre + mid
        m_dn = b0[M, pl.ds(k0, KC), inner, :]
        m_up = b0[M, pl.ds(2 + k0, KC), inner, :]
        z_lo = vertical_mix * (m_dn * m0)
        z_hi = vertical_mix * (m0 * m_up)
        w[16, kk] = z_lo
        w[17, kk] = z_hi
        w[18, kk] = 1.0 + centre - (z_lo + z_hi)
        return carry

    lax.fori_loop(0, levels // KC, weights_body, 0, unroll=True)

    def step(src, xh, f, k0, forward):
        kk = pl.ds(k0, KC)
        c = rows_at(src, f, k0, 0)
        cm2, cm1, cp1, cp2 = shift_x(c, xh[f, kk], xh[f, kk], lane, cols)
        ym2, ym1 = rows_at(src, f, k0, -2), rows_at(src, f, k0, -1)
        yp1, yp2 = rows_at(src, f, k0, 1), rows_at(src, f, k0, 2)
        zm = src[f, pl.ds(k0, KC), inner, :]
        zp = src[f, pl.ds(2 + k0, KC), inner, :]
        o = 0 if forward else 8
        sx = (w[o + 0, kk] * cm2 + w[o + 1, kk] * cm1) + (w[o + 2, kk] * cp1 + w[o + 3, kk] * cp2)
        sy = (w[o + 4, kk] * ym2 + w[o + 5, kk] * ym1) + (w[o + 6, kk] * yp1 + w[o + 7, kk] * yp2)
        sz = w[16, kk] * zm + w[17, kk] * zp
        return (w[18, kk] * c + sz) + (sx + sy)

    def step1_loop(g):
        def body(i, carry):
            k0 = pl.multiple_of(i * KC, KC)
            for f in (2 * g, 2 * g + 1):
                b1[f, pl.ds(1 + k0, KC), inner, :] = step(b0, x0, f, k0, g == 0)
            return carry

        lax.fori_loop(0, levels // KC, body, 0, unroll=True)

    def out_copy(f, i):
        chunk = pl.ds(pl.multiple_of(i * KC, KC), KC)
        return pltpu.make_async_copy(res.at[f, chunk], o_all.at[f, chunk], out_sem.at[f, i])

    def step2_loop(g):
        def body(i, carry):
            k0 = pl.multiple_of(i * KC, KC)
            for f in (2 * g, 2 * g + 1):
                res[f, pl.ds(k0, KC)] = step(b1, x1, f, k0, g == 0)
                out_copy(f, i).start()
            return carry

        lax.fori_loop(0, levels // KC, body, 0, unroll=True)

    receive(1)
    step1_loop(0)
    send(3)
    receive(2)
    step1_loop(1)
    send(4)
    for r in range(3):
        finish_sends(r)
    receive(3)
    step2_loop(0)
    receive(4)
    step2_loop(1)
    finish_sends(3)
    finish_sends(4)
    for f in range(N_TRACERS):
        for i in range(levels // KC):
            out_copy(f, i).wait()


def split_kernel(stacked, o_t, o_s, o_ct, o_cs, held, in_sem, out_sem):
    levels = stacked.shape[1]
    chunks = [(f, pl.ds(i * KC, KC)) for f in range(N_TRACERS) for i in range(levels // KC)]
    ins = []
    for j, (f, kk) in enumerate(chunks):
        cp = pltpu.make_async_copy(stacked.at[f, kk], held.at[f, kk], in_sem.at[j])
        cp.start()
        ins.append(cp)
    dsts = (o_t, o_s, o_ct, o_cs)
    outs = []
    for j, (f, kk) in enumerate(chunks):
        ins[j].wait()
        cp = pltpu.make_async_copy(held.at[f, kk], dsts[f].at[kk], out_sem.at[j])
        cp.start()
        outs.append(cp)
    for cp in outs:
        cp.wait()


def local(n_ew, n_ns, temp, salt, u_east, v_north, wet, cot_temp, cot_salt):
    levels, rows, cols = temp.shape
    f32 = jnp.float32
    any_spec = pl.BlockSpec(memory_space=pl.ANY)
    vmem_spec = pl.BlockSpec(memory_space=pltpu.VMEM)
    out = jax.ShapeDtypeStruct((levels, rows, cols), f32)
    call = pl.pallas_call(
        functools.partial(kernel, n_ew, n_ns, levels, rows, cols),
        out_shape=jax.ShapeDtypeStruct((N_TRACERS, levels, rows, cols), f32),
        in_specs=[any_spec] * 7,
        out_specs=any_spec,
        scratch_shapes=[
            pltpu.VMEM((N_FIELDS, levels + 2, rows + 2 * PAD, cols), f32),
            pltpu.VMEM((X_FIELDS, levels, rows, cols), f32),
            pltpu.VMEM((X_FIELDS, cols, levels * rows), f32),
            pltpu.VMEM((X_FIELDS, cols, levels * rows), f32),
            pltpu.VMEM((N_TRACERS, levels + 2, rows + 2 * PAD, cols), f32),
            pltpu.VMEM((N_TRACERS, levels, rows, cols), f32),
            pltpu.VMEM((N_TRACERS, cols, levels * rows), f32),
            pltpu.VMEM((N_TRACERS, cols, levels * rows), f32),
            pltpu.VMEM((19, levels, rows, cols), f32),
            pltpu.VMEM((N_TRACERS, levels, rows, cols), f32),
            pltpu.VMEM((levels, rows, cols), jnp.int32),
            pltpu.SemaphoreType.DMA((7,)),
            pltpu.SemaphoreType.DMA((5, 4)),
            pltpu.SemaphoreType.DMA((5, 4)),
            pltpu.SemaphoreType.DMA((N_TRACERS, levels // KC)),
        ],
        compiler_params=pltpu.CompilerParams(
            collective_id=0, has_side_effects=True, vmem_limit_bytes=56 * 1024 * 1024
        ),
    )
    stacked = call(temp, salt, cot_temp, cot_salt, u_east, v_north, wet)
    return pl.pallas_call(
        split_kernel,
        out_shape=(out,) * 4,
        in_specs=[any_spec],
        out_specs=(any_spec,) * 4,
        scratch_shapes=[
            pltpu.VMEM((N_TRACERS, levels, rows, cols), f32),
            pltpu.SemaphoreType.DMA((N_TRACERS * levels // KC,)),
            pltpu.SemaphoreType.DMA((N_TRACERS * levels // KC,)),
        ],
    )(stacked)


def solution(mesh):
    spec = P(None, "ns", "ew")
    n_ew = mesh.shape["ew"]
    n_ns = mesh.shape["ns"]
    return jax.shard_map(
        functools.partial(local, n_ew, n_ns), mesh=mesh,
        in_specs=(spec,) * 7, out_specs=(spec,) * 4, check_vma=False,
    )
```

```python
import functools

import jax
import jax.numpy as jnp
from jax import lax
from jax.experimental import pallas as pl
from jax.experimental.pallas import tpu as pltpu
from jax.sharding import PartitionSpec as P

horizontal_mix = 0.05
vertical_mix = 0.2

PAD = 8
KC = 4
N_FIELDS = 7
X_FIELDS = 6
N_TRACERS = 4
U, M, V = 4, 5, 6
MESH = pl.DeviceIdType.MESH


def coefficients(speed):
    magnitude = jnp.abs(speed)
    return (
        (-speed - magnitude) / 12.0,
        (7.0 * speed + 3.0 * magnitude) / 12.0 + horizontal_mix,
        (7.0 * speed - 3.0 * magnitude) / 12.0 - horizontal_mix,
        (-speed + magnitude) / 12.0,
    )


def shift_x(c, left, right, lane, cols):
    cm1 = pltpu.roll(jnp.where(lane >= cols - 1, left, c), 1, 2)
    cm2 = pltpu.roll(jnp.where(lane >= cols - 2, left, c), 2, 2)
    cp1 = pltpu.roll(jnp.where(lane < 1, right, c), cols - 1, 2)
    cp2 = pltpu.roll(jnp.where(lane < 2, right, c), cols - 2, 2)
    return cm2, cm1, cp1, cp2


def kernel(n_ew, n_ns, levels, rows, cols,
           t_hbm, s_hbm, ct_hbm, cs_hbm, u_hbm, v_hbm, wet_ref,
           o_all,
           b0, x0, ts0, rt0, b1, x1, ts1, rt1, w, res, wet_vmem, load_sem, send_sem, recv_sem, out_sem):
    ew = lax.axis_index("ew")
    ns = lax.axis_index("ns")
    east = (lax.rem(ew + 1, n_ew), ns)
    west = (lax.rem(ew + n_ew - 1, n_ew), ns)
    north = (ew, jnp.minimum(ns + 1, n_ns - 1))
    south = (ew, jnp.maximum(ns - 1, 0))
    has_north = ns < n_ns - 1
    has_south = ns > 0
    inner = pl.ds(PAD, rows)
    lev = pl.ds(1, levels)

    barrier = pltpu.get_barrier_semaphore()
    pl.semaphore_signal(barrier, 1, device_id=east, device_id_type=MESH)
    pl.semaphore_signal(barrier, 1, device_id=west, device_id_type=MESH)

    @pl.when(has_north)
    def _():
        pl.semaphore_signal(barrier, 1, device_id=north, device_id_type=MESH)

    @pl.when(has_south)
    def _():
        pl.semaphore_signal(barrier, 1, device_id=south, device_id_type=MESH)

    loads = []
    fields = ((0, t_hbm), (1, s_hbm), (2, ct_hbm), (3, cs_hbm), (U, u_hbm), (V, v_hbm))
    for j, (f, src) in enumerate(fields):
        cp = pltpu.make_async_copy(src, b0.at[f, lev, inner, :], load_sem.at[j])
        cp.start()
        loads.append(cp)
    wet_load = pltpu.make_async_copy(wet_ref, wet_vmem, load_sem.at[len(fields)])
    wet_load.start()

    for buf, nf in ((b0, N_FIELDS), (b1, N_TRACERS)):
        zl = jnp.zeros((nf, 1, rows + 2 * PAD, cols), jnp.float32)
        buf[:, pl.ds(0, 1), :, :] = zl
        buf[:, pl.ds(levels + 1, 1), :, :] = zl
        zr = jnp.zeros((nf, levels, 2, cols), jnp.float32)

        @pl.when(jnp.logical_not(has_south))
        def _():
            buf[:, lev, pl.ds(PAD - 2, 2), :] = zr

        @pl.when(jnp.logical_not(has_north))
        def _():
            buf[:, lev, pl.ds(PAD + rows, 2), :] = zr

    wet_load.wait()
    b0[M, lev, inner, :] = wet_vmem[...].astype(jnp.float32)
    for cp in loads:
        cp.wait()

    peers = 2 + has_north.astype(jnp.int32) + has_south.astype(jnp.int32)
    pl.semaphore_wait(barrier, peers)

    def group(r):
        if r == 0:
            return b0, ts0, rt0, x0, pl.ds(M, 2), pl.ds(U, 2)
        g = pl.ds(2 * ((r - 1) % 2), 2)
        if r <= 2:
            return b0, ts0, rt0, x0, g, g
        return b1, ts1, rt1, x1, g, g

    def edge_copy(r, d, dev):
        buf, ts, rt, _, fy, fx = group(r)
        if d == 0:
            src = buf.at[fy, lev, pl.ds(PAD + rows - 2, 2), :]
            dst = buf.at[fy, lev, pl.ds(PAD - 2, 2), :]
        elif d == 1:
            src = buf.at[fy, lev, pl.ds(PAD, 2), :]
            dst = buf.at[fy, lev, pl.ds(PAD + rows, 2), :]
        elif d == 2:
            src = ts.at[fx, pl.ds(cols - 2, 2), :]
            dst = rt.at[fx, pl.ds(cols - 2, 2), :]
        else:
            src = ts.at[fx, pl.ds(0, 2), :]
            dst = rt.at[fx, pl.ds(0, 2), :]
        return pltpu.make_async_remote_copy(
            src_ref=src, dst_ref=dst, send_sem=send_sem.at[r, d], recv_sem=recv_sem.at[r, d],
            device_id=dev, device_id_type=MESH,
        )

    def x_fields(r):
        if r == 0:
            return (U, M)
        g = (r - 1) % 2
        return range(2 * g, 2 * g + 2)

    outgoing = ((0, north, has_north), (1, south, has_south), (2, east, None), (3, west, None))
    incoming = ((0, south, has_south), (1, north, has_north), (2, west, None), (3, east, None))

    def each(r, pairs, action):
        for d, dev, cond in pairs:
            if cond is None:
                action(edge_copy(r, d, dev))
            else:
                pl.when(cond)(lambda d=d, dev=dev: action(edge_copy(r, d, dev)))

    def send_rows(r):
        each(r, outgoing[:2], lambda c: c.start())

    def send_columns(r):
        buf, ts = group(r)[:2]
        for f in x_fields(r):
            ts[f] = buf[f, lev, inner, :].reshape(levels * rows, cols).T
        each(r, outgoing[2:], lambda c: c.start())

    def send(r):
        send_rows(r)
        send_columns(r)

    def receive(r):
        rt, x = group(r)[2:4]
        each(r, incoming, lambda c: c.wait_recv())
        for f in x_fields(r):
            x[f] = rt[f].T.reshape(levels, rows, cols)

    def finish_sends(r):
        each(r, outgoing, lambda c: c.wait_send())

    for r in range(3):
        send_rows(r)
    for r in range(3):
        send_columns(r)
    receive(0)

    lane = lax.broadcasted_iota(jnp.int32, (KC, rows, cols), 2)

    def rows_at(buf, f, k0, d):
        return buf[f, pl.ds(1 + k0, KC), pl.ds(PAD + d, rows), :]

    def weights_body(i, carry):
        k0 = pl.multiple_of(i * KC, KC)
        kk = pl.ds(k0, KC)
        u0 = rows_at(b0, U, k0, 0)
        um2, um1, up1, _ = shift_x(u0, x0[U, kk], x0[U, kk], lane, cols)
        m0 = rows_at(b0, M, k0, 0)
        mm2, mm1, mp1, mp2 = shift_x(m0, x0[M, kk], x0[M, kk], lane, cols)
        v0 = rows_at(b0, V, k0, 0)
        vm1, vm2, vp1 = rows_at(b0, V, k0, -1), rows_at(b0, V, k0, -2), rows_at(b0, V, k0, 1)
        nm2, nm1 = rows_at(b0, M, k0, -2), rows_at(b0, M, k0, -1)
        np1, np2 = rows_at(b0, M, k0, 1), rows_at(b0, M, k0, 2)
        centre = None
        for base, (s_m2, s_m1, s_0, s_p1), (q_m2, q_m1, q_0, q_p1, q_p2) in (
            (0, (um2, um1, u0, up1), (mm2, mm1, m0, mp1, mp2)),
            (4, (vm2, vm1, v0, vp1), (nm2, nm1, m0, np1, np2)),
        ):
            a0 = coefficients(s_0)
            am1 = coefficients(s_m1)
            o0 = q_0 * q_p1
            om1 = q_m1 * q_0
            here = [o0 * a0[k] for k in range(4)]
            back = [om1 * am1[k] for k in range(4)]
            ahead0 = (q_p1 * q_p2) * coefficients(s_p1)[0]
            behind3 = (q_m2 * q_m1) * coefficients(s_m2)[3]
            w[base + 0, kk] = back[0]
            w[base + 1, kk] = back[1] - here[0]
            w[base + 2, kk] = back[3] - here[2]
            w[base + 3, kk] = -here[3]
            w[8 + base + 0, kk] = -behind3
            w[8 + base + 1, kk] = behind3 - back[2]
            w[8 + base + 2, kk] = here[1] - ahead0
            w[8 + base + 3, kk] = ahead0
            mid = back[2] - here[1]
            centre = mid if centre is None else centre + mid
        m_dn = b0[M, pl.ds(k0, KC), inner, :]
        m_up = b0[M, pl.ds(2 + k0, KC), inner, :]
        z_lo = vertical_mix * (m_dn * m0)
        z_hi = vertical_mix * (m0 * m_up)
        w[16, kk] = z_lo
        w[17, kk] = z_hi
        w[18, kk] = 1.0 + centre - (z_lo + z_hi)
        return carry

    lax.fori_loop(0, levels // KC, weights_body, 0, unroll=True)

    def step(src, xh, f, k0, forward):
        kk = pl.ds(k0, KC)
        c = rows_at(src, f, k0, 0)
        cm2, cm1, cp1, cp2 = shift_x(c, xh[f, kk], xh[f, kk], lane, cols)
        ym2, ym1 = rows_at(src, f, k0, -2), rows_at(src, f, k0, -1)
        yp1, yp2 = rows_at(src, f, k0, 1), rows_at(src, f, k0, 2)
        zm = src[f, pl.ds(k0, KC), inner, :]
        zp = src[f, pl.ds(2 + k0, KC), inner, :]
        o = 0 if forward else 8
        sx = (w[o + 0, kk] * cm2 + w[o + 1, kk] * cm1) + (w[o + 2, kk] * cp1 + w[o + 3, kk] * cp2)
        sy = (w[o + 4, kk] * ym2 + w[o + 5, kk] * ym1) + (w[o + 6, kk] * yp1 + w[o + 7, kk] * yp2)
        sz = w[16, kk] * zm + w[17, kk] * zp
        return (w[18, kk] * c + sz) + (sx + sy)

    def step1_loop(g):
        def body(i, carry):
            k0 = pl.multiple_of(i * KC, KC)
            for f in (2 * g, 2 * g + 1):
                b1[f, pl.ds(1 + k0, KC), inner, :] = step(b0, x0, f, k0, g == 0)
            return carry

        lax.fori_loop(0, levels // KC, body, 0, unroll=True)

    def out_copy(f, i):
        chunk = pl.ds(pl.multiple_of(i * KC, KC), KC)
        return pltpu.make_async_copy(res.at[f, chunk], o_all.at[f, chunk], out_sem.at[f, i])

    def step2_loop(g):
        def body(i, carry):
            k0 = pl.multiple_of(i * KC, KC)
            for f in (2 * g, 2 * g + 1):
                res[f, pl.ds(k0, KC)] = step(b1, x1, f, k0, g == 0)
                out_copy(f, i).start()
            return carry

        lax.fori_loop(0, levels // KC, body, 0, unroll=True)

    receive(1)
    step1_loop(0)
    send(3)
    receive(2)
    step1_loop(1)
    send(4)
    for r in range(3):
        finish_sends(r)
    receive(3)
    step2_loop(0)
    receive(4)
    step2_loop(1)
    finish_sends(3)
    finish_sends(4)
    for f in range(N_TRACERS):
        for i in range(levels // KC):
            out_copy(f, i).wait()


def split_kernel(stacked, o_t, o_s, o_ct, o_cs, held, in_sem, out_sem):
    ins = []
    for f in range(N_TRACERS):
        cp = pltpu.make_async_copy(stacked.at[f], held.at[f], in_sem.at[f])
        cp.start()
        ins.append(cp)
    outs = []
    for f, dst in enumerate((o_t, o_s, o_ct, o_cs)):
        ins[f].wait()
        cp = pltpu.make_async_copy(held.at[f], dst, out_sem.at[f])
        cp.start()
        outs.append(cp)
    for cp in outs:
        cp.wait()


def local(n_ew, n_ns, temp, salt, u_east, v_north, wet, cot_temp, cot_salt):
    levels, rows, cols = temp.shape
    f32 = jnp.float32
    any_spec = pl.BlockSpec(memory_space=pl.ANY)
    vmem_spec = pl.BlockSpec(memory_space=pltpu.VMEM)
    out = jax.ShapeDtypeStruct((levels, rows, cols), f32)
    call = pl.pallas_call(
        functools.partial(kernel, n_ew, n_ns, levels, rows, cols),
        out_shape=jax.ShapeDtypeStruct((N_TRACERS, levels, rows, cols), f32),
        in_specs=[any_spec] * 7,
        out_specs=any_spec,
        scratch_shapes=[
            pltpu.VMEM((N_FIELDS, levels + 2, rows + 2 * PAD, cols), f32),
            pltpu.VMEM((X_FIELDS, levels, rows, cols), f32),
            pltpu.VMEM((X_FIELDS, cols, levels * rows), f32),
            pltpu.VMEM((X_FIELDS, cols, levels * rows), f32),
            pltpu.VMEM((N_TRACERS, levels + 2, rows + 2 * PAD, cols), f32),
            pltpu.VMEM((N_TRACERS, levels, rows, cols), f32),
            pltpu.VMEM((N_TRACERS, cols, levels * rows), f32),
            pltpu.VMEM((N_TRACERS, cols, levels * rows), f32),
            pltpu.VMEM((19, levels, rows, cols), f32),
            pltpu.VMEM((N_TRACERS, levels, rows, cols), f32),
            pltpu.VMEM((levels, rows, cols), jnp.int32),
            pltpu.SemaphoreType.DMA((7,)),
            pltpu.SemaphoreType.DMA((5, 4)),
            pltpu.SemaphoreType.DMA((5, 4)),
            pltpu.SemaphoreType.DMA((N_TRACERS, levels // KC)),
        ],
        compiler_params=pltpu.CompilerParams(
            collective_id=0, has_side_effects=True, vmem_limit_bytes=56 * 1024 * 1024
        ),
    )
    stacked = call(temp, salt, cot_temp, cot_salt, u_east, v_north, wet)
    return pl.pallas_call(
        split_kernel,
        out_shape=(out,) * 4,
        in_specs=[any_spec],
        out_specs=(any_spec,) * 4,
        scratch_shapes=[
            pltpu.VMEM((N_TRACERS, levels, rows, cols), f32),
            pltpu.SemaphoreType.DMA((N_TRACERS,)),
            pltpu.SemaphoreType.DMA((N_TRACERS,)),
        ],
    )(stacked)


def solution(mesh):
    spec = P(None, "ns", "ew")
    n_ew = mesh.shape["ew"]
    n_ns = mesh.shape["ns"]
    return jax.shard_map(
        functools.partial(local, n_ew, n_ns), mesh=mesh,
        in_specs=(spec,) * 7, out_specs=(spec,) * 4, check_vma=False,
    )
```

```python
import functools

import jax
import jax.numpy as jnp
from jax import lax
from jax.experimental import pallas as pl
from jax.experimental.pallas import tpu as pltpu
from jax.sharding import PartitionSpec as P

horizontal_mix = 0.05
vertical_mix = 0.2

PAD = 8
KC = 4
N_FIELDS = 7
X_FIELDS = 6
N_TRACERS = 4
U, M, V = 4, 5, 6
MESH = pl.DeviceIdType.MESH


def coefficients(speed):
    magnitude = jnp.abs(speed)
    return (
        (-speed - magnitude) / 12.0,
        (7.0 * speed + 3.0 * magnitude) / 12.0 + horizontal_mix,
        (7.0 * speed - 3.0 * magnitude) / 12.0 - horizontal_mix,
        (-speed + magnitude) / 12.0,
    )


def shift_x(c, left, right, lane, cols):
    cm1 = pltpu.roll(jnp.where(lane >= cols - 1, left, c), 1, 2)
    cm2 = pltpu.roll(jnp.where(lane >= cols - 2, left, c), 2, 2)
    cp1 = pltpu.roll(jnp.where(lane < 1, right, c), cols - 1, 2)
    cp2 = pltpu.roll(jnp.where(lane < 2, right, c), cols - 2, 2)
    return cm2, cm1, cp1, cp2


def kernel(n_ew, n_ns, levels, rows, cols,
           t_hbm, s_hbm, ct_hbm, cs_hbm, u_hbm, v_hbm, wet_ref,
           o_all,
           b0, x0, ts0, rt0, b1, x1, ts1, rt1, w, res, wet_vmem, load_sem, send_sem, recv_sem, out_sem):
    ew = lax.axis_index("ew")
    ns = lax.axis_index("ns")
    east = (lax.rem(ew + 1, n_ew), ns)
    west = (lax.rem(ew + n_ew - 1, n_ew), ns)
    north = (ew, jnp.minimum(ns + 1, n_ns - 1))
    south = (ew, jnp.maximum(ns - 1, 0))
    has_north = ns < n_ns - 1
    has_south = ns > 0
    inner = pl.ds(PAD, rows)
    lev = pl.ds(1, levels)

    barrier = pltpu.get_barrier_semaphore()
    pl.semaphore_signal(barrier, 1, device_id=east, device_id_type=MESH)
    pl.semaphore_signal(barrier, 1, device_id=west, device_id_type=MESH)

    @pl.when(has_north)
    def _():
        pl.semaphore_signal(barrier, 1, device_id=north, device_id_type=MESH)

    @pl.when(has_south)
    def _():
        pl.semaphore_signal(barrier, 1, device_id=south, device_id_type=MESH)

    loads = []
    fields = ((0, t_hbm), (1, s_hbm), (2, ct_hbm), (3, cs_hbm), (U, u_hbm), (V, v_hbm))
    for j, (f, src) in enumerate(fields):
        cp = pltpu.make_async_copy(src, b0.at[f, lev, inner, :], load_sem.at[j])
        cp.start()
        loads.append(cp)
    wet_load = pltpu.make_async_copy(wet_ref, wet_vmem, load_sem.at[len(fields)])
    wet_load.start()

    for buf, nf in ((b0, N_FIELDS), (b1, N_TRACERS)):
        zl = jnp.zeros((nf, 1, rows + 2 * PAD, cols), jnp.float32)
        buf[:, pl.ds(0, 1), :, :] = zl
        buf[:, pl.ds(levels + 1, 1), :, :] = zl
        zr = jnp.zeros((nf, levels, 2, cols), jnp.float32)

        @pl.when(jnp.logical_not(has_south))
        def _():
            buf[:, lev, pl.ds(PAD - 2, 2), :] = zr

        @pl.when(jnp.logical_not(has_north))
        def _():
            buf[:, lev, pl.ds(PAD + rows, 2), :] = zr

    wet_load.wait()
    b0[M, lev, inner, :] = wet_vmem[...].astype(jnp.float32)
    for cp in loads:
        cp.wait()

    peers = 2 + has_north.astype(jnp.int32) + has_south.astype(jnp.int32)
    pl.semaphore_wait(barrier, peers)

    def group(r):
        if r == 0:
            return b0, ts0, rt0, x0, pl.ds(M, 2), pl.ds(U, 2)
        g = pl.ds(2 * ((r - 1) % 2), 2)
        if r <= 2:
            return b0, ts0, rt0, x0, g, g
        return b1, ts1, rt1, x1, g, g

    def edge_copy(r, d, dev):
        buf, ts, rt, _, fy, fx = group(r)
        if d == 0:
            src = buf.at[fy, lev, pl.ds(PAD + rows - 2, 2), :]
            dst = buf.at[fy, lev, pl.ds(PAD - 2, 2), :]
        elif d == 1:
            src = buf.at[fy, lev, pl.ds(PAD, 2), :]
            dst = buf.at[fy, lev, pl.ds(PAD + rows, 2), :]
        elif d == 2:
            src = ts.at[fx, pl.ds(cols - 2, 2), :]
            dst = rt.at[fx, pl.ds(cols - 2, 2), :]
        else:
            src = ts.at[fx, pl.ds(0, 2), :]
            dst = rt.at[fx, pl.ds(0, 2), :]
        return pltpu.make_async_remote_copy(
            src_ref=src, dst_ref=dst, send_sem=send_sem.at[r, d], recv_sem=recv_sem.at[r, d],
            device_id=dev, device_id_type=MESH,
        )

    def x_fields(r):
        if r == 0:
            return (U, M)
        g = (r - 1) % 2
        return range(2 * g, 2 * g + 2)

    outgoing = ((0, north, has_north), (1, south, has_south), (2, east, None), (3, west, None))
    incoming = ((0, south, has_south), (1, north, has_north), (2, west, None), (3, east, None))

    def each(r, pairs, action):
        for d, dev, cond in pairs:
            if cond is None:
                action(edge_copy(r, d, dev))
            else:
                pl.when(cond)(lambda d=d, dev=dev: action(edge_copy(r, d, dev)))

    def send_rows(r):
        each(r, outgoing[:2], lambda c: c.start())

    def send_columns(r):
        buf, ts = group(r)[:2]
        for f in x_fields(r):
            ts[f] = buf[f, lev, inner, :].reshape(levels * rows, cols).T
        each(r, outgoing[2:], lambda c: c.start())

    def send(r):
        send_rows(r)
        send_columns(r)

    def receive(r):
        rt, x = group(r)[2:4]
        each(r, incoming, lambda c: c.wait_recv())
        for f in x_fields(r):
            x[f] = rt[f].T.reshape(levels, rows, cols)

    def finish_sends(r):
        each(r, outgoing, lambda c: c.wait_send())

    send(0)
    for r in (1, 2):
        send_rows(r)
    for r in (1, 2):
        send_columns(r)
    receive(0)

    lane = lax.broadcasted_iota(jnp.int32, (KC, rows, cols), 2)

    def rows_at(buf, f, k0, d):
        return buf[f, pl.ds(1 + k0, KC), pl.ds(PAD + d, rows), :]

    def weights_body(i, carry):
        k0 = pl.multiple_of(i * KC, KC)
        kk = pl.ds(k0, KC)
        u0 = rows_at(b0, U, k0, 0)
        um2, um1, up1, _ = shift_x(u0, x0[U, kk], x0[U, kk], lane, cols)
        m0 = rows_at(b0, M, k0, 0)
        mm2, mm1, mp1, mp2 = shift_x(m0, x0[M, kk], x0[M, kk], lane, cols)
        v0 = rows_at(b0, V, k0, 0)
        vm1, vm2, vp1 = rows_at(b0, V, k0, -1), rows_at(b0, V, k0, -2), rows_at(b0, V, k0, 1)
        nm2, nm1 = rows_at(b0, M, k0, -2), rows_at(b0, M, k0, -1)
        np1, np2 = rows_at(b0, M, k0, 1), rows_at(b0, M, k0, 2)
        centre = None
        for base, (s_m2, s_m1, s_0, s_p1), (q_m2, q_m1, q_0, q_p1, q_p2) in (
            (0, (um2, um1, u0, up1), (mm2, mm1, m0, mp1, mp2)),
            (4, (vm2, vm1, v0, vp1), (nm2, nm1, m0, np1, np2)),
        ):
            a0 = coefficients(s_0)
            am1 = coefficients(s_m1)
            o0 = q_0 * q_p1
            om1 = q_m1 * q_0
            here = [o0 * a0[k] for k in range(4)]
            back = [om1 * am1[k] for k in range(4)]
            ahead0 = (q_p1 * q_p2) * coefficients(s_p1)[0]
            behind3 = (q_m2 * q_m1) * coefficients(s_m2)[3]
            w[base + 0, kk] = back[0]
            w[base + 1, kk] = back[1] - here[0]
            w[base + 2, kk] = back[3] - here[2]
            w[base + 3, kk] = -here[3]
            w[8 + base + 0, kk] = -behind3
            w[8 + base + 1, kk] = behind3 - back[2]
            w[8 + base + 2, kk] = here[1] - ahead0
            w[8 + base + 3, kk] = ahead0
            mid = back[2] - here[1]
            centre = mid if centre is None else centre + mid
        m_dn = b0[M, pl.ds(k0, KC), inner, :]
        m_up = b0[M, pl.ds(2 + k0, KC), inner, :]
        z_lo = vertical_mix * (m_dn * m0)
        z_hi = vertical_mix * (m0 * m_up)
        w[16, kk] = z_lo
        w[17, kk] = z_hi
        w[18, kk] = 1.0 + centre - (z_lo + z_hi)
        return carry

    lax.fori_loop(0, levels // KC, weights_body, 0, unroll=True)

    def step(src, xh, f, k0, forward):
        kk = pl.ds(k0, KC)
        c = rows_at(src, f, k0, 0)
        cm2, cm1, cp1, cp2 = shift_x(c, xh[f, kk], xh[f, kk], lane, cols)
        ym2, ym1 = rows_at(src, f, k0, -2), rows_at(src, f, k0, -1)
        yp1, yp2 = rows_at(src, f, k0, 1), rows_at(src, f, k0, 2)
        zm = src[f, pl.ds(k0, KC), inner, :]
        zp = src[f, pl.ds(2 + k0, KC), inner, :]
        o = 0 if forward else 8
        sx = (w[o + 0, kk] * cm2 + w[o + 1, kk] * cm1) + (w[o + 2, kk] * cp1 + w[o + 3, kk] * cp2)
        sy = (w[o + 4, kk] * ym2 + w[o + 5, kk] * ym1) + (w[o + 6, kk] * yp1 + w[o + 7, kk] * yp2)
        sz = w[16, kk] * zm + w[17, kk] * zp
        return (w[18, kk] * c + sz) + (sx + sy)

    def step1_loop(g):
        def body(i, carry):
            k0 = pl.multiple_of(i * KC, KC)
            for f in (2 * g, 2 * g + 1):
                b1[f, pl.ds(1 + k0, KC), inner, :] = step(b0, x0, f, k0, g == 0)
            return carry

        lax.fori_loop(0, levels // KC, body, 0, unroll=True)

    def out_copy(f, i):
        chunk = pl.ds(pl.multiple_of(i * KC, KC), KC)
        return pltpu.make_async_copy(res.at[f, chunk], o_all.at[f, chunk], out_sem.at[f, i])

    def step2_loop(g):
        def body(i, carry):
            k0 = pl.multiple_of(i * KC, KC)
            for f in (2 * g, 2 * g + 1):
                res[f, pl.ds(k0, KC)] = step(b1, x1, f, k0, g == 0)
                out_copy(f, i).start()
            return carry

        lax.fori_loop(0, levels // KC, body, 0, unroll=True)

    receive(1)
    step1_loop(0)
    send(3)
    receive(2)
    step1_loop(1)
    send(4)
    for r in range(3):
        finish_sends(r)
    receive(3)
    step2_loop(0)
    receive(4)
    step2_loop(1)
    finish_sends(3)
    finish_sends(4)
    for f in range(N_TRACERS):
        for i in range(levels // KC):
            out_copy(f, i).wait()


def split_kernel(stacked, o_t, o_s, o_ct, o_cs, held, in_sem, out_sem):
    ins = []
    for f in range(N_TRACERS):
        cp = pltpu.make_async_copy(stacked.at[f], held.at[f], in_sem.at[f])
        cp.start()
        ins.append(cp)
    outs = []
    for f, dst in enumerate((o_t, o_s, o_ct, o_cs)):
        ins[f].wait()
        cp = pltpu.make_async_copy(held.at[f], dst, out_sem.at[f])
        cp.start()
        outs.append(cp)
    for cp in outs:
        cp.wait()


def local(n_ew, n_ns, temp, salt, u_east, v_north, wet, cot_temp, cot_salt):
    levels, rows, cols = temp.shape
    f32 = jnp.float32
    any_spec = pl.BlockSpec(memory_space=pl.ANY)
    vmem_spec = pl.BlockSpec(memory_space=pltpu.VMEM)
    out = jax.ShapeDtypeStruct((levels, rows, cols), f32)
    call = pl.pallas_call(
        functools.partial(kernel, n_ew, n_ns, levels, rows, cols),
        out_shape=jax.ShapeDtypeStruct((N_TRACERS, levels, rows, cols), f32),
        in_specs=[any_spec] * 7,
        out_specs=any_spec,
        scratch_shapes=[
            pltpu.VMEM((N_FIELDS, levels + 2, rows + 2 * PAD, cols), f32),
            pltpu.VMEM((X_FIELDS, levels, rows, cols), f32),
            pltpu.VMEM((X_FIELDS, cols, levels * rows), f32),
            pltpu.VMEM((X_FIELDS, cols, levels * rows), f32),
            pltpu.VMEM((N_TRACERS, levels + 2, rows + 2 * PAD, cols), f32),
            pltpu.VMEM((N_TRACERS, levels, rows, cols), f32),
            pltpu.VMEM((N_TRACERS, cols, levels * rows), f32),
            pltpu.VMEM((N_TRACERS, cols, levels * rows), f32),
            pltpu.VMEM((19, levels, rows, cols), f32),
            pltpu.VMEM((N_TRACERS, levels, rows, cols), f32),
            pltpu.VMEM((levels, rows, cols), jnp.int32),
            pltpu.SemaphoreType.DMA((7,)),
            pltpu.SemaphoreType.DMA((5, 4)),
            pltpu.SemaphoreType.DMA((5, 4)),
            pltpu.SemaphoreType.DMA((N_TRACERS, levels // KC)),
        ],
        compiler_params=pltpu.CompilerParams(
            collective_id=0, has_side_effects=True, vmem_limit_bytes=56 * 1024 * 1024
        ),
    )
    stacked = call(temp, salt, cot_temp, cot_salt, u_east, v_north, wet)
    return pl.pallas_call(
        split_kernel,
        out_shape=(out,) * 4,
        in_specs=[any_spec],
        out_specs=(any_spec,) * 4,
        scratch_shapes=[
            pltpu.VMEM((N_TRACERS, levels, rows, cols), f32),
            pltpu.SemaphoreType.DMA((N_TRACERS,)),
            pltpu.SemaphoreType.DMA((N_TRACERS,)),
        ],
    )(stacked)


def solution(mesh):
    spec = P(None, "ns", "ew")
    n_ew = mesh.shape["ew"]
    n_ns = mesh.shape["ns"]
    return jax.shard_map(
        functools.partial(local, n_ew, n_ns), mesh=mesh,
        in_specs=(spec,) * 7, out_specs=(spec,) * 4, check_vma=False,
    )
```

```python
import functools

import jax
import jax.numpy as jnp
from jax import lax
from jax.experimental import pallas as pl
from jax.experimental.pallas import tpu as pltpu
from jax.sharding import PartitionSpec as P

horizontal_mix = 0.05
vertical_mix = 0.2

PAD = 8
KC = 2
N_FIELDS = 7
X_FIELDS = 6
N_TRACERS = 4
U, M, V = 4, 5, 6
MESH = pl.DeviceIdType.MESH


def coefficients(speed):
    magnitude = jnp.abs(speed)
    return (
        (-speed - magnitude) / 12.0,
        (7.0 * speed + 3.0 * magnitude) / 12.0 + horizontal_mix,
        (7.0 * speed - 3.0 * magnitude) / 12.0 - horizontal_mix,
        (-speed + magnitude) / 12.0,
    )


def shift_x(c, left, right, lane, cols):
    cm1 = pltpu.roll(jnp.where(lane >= cols - 1, left, c), 1, 2)
    cm2 = pltpu.roll(jnp.where(lane >= cols - 2, left, c), 2, 2)
    cp1 = pltpu.roll(jnp.where(lane < 1, right, c), cols - 1, 2)
    cp2 = pltpu.roll(jnp.where(lane < 2, right, c), cols - 2, 2)
    return cm2, cm1, cp1, cp2


def kernel(n_ew, n_ns, levels, rows, cols,
           t_hbm, s_hbm, ct_hbm, cs_hbm, u_hbm, v_hbm, wet_ref,
           o_all,
           b0, x0, ts0, rt0, b1, x1, ts1, rt1, w, res, wet_vmem, load_sem, send_sem, recv_sem, out_sem):
    ew = lax.axis_index("ew")
    ns = lax.axis_index("ns")
    east = (lax.rem(ew + 1, n_ew), ns)
    west = (lax.rem(ew + n_ew - 1, n_ew), ns)
    north = (ew, jnp.minimum(ns + 1, n_ns - 1))
    south = (ew, jnp.maximum(ns - 1, 0))
    has_north = ns < n_ns - 1
    has_south = ns > 0
    inner = pl.ds(PAD, rows)
    lev = pl.ds(1, levels)

    barrier = pltpu.get_barrier_semaphore()
    pl.semaphore_signal(barrier, 1, device_id=east, device_id_type=MESH)
    pl.semaphore_signal(barrier, 1, device_id=west, device_id_type=MESH)

    @pl.when(has_north)
    def _():
        pl.semaphore_signal(barrier, 1, device_id=north, device_id_type=MESH)

    @pl.when(has_south)
    def _():
        pl.semaphore_signal(barrier, 1, device_id=south, device_id_type=MESH)

    loads = []
    fields = ((0, t_hbm), (1, s_hbm), (2, ct_hbm), (3, cs_hbm), (U, u_hbm), (V, v_hbm))
    for j, (f, src) in enumerate(fields):
        cp = pltpu.make_async_copy(src, b0.at[f, lev, inner, :], load_sem.at[j])
        cp.start()
        loads.append(cp)
    wet_load = pltpu.make_async_copy(wet_ref, wet_vmem, load_sem.at[len(fields)])
    wet_load.start()

    for buf, nf in ((b0, N_FIELDS), (b1, N_TRACERS)):
        zl = jnp.zeros((nf, 1, rows + 2 * PAD, cols), jnp.float32)
        buf[:, pl.ds(0, 1), :, :] = zl
        buf[:, pl.ds(levels + 1, 1), :, :] = zl
        zr = jnp.zeros((nf, levels, 2, cols), jnp.float32)

        @pl.when(jnp.logical_not(has_south))
        def _():
            buf[:, lev, pl.ds(PAD - 2, 2), :] = zr

        @pl.when(jnp.logical_not(has_north))
        def _():
            buf[:, lev, pl.ds(PAD + rows, 2), :] = zr

    wet_load.wait()
    b0[M, lev, inner, :] = wet_vmem[...].astype(jnp.float32)
    for cp in loads:
        cp.wait()

    peers = 2 + has_north.astype(jnp.int32) + has_south.astype(jnp.int32)
    pl.semaphore_wait(barrier, peers)

    def group(r):
        if r == 0:
            return b0, ts0, rt0, x0, pl.ds(M, 2), pl.ds(U, 2)
        g = pl.ds(2 * ((r - 1) % 2), 2)
        if r <= 2:
            return b0, ts0, rt0, x0, g, g
        return b1, ts1, rt1, x1, g, g

    def edge_copy(r, d, dev):
        buf, ts, rt, _, fy, fx = group(r)
        if d == 0:
            src = buf.at[fy, lev, pl.ds(PAD + rows - 2, 2), :]
            dst = buf.at[fy, lev, pl.ds(PAD - 2, 2), :]
        elif d == 1:
            src = buf.at[fy, lev, pl.ds(PAD, 2), :]
            dst = buf.at[fy, lev, pl.ds(PAD + rows, 2), :]
        elif d == 2:
            src = ts.at[fx, pl.ds(cols - 2, 2), :]
            dst = rt.at[fx, pl.ds(cols - 2, 2), :]
        else:
            src = ts.at[fx, pl.ds(0, 2), :]
            dst = rt.at[fx, pl.ds(0, 2), :]
        return pltpu.make_async_remote_copy(
            src_ref=src, dst_ref=dst, send_sem=send_sem.at[r, d], recv_sem=recv_sem.at[r, d],
            device_id=dev, device_id_type=MESH,
        )

    def x_fields(r):
        if r == 0:
            return (U, M)
        g = (r - 1) % 2
        return range(2 * g, 2 * g + 2)

    outgoing = ((0, north, has_north), (1, south, has_south), (2, east, None), (3, west, None))
    incoming = ((0, south, has_south), (1, north, has_north), (2, west, None), (3, east, None))

    def each(r, pairs, action):
        for d, dev, cond in pairs:
            if cond is None:
                action(edge_copy(r, d, dev))
            else:
                pl.when(cond)(lambda d=d, dev=dev: action(edge_copy(r, d, dev)))

    def send_rows(r):
        each(r, outgoing[:2], lambda c: c.start())

    def send_columns(r):
        buf, ts = group(r)[:2]
        for f in x_fields(r):
            ts[f] = buf[f, lev, inner, :].reshape(levels * rows, cols).T
        each(r, outgoing[2:], lambda c: c.start())

    def send(r):
        send_rows(r)
        send_columns(r)

    def receive(r):
        rt, x = group(r)[2:4]
        each(r, incoming, lambda c: c.wait_recv())
        for f in x_fields(r):
            x[f] = rt[f].T.reshape(levels, rows, cols)

    def finish_sends(r):
        each(r, outgoing, lambda c: c.wait_send())

    for r in range(3):
        send_rows(r)
    for r in range(3):
        send_columns(r)
    receive(0)

    lane = lax.broadcasted_iota(jnp.int32, (KC, rows, cols), 2)

    def rows_at(buf, f, k0, d):
        return buf[f, pl.ds(1 + k0, KC), pl.ds(PAD + d, rows), :]

    def weights_body(i, carry):
        k0 = pl.multiple_of(i * KC, KC)
        kk = pl.ds(k0, KC)
        u0 = rows_at(b0, U, k0, 0)
        um2, um1, up1, _ = shift_x(u0, x0[U, kk], x0[U, kk], lane, cols)
        m0 = rows_at(b0, M, k0, 0)
        mm2, mm1, mp1, mp2 = shift_x(m0, x0[M, kk], x0[M, kk], lane, cols)
        v0 = rows_at(b0, V, k0, 0)
        vm1, vm2, vp1 = rows_at(b0, V, k0, -1), rows_at(b0, V, k0, -2), rows_at(b0, V, k0, 1)
        nm2, nm1 = rows_at(b0, M, k0, -2), rows_at(b0, M, k0, -1)
        np1, np2 = rows_at(b0, M, k0, 1), rows_at(b0, M, k0, 2)
        centre = None
        for base, (s_m2, s_m1, s_0, s_p1), (q_m2, q_m1, q_0, q_p1, q_p2) in (
            (0, (um2, um1, u0, up1), (mm2, mm1, m0, mp1, mp2)),
            (4, (vm2, vm1, v0, vp1), (nm2, nm1, m0, np1, np2)),
        ):
            a0 = coefficients(s_0)
            am1 = coefficients(s_m1)
            o0 = q_0 * q_p1
            om1 = q_m1 * q_0
            here = [o0 * a0[k] for k in range(4)]
            back = [om1 * am1[k] for k in range(4)]
            ahead0 = (q_p1 * q_p2) * coefficients(s_p1)[0]
            behind3 = (q_m2 * q_m1) * coefficients(s_m2)[3]
            w[base + 0, kk] = back[0]
            w[base + 1, kk] = back[1] - here[0]
            w[base + 2, kk] = back[3] - here[2]
            w[base + 3, kk] = -here[3]
            w[8 + base + 0, kk] = -behind3
            w[8 + base + 1, kk] = behind3 - back[2]
            w[8 + base + 2, kk] = here[1] - ahead0
            w[8 + base + 3, kk] = ahead0
            mid = back[2] - here[1]
            centre = mid if centre is None else centre + mid
        m_dn = b0[M, pl.ds(k0, KC), inner, :]
        m_up = b0[M, pl.ds(2 + k0, KC), inner, :]
        z_lo = vertical_mix * (m_dn * m0)
        z_hi = vertical_mix * (m0 * m_up)
        w[16, kk] = z_lo
        w[17, kk] = z_hi
        w[18, kk] = 1.0 + centre - (z_lo + z_hi)
        return carry

    lax.fori_loop(0, levels // KC, weights_body, 0, unroll=True)

    def step(src, xh, f, k0, forward):
        kk = pl.ds(k0, KC)
        c = rows_at(src, f, k0, 0)
        cm2, cm1, cp1, cp2 = shift_x(c, xh[f, kk], xh[f, kk], lane, cols)
        ym2, ym1 = rows_at(src, f, k0, -2), rows_at(src, f, k0, -1)
        yp1, yp2 = rows_at(src, f, k0, 1), rows_at(src, f, k0, 2)
        zm = src[f, pl.ds(k0, KC), inner, :]
        zp = src[f, pl.ds(2 + k0, KC), inner, :]
        o = 0 if forward else 8
        sx = (w[o + 0, kk] * cm2 + w[o + 1, kk] * cm1) + (w[o + 2, kk] * cp1 + w[o + 3, kk] * cp2)
        sy = (w[o + 4, kk] * ym2 + w[o + 5, kk] * ym1) + (w[o + 6, kk] * yp1 + w[o + 7, kk] * yp2)
        sz = w[16, kk] * zm + w[17, kk] * zp
        return (w[18, kk] * c + sz) + (sx + sy)

    def step1_loop(g):
        def body(i, carry):
            k0 = pl.multiple_of(i * KC, KC)
            for f in (2 * g, 2 * g + 1):
                b1[f, pl.ds(1 + k0, KC), inner, :] = step(b0, x0, f, k0, g == 0)
            return carry

        lax.fori_loop(0, levels // KC, body, 0, unroll=True)

    def out_copy(f, i):
        chunk = pl.ds(pl.multiple_of(i * KC, KC), KC)
        return pltpu.make_async_copy(res.at[f, chunk], o_all.at[f, chunk], out_sem.at[f, i])

    def step2_loop(g):
        def body(i, carry):
            k0 = pl.multiple_of(i * KC, KC)
            for f in (2 * g, 2 * g + 1):
                res[f, pl.ds(k0, KC)] = step(b1, x1, f, k0, g == 0)
                out_copy(f, i).start()
            return carry

        lax.fori_loop(0, levels // KC, body, 0, unroll=True)

    receive(1)
    step1_loop(0)
    send(3)
    receive(2)
    step1_loop(1)
    send(4)
    for r in range(3):
        finish_sends(r)
    receive(3)
    step2_loop(0)
    receive(4)
    step2_loop(1)
    finish_sends(3)
    finish_sends(4)
    for f in range(N_TRACERS):
        for i in range(levels // KC):
            out_copy(f, i).wait()


def split_kernel(stacked, o_t, o_s, o_ct, o_cs, held, in_sem, out_sem):
    ins = []
    for f in range(N_TRACERS):
        cp = pltpu.make_async_copy(stacked.at[f], held.at[f], in_sem.at[f])
        cp.start()
        ins.append(cp)
    outs = []
    for f, dst in enumerate((o_t, o_s, o_ct, o_cs)):
        ins[f].wait()
        cp = pltpu.make_async_copy(held.at[f], dst, out_sem.at[f])
        cp.start()
        outs.append(cp)
    for cp in outs:
        cp.wait()


def local(n_ew, n_ns, temp, salt, u_east, v_north, wet, cot_temp, cot_salt):
    levels, rows, cols = temp.shape
    f32 = jnp.float32
    any_spec = pl.BlockSpec(memory_space=pl.ANY)
    vmem_spec = pl.BlockSpec(memory_space=pltpu.VMEM)
    out = jax.ShapeDtypeStruct((levels, rows, cols), f32)
    call = pl.pallas_call(
        functools.partial(kernel, n_ew, n_ns, levels, rows, cols),
        out_shape=jax.ShapeDtypeStruct((N_TRACERS, levels, rows, cols), f32),
        in_specs=[any_spec] * 7,
        out_specs=any_spec,
        scratch_shapes=[
            pltpu.VMEM((N_FIELDS, levels + 2, rows + 2 * PAD, cols), f32),
            pltpu.VMEM((X_FIELDS, levels, rows, cols), f32),
            pltpu.VMEM((X_FIELDS, cols, levels * rows), f32),
            pltpu.VMEM((X_FIELDS, cols, levels * rows), f32),
            pltpu.VMEM((N_TRACERS, levels + 2, rows + 2 * PAD, cols), f32),
            pltpu.VMEM((N_TRACERS, levels, rows, cols), f32),
            pltpu.VMEM((N_TRACERS, cols, levels * rows), f32),
            pltpu.VMEM((N_TRACERS, cols, levels * rows), f32),
            pltpu.VMEM((19, levels, rows, cols), f32),
            pltpu.VMEM((N_TRACERS, levels, rows, cols), f32),
            pltpu.VMEM((levels, rows, cols), jnp.int32),
            pltpu.SemaphoreType.DMA((7,)),
            pltpu.SemaphoreType.DMA((5, 4)),
            pltpu.SemaphoreType.DMA((5, 4)),
            pltpu.SemaphoreType.DMA((N_TRACERS, levels // KC)),
        ],
        compiler_params=pltpu.CompilerParams(
            collective_id=0, has_side_effects=True, vmem_limit_bytes=56 * 1024 * 1024
        ),
    )
    stacked = call(temp, salt, cot_temp, cot_salt, u_east, v_north, wet)
    return pl.pallas_call(
        split_kernel,
        out_shape=(out,) * 4,
        in_specs=[any_spec],
        out_specs=(any_spec,) * 4,
        scratch_shapes=[
            pltpu.VMEM((N_TRACERS, levels, rows, cols), f32),
            pltpu.SemaphoreType.DMA((N_TRACERS,)),
            pltpu.SemaphoreType.DMA((N_TRACERS,)),
        ],
    )(stacked)


def solution(mesh):
    spec = P(None, "ns", "ew")
    n_ew = mesh.shape["ew"]
    n_ns = mesh.shape["ns"]
    return jax.shard_map(
        functools.partial(local, n_ew, n_ns), mesh=mesh,
        in_specs=(spec,) * 7, out_specs=(spec,) * 4, check_vma=False,
    )
```
